32 devices in a mesh: section: 2 (over core), dp: 16 (over z, y, x).
Axes of the slice: x: 2, y: 2, z: 4, core: 2. Of those that a mesh axis runs over, the one named last changes fastest.
Arguments:
- tokens: bfloat16 [128, 256, 512], P('dp'), may hold values from -6 to 6
- out_cotangent: bfloat16 [128, 256, 512], P('dp'), may hold values from -8 to 8
- speaker: int32 [128], P('dp'), may hold values from 0 to 2559
- valid: int32 [128], P('dp'), may hold values 0 or 1
- conv_weight: float32 [2, 7, 512], P('section'), may hold values from -2 to 2
- conv_bias: float32 [2, 512], P('section'), may hold values from -3 to 3
- scale_table: float32 [2, 2560, 512], P('section'), may hold values from 0.1 to 1.9
- shift_table: float32 [2, 2560, 512], P('section'), may hold values from -3 to 3
- up_weight: bfloat16 [2, 512, 1536], P('section'), may hold values from -0.25 to 0.25
- up_bias: float32 [2, 1536], P('section'), may hold values from -3 to 3
- down_weight: bfloat16 [2, 1536, 512], P('section'), may hold values from -0.15625 to 0.15625
- down_bias: float32 [2, 512], P('section'), may hold values from -3 to 3
- layer_scale: float32 [2, 512], P('section'), may hold values from 0.5 to 1.5
Outputs:
- block_outputs: bfloat16 [2, 128, 256, 512], P('section', 'dp')
- input_grads: bfloat16 [2, 128, 256, 512], P('section', 'dp')
- grad_conv_weight: float32 [2, 7, 512], P('section', None, 'dp')
- grad_conv_bias: float32 [2, 512], P('section', 'dp')
- grad_scale_table: float32 [2, 2560, 512], P('section', 'dp')
- grad_shift_table: float32 [2, 2560, 512], P('section', 'dp')
- grad_up_weight: float32 [2, 512, 1536], P('section', 'dp')
- grad_up_bias: float32 [2, 1536], P('section', 'dp')
- grad_down_weight: float32 [2, 1536, 512], P('section', 'dp')
- grad_down_bias: float32 [2, 512], P('section', 'dp')
- grad_layer_scale: float32 [2, 512], P('section', 'dp')
The draws below stay inside these ranges and needn't reach their ends.
All inputs are finite; a program needn't handle non-finite values. No bound on the sum of `valid` on one device may be relied on, other than what follows from the above.
Results may differ from the reference program's by a relative error of at most 0.0074.
Values may be sent and summed in bfloat16 or wider, within the bound.
No kernel may reach another device: no remote copies, remote signals or barrier semaphores. Data moves between devices by JAX's collectives and lax.ppermute only.
A program may use at most 192 MiB of HBM per device.

```python
import jax
import jax.numpy as jnp
from jax import lax

D = 512
H = 1536
SPEAKERS = 2560
KERNEL = 7
L = 256
MICRO = 4
SLOTS = 2
CLIPS = 128


def place_ends(drawn, own_key, smallest, largest):
    index_at = [jax.random.randint(jax.random.fold_in(own_key, axis), (), 0, length) for axis, length in enumerate(drawn.shape)]
    main_axis = drawn.shape.index(max(drawn.shape))
    next_to = index_at[:main_axis] + [(index_at[main_axis] + 1) % drawn.shape[main_axis]] + index_at[main_axis + 1:]
    return drawn.at[tuple(index_at)].set(smallest).at[tuple(next_to)].set(largest)


def with_spikes(values, own_key, source, target, blocks, factor):
    owner, partner = [(jnp.arange(values.shape[dim]) // (values.shape[dim] // blocks)).reshape([-1 if axis == dim else 1 for axis in range(values.ndim)]) for dim in (source, target)]
    chosen = jax.random.permutation(own_key, blocks)[partner]
    strong = (owner == chosen) | (owner == (partner + blocks // 2) % blocks)
    return jnp.where(strong, factor * values, values)


def block_levels(rng, dims, pieces, smallest, top_value):
    loudness, own = 1.0, jax.random.fold_in(rng, 6)
    for axis_at, parts in pieces:
        draws = jnp.exp(jax.random.uniform(jax.random.fold_in(own, axis_at), (parts,), jnp.float32, smallest / len(pieces), top_value / len(pieces)))
        loudness = loudness * jnp.repeat(draws, dims[axis_at] // parts).reshape([-1 if axis == axis_at else 1 for axis in range(len(dims))])
    return loudness


def gaussian(stream_key, dims, scale, limit, cuts=(), dtype=jnp.bfloat16):
    result = jax.random.normal(stream_key, dims, jnp.float32) * scale
    if len(cuts) > 0:
        result = block_levels(stream_key, dims, cuts, -0.22, 0.18) * result
    return jnp.clip(result, min=-limit, max=limit).astype(dtype)


def bell_draw_with(own_key, dims, scale, bound, pieces, heavy, held_as=jnp.bfloat16):
    drawn = scale * jax.random.normal(own_key, dims, jnp.float32)
    if pieces:
        drawn = drawn * block_levels(own_key, dims, pieces, -0.22, 0.18)
    return jnp.clip(with_spikes(drawn, jax.random.fold_in(own_key, 3), *heavy), -bound, bound).astype(held_as)


def setup_inputs(seed: int = 0) -> dict:
    streams_of = jax.random.split(jax.random.key(seed), 14)
    return {
        "tokens": gaussian(streams_of[0], (CLIPS, L, D), 1.0, 6.0, ((0, 16),)),
        "out_cotangent": bell_draw_with(streams_of[1], (CLIPS, L, D), 1.0, 8.0, ((0, 16),), (0, 2, 16, 2.0)),
        "speaker": place_ends(jax.random.randint(streams_of[2], (CLIPS,), 0, SPEAKERS), jax.random.fold_in(streams_of[2], 1), 0, SPEAKERS - 1).astype(jnp.int32),
        "valid": place_ends((jax.random.randint(streams_of[3], (CLIPS,), 0, 4) < 3).astype(jnp.int32), jax.random.fold_in(streams_of[3], 1), 0, 1),
        "conv_weight": gaussian(streams_of[4], (2, KERNEL, D), KERNEL ** -0.5, 2.0, ((0, 2),), jnp.float32),
        "conv_bias": gaussian(streams_of[5], (2, D), 0.5, 3.0, ((0, 2),), jnp.float32),
        "scale_table": jnp.clip(1.0 + 0.18 * jax.random.normal(streams_of[6], (2, SPEAKERS, D), jnp.float32), 0.1, 1.9),
        "shift_table": gaussian(streams_of[7], (2, SPEAKERS, D), 0.5, 3.0, ((0, 2),), jnp.float32),
        "up_weight": gaussian(streams_of[8], (2, D, H), D ** -0.5, 0.25, ((0, 2),)),
        "up_bias": gaussian(streams_of[9], (2, H), 0.5, 3.0, ((0, 2),), jnp.float32),
        "down_weight": gaussian(streams_of[10], (2, H, D), H ** -0.5, 0.15625, ((0, 2),)),
        "down_bias": gaussian(streams_of[11], (2, D), 0.5, 3.0, ((0, 2),), jnp.float32),
        "layer_scale": jnp.clip(0.5 + 1.0 * jax.random.uniform(streams_of[12], (2, D), jnp.float32) ** block_levels(streams_of[12], (2, D), ((0, 2),), -0.2, 0.2), 0.5, 1.5),
    }


highest = lax.Precision.HIGHEST

@jax.custom_vjp
def low(v):
    return lax.optimization_barrier(v.astype(jnp.bfloat16)).astype(jnp.float32)

@jax.custom_vjp
def low_back(v):
    return v

def low_keep(v):
    return (low(v), None)

def low_pass(kept, grad):
    return (grad,)

def back_keep(v):
    return (v, None)

def back_low(kept, grad):
    return (low(grad),)
low.defvjp(low_keep, low_pass)
low_back.defvjp(back_keep, back_low)

def block_forward(inputs, speaker_ids, params):
    kernel_taps, conv_shift, scale_rows, shift_rows, up_mat, up_shift, down_mat, down_shift, gains = params
    frames = inputs.shape[1]
    padded = jnp.pad(inputs, ((0, 0), (3, 3), (0, 0)))
    conv = conv_shift + padded[:, 0:frames, :] * kernel_taps[0]
    for offset in range(1, KERNEL):
        conv = conv + padded[:, offset:offset + frames, :] * kernel_taps[offset]
    centred = conv - lax.optimization_barrier(jnp.mean(conv, axis=-1, keepdims=True))
    normed = centred * lax.rsqrt(lax.optimization_barrier(jnp.mean(centred * centred, axis=-1, keepdims=True)) + 1e-06)
    adapted = low(normed * scale_rows[speaker_ids][:, None, :] + shift_rows[speaker_ids][:, None, :])
    hidden_pre = low_back(jnp.einsum('gld,dh->glh', adapted, up_mat, precision=highest) + up_shift)
    activated = low(jax.nn.gelu(hidden_pre, approximate=False))
    branch = low_back(jnp.einsum('glh,hd->gld', activated, down_mat, precision=highest) + down_shift)
    return inputs + gains * branch

def reference(tokens, out_cotangent, speaker, valid, conv_weight, conv_bias, scale_table, shift_table, up_weight, up_bias, down_weight, down_bias, layer_scale):
    weights = (conv_weight, conv_bias, scale_table, shift_table, up_weight.astype(jnp.float32), up_bias, down_weight.astype(jnp.float32), down_bias, layer_scale)
    first = tuple((item[0] for item in weights))
    second = tuple((item[1] for item in weights))
    per_group = MICRO * SLOTS
    groups = tokens.shape[0] // per_group
    inputs_all = tokens.reshape(groups, per_group, L, D)
    cot_all = out_cotangent.reshape(groups, per_group, L, D)
    speaker_all = speaker.reshape(groups, per_group)
    valid_all = valid.reshape(groups, per_group)

    def advance(totals, item):
        group_in, group_cot, group_speaker, group_valid = item
        inputs = group_in.astype(jnp.float32)
        between = jnp.zeros_like(inputs)

        def forward(inputs, between, first, second):
            out_first = block_forward(inputs, group_speaker, first)
            passed = low_back(low(out_first) + between)
            out_second = block_forward(passed, group_speaker, second)
            return (passed, out_second)
        (passed, out_second), pull = jax.vjp(forward, inputs, between, first, second)
        grad_top = group_cot.astype(jnp.float32) * group_valid.astype(jnp.float32)[:, None, None]
        grad_in, grad_between, grad_first, grad_second = pull((jnp.zeros_like(passed), grad_top))
        totals = tuple((total + jnp.stack([one, two]) for total, one, two in zip(totals, grad_first, grad_second)))
        return (totals, (passed.astype(jnp.bfloat16), out_second.astype(jnp.bfloat16), grad_in.astype(jnp.bfloat16), grad_between.astype(jnp.bfloat16)))
    start = tuple((jnp.zeros(item.shape, jnp.float32) for item in weights))
    totals, outs = lax.scan(advance, start, (inputs_all, cot_all, speaker_all, valid_all))
    block_outputs = jnp.stack([outs[0].reshape(tokens.shape), outs[1].reshape(tokens.shape)])
    input_grads = jnp.stack([outs[2].reshape(tokens.shape), outs[3].reshape(tokens.shape)])
    return (block_outputs, input_grads, totals[0], totals[1], totals[2], totals[3], totals[4], totals[5], totals[6], totals[7], totals[8])
```

```python
import functools

import jax
import jax.numpy as jnp
from jax import lax
from jax.experimental import pallas as pl
from jax.experimental.pallas import tpu as pltpu
from jax.sharding import PartitionSpec as P

F32 = jnp.float32
BF16 = jnp.bfloat16
PAIR = ("section", "dp")
TILE = 512
HALF_ROOT = 0.7071067811865476
DENSITY = 0.3989422804014327
BLOCKS = 16
ORDERS = ((0, 1, 2, 3), (2, 0, 1, 3))
ANY = pl.BlockSpec(memory_space=pltpu.HBM)
VMEM = pl.BlockSpec(memory_space=pltpu.VMEM)
SMEM = pl.BlockSpec(memory_space=pltpu.SMEM)

TAPS, CONV, UPB, DOWNB, GAIN, SCALE, SHIFT, SMALL = 0, 7, 8, 11, 12, 16, 20, 24


def position(block, order):
    place = 0
    for bit in order:
        place = 2 * place + ((block >> bit) & 1)
    return place


def dot(a, b, dims):
    return lax.dot_general(a, b, (dims, ((), ())), preferred_element_type=F32)


NN = ((1,), (0,))
NT = ((1,), (1,))
TN = ((0,), (0,))


def shifted(x, offset):
    if offset == 0:
        return x
    frames = x.shape[0]
    rows = lax.broadcasted_iota(jnp.int32, (frames, 1), 0)
    rolled = pltpu.roll(x, (-offset) % frames, 0)
    kept = rows < frames - offset if offset > 0 else rows >= -offset
    return jnp.where(kept, rolled, 0.0)


def wide(x, width):
    return jnp.concatenate([x] * (width // 128), axis=1)


def rowsum(x):
    return jnp.sum(x, axis=0, keepdims=True)


def normalize(x, small, clip):
    conv = small[CONV : CONV + 1] + x * small[3:4]
    for k in range(7):
        if k != 3:
            conv = conv + shifted(x, k - 3) * small[k : k + 1]
    centred = conv - jnp.mean(conv, axis=-1, keepdims=True)
    inv = lax.rsqrt(jnp.mean(centred * centred, axis=-1, keepdims=True) + 1e-06)
    normed = centred * inv
    scale = small[pl.ds(SCALE + clip, 1)]
    shift = small[pl.ds(SHIFT + clip, 1)]
    adapted = (normed * scale + shift).astype(BF16)
    return adapted, normed.astype(BF16), jnp.broadcast_to(inv, (x.shape[0], 128))


def prep_body(sec, speaker, taps, conv, upb, downb, gain, scale_hbm, shift_hbm, own, other, sems):
    width = own.shape[1]
    half = SMALL - SHIFT
    copies = []
    for side, out in enumerate((own, other)):
        first = (sec[0] if side == 0 else 1 - sec[0]) * half
        for clip in range(half):
            row = speaker[first + clip]
            for kind, table in enumerate((scale_hbm, shift_hbm)):
                copies.append(
                    pltpu.make_async_copy(
                        table.at[0, pl.ds(row, 1)],
                        out.at[pl.ds((SCALE, SHIFT)[kind] + clip, 1)],
                        sems.at[side, kind, clip],
                    )
                )
    for copy in copies:
        copy.start()
    for out in (own, other):
        for k in range(7):
            out[TAPS + k : TAPS + k + 1] = taps[k]
        out[CONV : CONV + 1] = conv[...]
        for k in range(DOWNB - UPB):
            out[UPB + k : UPB + k + 1] = upb[:, k * width : (k + 1) * width]
        out[DOWNB : DOWNB + 1] = downb[...]
        out[GAIN : GAIN + 1] = gain[...]
        out[GAIN + 1 : SCALE] = jnp.zeros((SCALE - GAIN - 1, width), F32)
    for copy in copies:
        copy.wait()


def first_norm_body(sec, tokens, small, adapted, normed, inv):
    clip = pl.program_id(0)
    a, n, r = normalize(tokens[0].astype(F32), small, clip)
    adapted[...] = a
    normed[...] = n
    inv[...] = r


def forward_tiles(adapted, up, down, small, act, slope, acc):
    clips = acc.shape[0] // 256
    for j in range(3):
        bias = small[UPB + j : UPB + j + 1]
        for r in range(clips):
            rows = slice(r * 256, (r + 1) * 256)
            pre = dot(adapted[rows], up[:, j * TILE : (j + 1) * TILE], NN) + bias
            phi = 0.5 * lax.erf(pre * HALF_ROOT) + 0.5
            low = (pre * phi).astype(BF16)
            act[j, rows] = low
            slope[j, rows] = (phi + pre * (DENSITY * jnp.exp(-0.5 * pre * pre))).astype(BF16)
            part = dot(low, down[j * TILE : (j + 1) * TILE], NN)
            if j == 0:
                acc[rows] = part
            else:
                acc[rows] = acc[rows] + part


def activation_tile(j, gb, down, slope, sums):
    total = jnp.zeros((1, TILE), F32)
    for r in range(gb.shape[0] // 256):
        rows = slice(r * 256, (r + 1) * 256)
        gact = dot(gb[rows], down[j * TILE : (j + 1) * TILE], NT)
        gpre = (gact * slope[j, rows].astype(F32)).astype(BF16)
        slope[j, rows] = gpre
        total = total + rowsum(gpre.astype(F32))
    sums[UPB + j : UPB + j + 1] = total


def weight_tile(j, gb, adapted, act, gpre, upd, dnd):
    gup = dot(adapted[...], gpre, TN).astype(BF16)
    share = TILE // BLOCKS
    for i in range(BLOCKS):
        upd[position(i, ORDERS[0]), j * share : (j + 1) * share] = gup[i * share : (i + 1) * share]
    gdn = dot(act, gb[...], TN).astype(BF16)
    share = 3 * TILE // BLOCKS
    at = j * TILE
    while at < (j + 1) * TILE:
        stop = min((at // share + 1) * share, (j + 1) * TILE)
        first = at % share
        dnd[position(at // share, ORDERS[1]), first : first + stop - at] = gdn[
            at - j * TILE : stop - j * TILE
        ]
        at = stop


def norm_backward(gad, normed, inv, small, clip, grad_out, v):
    n = normed.astype(F32)
    width = n.shape[1]
    scale = small[pl.ds(SCALE + clip, 1)]
    g_shift = rowsum(gad)
    g_scale = rowsum(gad * n)
    gn = gad * scale
    m1 = jnp.mean(gn, axis=-1, keepdims=True)
    m2 = jnp.mean(gn * n, axis=-1, keepdims=True)
    gc = (gn - m1 - n * m2) * wide(inv, width)
    g_conv = rowsum(gc)
    total = grad_out
    g_taps = []
    for k in range(7):
        moved = shifted(gc, 3 - k)
        total = total + moved * small[k : k + 1]
        g_taps.append(rowsum(moved * v))
    return total.astype(BF16), jnp.concatenate(g_taps + [g_conv], axis=0), g_scale, g_shift


def place_weights(sec, block, up_own, up_got, down_own, down_got, up, down, sems, start):
    def go(up_from, down_from):
        for source, target, sem in ((up_from, up, sems.at[0]), (down_from, down, sems.at[1])):
            copy = pltpu.make_async_copy(source, target, sem)
            copy.start() if start else copy.wait()

    if not start:
        go(up_own, down_own)
        return

    @pl.when(sec[0] == block)
    def _():
        go(up_own, down_own)

    @pl.when(sec[0] != block)
    def _():
        go(up_got, down_got)


def route(sec, upd, dnd, keep, send, sems, start):
    def go(kept, sent):
        for source, target, sem in ((kept, keep, sems.at[0]), (sent, send, sems.at[1])):
            copy = pltpu.make_async_copy(source, target, sem)
            copy.start() if start else copy.wait()

    if not start:
        go(upd, dnd)
        return

    @pl.when(sec[0] == 0)
    def _():
        go(upd, dnd)

    @pl.when(sec[0] != 0)
    def _():
        go(dnd, upd)


def main_body(
    sec, valid, adapted0, tokens, cot, small0, small1, up_own, up_got, down_own, down_got,
    gin1, gb0, sums0, sums1, out_own, out_send, act_hbm, gpre_hbm, keep, send,
    up0, down0, up1, down1, act0, slope0, act1, slope1, acc, adapted1, normed1, inv1, branch0, gb1,
    out0, out1, upd, dnd, sems,
):
    clips = acc.shape[0] // 256
    weights = (up_own, up_got, down_own, down_got)
    place_weights(sec, 0, *weights, up0, down0, sems.at[0], True)
    place_weights(sec, 1, *weights, up1, down1, sems.at[1], True)
    place_weights(sec, 0, *weights, up0, down0, sems.at[0], False)
    forward_tiles(adapted0, up0, down0, small0, act0, slope0, acc)
    save_act = pltpu.make_async_copy(act0, act_hbm, sems.at[2, 0])
    save_act.start()

    def between(r):
        rows = pl.ds(pl.multiple_of(r * 256, 256), 256)
        branch = acc[rows] + small0[DOWNB : DOWNB + 1]
        branch0[rows] = branch
        result = (tokens[r].astype(F32) + small0[GAIN : GAIN + 1] * branch).astype(BF16)
        out0[r] = result
        a, n, i = normalize(result.astype(F32), small1, r)
        adapted1[rows] = a
        normed1[rows] = n
        inv1[rows] = i

    pl.loop(0, clips)(between)
    place_weights(sec, 1, *weights, up1, down1, sems.at[1], False)
    forward_tiles(adapted1, up1, down1, small1, act1, slope1, acc)
    sums0[...] = jnp.zeros_like(sums0)
    sums1[...] = jnp.zeros_like(sums1)

    def top(r):
        rows = pl.ds(pl.multiple_of(r * 256, 256), 256)
        branch = acc[rows] + small1[DOWNB : DOWNB + 1]
        gain = small1[GAIN : GAIN + 1]
        out1[r] = (out0[r].astype(F32) + gain * branch).astype(BF16)
        grad = cot[r].astype(F32) * valid[sec[0] * clips + r].astype(F32)
        low = (grad * gain).astype(BF16)
        gb1[rows] = low
        sums1[GAIN : GAIN + 1] += rowsum(grad * branch)
        sums1[DOWNB : DOWNB + 1] += rowsum(low.astype(F32))

    pl.loop(0, clips)(top)
    half_own = out_own.at[pl.ds(sec[0] * clips, clips)]
    route(sec, out0, out1, half_own, out_send, sems.at[4], True)
    for j in range(3):
        activation_tile(j, gb1, down1, slope1, sums1)
        for r in range(clips):
            rows = slice(r * 256, (r + 1) * 256)
            part = dot(slope1[j, rows], up1[:, j * TILE : (j + 1) * TILE], NT)
            acc[rows] = part if j == 0 else acc[rows] + part
        weight_tile(j, gb1, adapted1, act1[j], slope1[j], upd, dnd)
    route(sec, upd, dnd, keep, send, sems.at[3], True)

    def under(r):
        rows = pl.ds(pl.multiple_of(r * 256, 256), 256)
        grad = cot[r].astype(F32) * valid[sec[0] * clips + r].astype(F32)
        gin, smalls, g_scale, g_shift = norm_backward(
            acc[rows], normed1[rows], inv1[rows], small1, r, grad, out0[r].astype(F32)
        )
        gin1[r] = gin
        sums1[TAPS : TAPS + 8] += smalls
        sums1[pl.ds(SCALE + r, 1)] = g_scale
        sums1[pl.ds(SHIFT + r, 1)] = g_shift
        grad0 = gin.astype(F32)
        low = (grad0 * small0[GAIN : GAIN + 1]).astype(BF16)
        gb0[rows] = low
        sums0[GAIN : GAIN + 1] += rowsum(grad0 * branch0[rows])
        sums0[DOWNB : DOWNB + 1] += rowsum(low.astype(F32))

    pl.loop(0, clips)(under)
    saves = []
    for j in range(3):
        activation_tile(j, gb0, down0, slope0, sums0)
        saves.append(pltpu.make_async_copy(slope0.at[j], gpre_hbm.at[j], sems.at[5 + j // 2, j % 2]))
        saves[-1].start()
    save_act.wait()
    route(sec, out0, out1, half_own, out_send, sems.at[4], False)
    route(sec, upd, dnd, keep, send, sems.at[3], False)
    for copy in saves:
        copy.wait()


def weights_body(sec, gb, adapted, act, gpre, keep, send, upd, dnd, sems):
    step = pl.program_id(0)
    for j in range(3):

        @pl.when(step == j)
        def _():
            weight_tile(j, gb, adapted, act[0], gpre[0], upd, dnd)

    @pl.when(step == 2)
    def _():
        route(sec, upd, dnd, keep, send, sems, True)
        route(sec, upd, dnd, keep, send, sems, False)


def last_body(
    first, sec, gpre, up_own, up_got, normed, inv, small, grad_out, tokens, sums_in, *rest
):
    gin, away, sums, up, sem = rest[-5:]
    step = pl.program_id(0)
    clip = first + step

    @pl.when(step == 0)
    def _():
        sums[...] = sums_in[...]

        @pl.when(sec[0] == 0)
        def _():
            pltpu.make_async_copy(up_own, up, sem).start()

        @pl.when(sec[0] != 0)
        def _():
            pltpu.make_async_copy(up_got, up, sem).start()

        pltpu.make_async_copy(up_own, up, sem).wait()

    gad = dot(gpre[0], up[:, :TILE], NT)
    for j in range(1, 3):
        gad = gad + dot(gpre[j], up[:, j * TILE : (j + 1) * TILE], NT)
    above = grad_out[0]
    out, smalls, g_scale, g_shift = norm_backward(
        gad, normed[...], inv[...], small, clip, above.astype(F32), tokens[0].astype(F32)
    )
    gin[0] = jnp.where(sec[0] == 0, out, above)
    away[0] = jnp.where(sec[0] == 0, above, out)
    sums[TAPS : TAPS + 8] += smalls
    sums[pl.ds(SCALE + clip, 1)] = g_scale
    sums[pl.ds(SHIFT + clip, 1)] = g_shift


def pick(first, a, b):
    return jnp.where(first, a, b)


def bit_of(spot, step):
    low, high = ORDERS[0][step], ORDERS[1][step]
    return (spot[1] >> (low if low == high else pick(spot[0] == 0, low, high))) & 1


def region(spot, level, step):
    start = 0
    for i in range(level, min(step, 4)):
        start = start + bit_of(spot, i) * (8 >> i)
    if step < 4:
        start = start + (1 - bit_of(spot, step)) * (8 >> step)
    return start


GATHER = (1, 2, 3, 0)


def gather_slot(spot):
    slot = 0
    for i, step in enumerate(GATHER):
        slot = slot + bit_of(spot, step) * (1 << i)
    return slot


def fetch(copies, source, first, rows, target, sem):
    copies.append(pltpu.make_async_copy(source.at[pl.ds(first, rows)], target, sem))
    copies[-1].start()


def add_up(buffers, rows):
    total = buffers[0][:rows].astype(F32)
    for buffer in buffers[1:]:
        total = total + buffer[:rows].astype(F32)
    return total


def pack_body(step, blocks, bases, share, extras, spot, speaker, *refs):
    levels = step + 2
    sources = [refs[b * levels : (b + 1) * levels] for b in range(blocks)]
    refs = refs[blocks * levels :]
    count = 1 if step == 4 else 8 >> step
    rows = count * share
    extra_in, refs = refs[: 3 * extras], refs[3 * extras :]
    packet, refs = (refs[0], refs[1:]) if step < 4 or extras else (None, refs)
    if extras:
        smalls_out, refs = refs[0], refs[1:]
    if step == 4:
        mine, away, refs = refs[0], refs[1], refs[2:]
    buffers, tail, sems = refs
    copies = []
    for b in range(blocks):
        for n in range(levels):
            level = max(n - 1, 0)
            base = bases[b][level]
            first = pl.multiple_of((region(spot, level, step)) * share + base, 32)
            fetch(copies, sources[b][n], first, rows, buffers.at[b, n], sems.at[b, n])
    head = blocks * rows if step < 4 else 0
    if extras and step == 1:
        sums0, sums1, got = extra_in
        own = pick(spot[0] == 0, sums0[...], sums1[...])
        other = got[...]
        low = pick(spot[0] == 0, own[SCALE:], other[SCALE:])
        high = pick(spot[0] == 0, other[SCALE:], own[SCALE:])
        packet[head : head + 16] = jnp.concatenate([low, high], axis=0).astype(BF16)
        width = own.shape[1]
        lane = lax.broadcasted_iota(jnp.int32, (1, width), 1)
        mine_lane = (lane >> 4) == gather_slot(spot)
        which = ((lane >> 3) & 1) * 4 + (lane & 3)
        code = jnp.zeros((1, width), jnp.int32)
        for c in range(8):
            code = jnp.where(mine_lane & (which == c), speaker[c], code)
        smalls_out[...] = own[:SCALE] + other[:SCALE]
        smalls_out[13:14] = (code >> 6).astype(F32)
        smalls_out[14:15] = (code & 63).astype(F32)
        packet[head + 16 : head + 32] = smalls_out[...].astype(BF16)
    elif extras:
        before, after, smalls_in = extra_in
        size = 16 << (step - 2)
        old_head = blocks * (8 >> (step - 1)) * share
        bit = bit_of(spot, GATHER[step - 2])
        for n, (source, spot_bit) in enumerate(((before, bit), (after, 1 - bit))):
            target = packet.at[pl.ds(pl.multiple_of(head + spot_bit * size, 16), size)]
            fetch(copies, source, old_head, size, target, sems.at[2, n])
        fetch(copies, after, old_head + size, 16, tail, sems.at[2, 2])
    for b in range(blocks):
        for n in range(levels):
            copies[b * levels + n].wait()
        total = add_up([buffers.at[b, n] for n in range(levels)], rows)
        if step < 4:
            packet[b * rows : (b + 1) * rows] = total.astype(BF16)
        else:
            @pl.when(spot[0] == b)
            def _():
                mine[...] = total

            @pl.when(spot[0] != b)
            def _():
                away[...] = total
    if extras and step > 1:
        for copy in copies[blocks * levels :]:
            copy.wait()
        smalls_out[...] = smalls_in[...] + tail[...].astype(F32)
        packet[head + 2 * size : head + 2 * size + 16] = smalls_out[...].astype(BF16)


def finish_body(
    spot, before, after, smalls_in, mine, got, scale, shift, up, down, smalls, rows_of, tail, sems
):
    size = rows_of.shape[0] // 2
    bit = bit_of(spot, GATHER[3])
    copies = []
    for n, (source, spot_bit) in enumerate(((before, bit), (after, 1 - bit))):
        target = rows_of.at[pl.ds(pl.multiple_of(spot_bit * size, 16), size)]
        fetch(copies, source, 0, size, target, sems.at[n])
    fetch(copies, after, size, 16, tail, sems.at[2])
    first = spot[0] == 0
    one, two = mine[...], got[...]
    up_rows = up.shape[0]
    ups = pick(first, one, two)
    for j in range(3):
        up[:, j * TILE : (j + 1) * TILE] = ups[j * up_rows : (j + 1) * up_rows]
    down[...] = pick(first, two, one)
    for copy in copies:
        copy.wait()
    total = smalls_in[...] + tail[...].astype(F32)
    smalls[...] = total
    owned = scale.shape[0]
    count = 2 * size
    who = total[13:14, :count] * 64.0 + total[14:15, :count]
    wanted = lax.broadcasted_iota(jnp.int32, (owned, count), 0) + spot[1] * owned
    hit = who == wanted.astype(F32)
    kind = (lax.broadcasted_iota(jnp.int32, (owned, count), 1) >> 2) & 1
    for k, out in enumerate((scale, shift)):
        out[...] = dot(jnp.where(hit & (kind == k), 1.0, 0.0).astype(BF16), rows_of[...], NN)


def struct(shape, dtype):
    return jax.ShapeDtypeStruct(shape, dtype)


def params(limit=60):
    return pltpu.CompilerParams(vmem_limit_bytes=limit * 1024 * 1024)


def local(
    tokens, out_cotangent, speaker, valid, conv_weight, conv_bias, scale_table, shift_table,
    up_weight, up_bias, down_weight, down_bias, layer_scale,
):
    section = lax.axis_index("section").astype(jnp.int32)
    place = lax.axis_index("dp").astype(jnp.int32)
    devices = lax.axis_size("dp")
    first_section = section == 0
    clips, frames, width = tokens.shape
    hidden = up_weight.shape[2]
    table_rows = scale_table.shape[1]
    half = clips // 2
    rows = half * frames
    sec = section[None]
    spot = jnp.stack([section, place])
    swap = [(0, 1), (1, 0)]

    own_small, other_small = pl.pallas_call(
        prep_body,
        out_shape=[struct((SMALL, width), F32)] * 2,
        in_specs=[SMEM, SMEM] + [VMEM] * 5 + [ANY] * 2,
        out_specs=[VMEM] * 2,
        scratch_shapes=[pltpu.SemaphoreType.DMA((2, 2, half))],
        name="prep",
    )(
        sec, speaker, conv_weight.transpose(1, 0, 2), conv_bias, up_bias, down_bias, layer_scale,
        scale_table, shift_table,
    )
    got_small = lax.ppermute(other_small, "section", swap)
    up_own, down_own = up_weight[0], down_weight[0]
    up_got = lax.ppermute(up_own, "section", swap)
    down_got = lax.ppermute(down_own, "section", swap)
    small0 = jnp.where(first_section, own_small, got_small)
    small1 = jnp.where(first_section, got_small, own_small)

    clip_block = (1, frames, width)
    mine = pl.BlockSpec(clip_block, lambda c, sec: (sec[0] * half + c, 0, 0))
    whole_small = pl.BlockSpec((SMALL, width), lambda c, sec: (0, 0))
    flat = pl.BlockSpec((frames, width), lambda c, sec: (c, 0))
    flat_inv = pl.BlockSpec((frames, 128), lambda c, sec: (c, 0))
    adapted0, normed0, inv0 = pl.pallas_call(
        first_norm_body,
        grid_spec=pltpu.PrefetchScalarGridSpec(
            num_scalar_prefetch=1,
            grid=(half,),
            in_specs=[mine, whole_small],
            out_specs=[flat, flat, flat_inv],
        ),
        out_shape=[
            struct((rows, width), BF16), struct((rows, width), BF16), struct((rows, 128), F32)
        ],
        name="first_norm",
    )(sec, tokens, small0)

    half_struct = struct((half, frames, width), BF16)
    whole_struct = struct((clips, frames, width), BF16)
    small_struct = struct((SMALL, width), F32)
    tiles = hidden // TILE
    tiled = (tiles, rows, TILE)
    share = hidden // BLOCKS
    gradient = (BLOCKS, share, width)
    gradient_struct = struct(gradient, BF16)
    half_spec = pl.BlockSpec((half, frames, width), lambda i, sec, valid: (sec[0], 0, 0))

    def full(*shape):
        return pl.BlockSpec(shape, lambda i, *_: (0,) * len(shape))

    gin1, gb0, sums0, sums1, out_own, out_send, act0, gpre0, keep1, send1 = pl.pallas_call(
        main_body,
        grid_spec=pltpu.PrefetchScalarGridSpec(
            num_scalar_prefetch=2,
            grid=(1,),
            in_specs=[full(rows, width), half_spec, half_spec, full(SMALL, width), full(SMALL, width)]
            + [ANY] * 4,
            out_specs=[full(half, frames, width), full(rows, width)]
            + [full(SMALL, width)] * 2
            + [ANY] * 6,
            scratch_shapes=[
                pltpu.VMEM((width, hidden), BF16),
                pltpu.VMEM((hidden, width), BF16),
                pltpu.VMEM((width, hidden), BF16),
                pltpu.VMEM((hidden, width), BF16),
                pltpu.VMEM(tiled, BF16),
                pltpu.VMEM(tiled, BF16),
                pltpu.VMEM(tiled, BF16),
                pltpu.VMEM(tiled, BF16),
                pltpu.VMEM((rows, width), F32),
                pltpu.VMEM((rows, width), BF16),
                pltpu.VMEM((rows, width), BF16),
                pltpu.VMEM((rows, 128), F32),
                pltpu.VMEM((rows, width), F32),
                pltpu.VMEM((rows, width), BF16),
                pltpu.VMEM((half, frames, width), BF16),
                pltpu.VMEM((half, frames, width), BF16),
                pltpu.VMEM(gradient, BF16),
                pltpu.VMEM(gradient, BF16),
                pltpu.SemaphoreType.DMA((7, 2)),
            ],
        ),
        out_shape=[
            half_struct, struct((rows, width), BF16), small_struct, small_struct,
            whole_struct, half_struct, struct(tiled, BF16), struct(tiled, BF16),
            gradient_struct, gradient_struct,
        ],
        compiler_params=params(),
        name="main",
    )(
        sec, valid, adapted0, tokens, out_cotangent, small0, small1, up_own, up_got, down_own, down_got
    )
    got1 = lax.ppermute(send1, "section", swap)
    got_out = lax.ppermute(out_send, "section", swap)

    tile_spec = pl.BlockSpec((1, rows, TILE), lambda j, *_: (j, 0, 0))
    keep0, send0 = pl.pallas_call(
        weights_body,
        grid_spec=pltpu.PrefetchScalarGridSpec(
            num_scalar_prefetch=1,
            grid=(tiles,),
            in_specs=[full(rows, width), full(rows, width), tile_spec, tile_spec],
            out_specs=[ANY, ANY],
            scratch_shapes=[
                pltpu.VMEM(gradient, BF16),
                pltpu.VMEM(gradient, BF16),
                pltpu.SemaphoreType.DMA((2,)),
            ],
        ),
        out_shape=[gradient_struct, gradient_struct],
        compiler_params=params(),
        name="weights",
    )(sec, gb0, adapted0, act0, gpre0)
    got0 = lax.ppermute(send0, "section", swap)

    def last(first, count, sums, *others):
        def at(c):
            return first + c

        return pl.pallas_call(
            functools.partial(last_body, first),
            grid_spec=pltpu.PrefetchScalarGridSpec(
                num_scalar_prefetch=1,
                grid=(count,),
                in_specs=[
                    pl.BlockSpec((tiles, frames, TILE), lambda c, sec: (0, at(c), 0)),
                    ANY,
                    ANY,
                    pl.BlockSpec((frames, width), lambda c, sec: (at(c), 0)),
                    pl.BlockSpec((frames, 128), lambda c, sec: (at(c), 0)),
                    whole_small,
                    pl.BlockSpec(clip_block, lambda c, sec: (at(c), 0, 0)),
                    pl.BlockSpec(clip_block, lambda c, sec: (sec[0] * half + at(c), 0, 0)),
                    whole_small,
                ]
                + [ANY] * len(others),
                out_specs=[
                    pl.BlockSpec(clip_block, lambda c, sec: (sec[0] * half + at(c), 0, 0)),
                    pl.BlockSpec(clip_block, lambda c, sec: (at(c), 0, 0)),
                    whole_small,
                ],
                scratch_shapes=[pltpu.VMEM((width, hidden), BF16), pltpu.SemaphoreType.DMA],
            ),
            out_shape=[whole_struct, half_struct, small_struct],
            input_output_aliases={10 + i: i for i in range(len(others))},
            compiler_params=params(),
            name="last",
        )(sec, gpre0, up_own, up_got, normed0, inv0, small0, gin1, tokens, sums, *others)

    gin_own, gin_send, sums0 = last(0, half, sums0)
    got_gin = lax.ppermute(gin_send, "section", swap)
    got_sums = lax.ppermute(pick(first_section, sums1, sums0), "section", swap)

    def joined(whole, got):
        return lax.dynamic_update_slice(whole, got, ((1 - section) * half, 0, 0))[None]

    block_outputs = joined(out_own, got_out)
    input_grads = joined(gin_own, got_gin)
    pairs = [[keep0, got0], [keep1, got1]]
    if devices == BLOCKS:
        outs = halved(spot, speaker, pairs, sums0, sums1, got_sums, table_rows)
    else:
        outs = scattered(section, place, devices, speaker, pairs, sums0, sums1, got_sums, table_rows)
    up_share, down_share, table_scale, table_shift, smalls = outs
    lanes = width // devices
    own_lanes = lax.dynamic_slice_in_dim(smalls, place * lanes, lanes, 1)
    up_bias_share = lax.dynamic_slice_in_dim(
        smalls[UPB : UPB + 3].reshape(-1), place * (hidden // devices), hidden // devices, 0
    )
    return (
        block_outputs,
        input_grads,
        own_lanes[TAPS : TAPS + 7][None],
        own_lanes[CONV : CONV + 1],
        table_scale[None],
        table_shift[None],
        up_share[None],
        up_bias_share[None],
        down_share[None],
        own_lanes[DOWNB : DOWNB + 1],
        own_lanes[GAIN : GAIN + 1],
    )


def exchanged(packet, step):
    devices = lax.axis_size("dp")
    moves = [
        (s * devices + i, s * devices + (i ^ (1 << ORDERS[s][step])))
        for s in range(2)
        for i in range(devices)
    ]
    return lax.ppermute(packet, PAIR, moves)


def halved(spot, speaker, pairs, sums0, sums1, got_sums, table_rows):
    _, share, width = pairs[0][0].shape
    pairs = [[piece.reshape(-1, width) for piece in pair] for pair in pairs]

    def pack(step, block_sources, bases, extra_in, name):
        blocks = len(block_sources)
        levels = step + 2
        count = 1 if step == 4 else 8 >> step
        rows = count * share
        extras = len(extra_in) > 0
        outs, specs = [], []
        size = (8 << step) if extras else 0
        length = (blocks * rows if step < 4 else 0) + (size + 16 if extras else 0)
        outs.append(struct((length, width), BF16))
        if extras:
            outs.append(struct((SCALE, width), F32))
        if step == 4:
            outs += [struct((share, width), F32)] * 2
        if extras and step == 1:
            extra_specs = [VMEM] * 3
        elif extras:
            extra_specs = [ANY, ANY, VMEM]
        else:
            extra_specs = []
        return pl.pallas_call(
            functools.partial(pack_body, step, blocks, bases, share, int(extras)),
            out_shape=outs,
            in_specs=[SMEM, SMEM] + [ANY] * (blocks * levels) + extra_specs,
            out_specs=[VMEM] * len(outs),
            scratch_shapes=[
                pltpu.VMEM((blocks, levels, rows, width), BF16),
                pltpu.VMEM((16, width), BF16),
                pltpu.SemaphoreType.DMA((3, max(levels, 3))),
            ],
            compiler_params=params(),
            name=name,
        )(spot, speaker, *[x for sources in block_sources for x in sources], *extra_in)

    for b in (1, 0):
        (packet,) = pack(0, [pairs[b]], [[0]], [], f"pack0_{b}")
        pairs[b].append(exchanged(packet, 0))
    bases = [[0, 0], [0, 0]]
    extra_in = [sums0, sums1, got_sums]
    for step in range(1, 4):
        packet, smalls = pack(step, pairs, bases, extra_in, f"pack{step}")
        got = exchanged(packet, step)
        rows = (8 >> step) * share
        for b in range(2):
            pairs[b].append(got)
            bases[b].append(b * rows)
        bases = [list(x) for x in bases]
        extra_in = [packet, got, smalls]
    packet, smalls, mine, away = pack(4, pairs, bases, extra_in, "pack4")
    got = exchanged(packet, 0)
    got_share = lax.ppermute(away, "section", [(0, 1), (1, 0)])
    owned = table_rows // BLOCKS
    up_rows = width // BLOCKS
    scale, shift, up, down, smalls = pl.pallas_call(
        finish_body,
        out_shape=[
            struct((owned, width), F32),
            struct((owned, width), F32),
            struct((up_rows, 3 * TILE), F32),
            struct((share, width), F32),
            struct((SCALE, width), F32),
        ],
        in_specs=[SMEM, ANY, ANY, VMEM, VMEM, VMEM],
        out_specs=[VMEM] * 5,
        scratch_shapes=[
            pltpu.VMEM((16 * BLOCKS, width), BF16),
            pltpu.VMEM((16, width), BF16),
            pltpu.SemaphoreType.DMA((3,)),
        ],
        name="finish",
    )(spot, packet, got, smalls, mine, got_share)
    return up, down, scale, shift, smalls


def scattered(section, place, devices, speaker, pairs, sums0, sums1, got_sums, table_rows):
    first_section = section == 0
    own_sums = pick(first_section, sums0, sums1)
    smalls = lax.psum(own_sums[:SCALE] + got_sums[:SCALE], "dp")
    clip_rows = jnp.stack([own_sums[SCALE:], got_sums[SCALE:]])
    clip_rows = pick(first_section, clip_rows, clip_rows[::-1]).astype(BF16)
    clips = speaker.shape[0]
    width = clip_rows.shape[-1]
    clip_rows = clip_rows.reshape(2, 2, clips // 2, width).transpose(1, 0, 2, 3).reshape(2, clips, width)
    gathered = lax.all_gather(clip_rows, "dp", axis=1, tiled=True)
    who = lax.all_gather(speaker, "dp", tiled=True)
    owned = table_rows // devices
    wanted = place * owned + jnp.arange(owned, dtype=jnp.int32)
    chosen = (who[None, :] == wanted[:, None]).astype(BF16)
    tables = [jnp.dot(chosen, gathered[k], preferred_element_type=F32) for k in range(2)]
    natural = []
    for order in ORDERS:
        natural.append(
            jnp.stack(
                [
                    jnp.stack([pair[0][position(i, order)].astype(F32) + pair[1][position(i, order)].astype(F32) for i in range(BLOCKS)])
                    for pair in pairs
                ]
            )
        )
    blocks, _, rows, width = natural[0].shape
    tiles = rows * BLOCKS // TILE
    up = natural[0].reshape(blocks, BLOCKS, tiles, rows // tiles, TILE).transpose(0, 1, 3, 2, 4)
    flat = pick(
        first_section, up.reshape(blocks, devices, -1), natural[1].reshape(blocks, devices, -1)
    )
    share = lax.psum_scatter(flat, "dp", scatter_dimension=1, tiled=True)[:, 0]
    own_share = lax.dynamic_index_in_dim(share, section, 0, keepdims=False)
    got_share = lax.ppermute(
        lax.dynamic_index_in_dim(share, 1 - section, 0, keepdims=False), "section", [(0, 1), (1, 0)]
    )
    up_share = pick(first_section, own_share, got_share).reshape(width // devices, -1)
    down_share = pick(first_section, got_share, own_share).reshape(-1, width)
    return up_share, down_share, tables[0], tables[1], smalls


def solution(mesh):
    placed = (
        P("dp", None, None),
        P("dp", None, None),
        P("dp"),
        P("dp"),
        P("section", None, None),
        P("section", None),
        P("section", None, None),
        P("section", None, None),
        P("section", None, None),
        P("section", None),
        P("section", None, None),
        P("section", None),
        P("section", None),
    )
    return jax.shard_map(
        local,
        mesh=mesh,
        in_specs=placed,
        out_specs=(
            P("section", "dp", None, None),
            P("section", "dp", None, None),
            P("section", None, "dp"),
            P("section", "dp"),
            P("section", "dp", None),
            P("section", "dp", None),
            P("section", "dp", None),
            P("section", "dp"),
            P("section", "dp", None),
            P("section", "dp"),
            P("section", "dp"),
        ),
        check_vma=False,
    )
```

```python
import functools

import jax
import jax.numpy as jnp
from jax import lax
from jax.experimental import pallas as pl
from jax.experimental.pallas import tpu as pltpu
from jax.sharding import PartitionSpec as P


F32 = jnp.float32
BF16 = jnp.bfloat16
PAIR = ("section", "dp")
TILE = 512
HALF_ROOT = 0.7071067811865476
DENSITY = 0.3989422804014327
BLOCKS = 16
ORDERS = ((0, 1, 2, 3), (2, 0, 1, 3))
ANY = pl.BlockSpec(memory_space=pl.ANY)
VMEM = pl.BlockSpec(memory_space=pltpu.VMEM)
SMEM = pl.BlockSpec(memory_space=pltpu.SMEM)

TAPS, CONV, UPB, DOWNB, GAIN, SCALE, SHIFT, SMALL = 0, 7, 8, 11, 12, 16, 20, 24


def position(block, order):
    place = 0
    for bit in order:
        place = 2 * place + ((block >> bit) & 1)
    return place


def dot(a, b, dims):
    return lax.dot_general(a, b, (dims, ((), ())), preferred_element_type=F32)


NN = ((1,), (0,))
NT = ((1,), (1,))
TN = ((0,), (0,))


def shifted(x, offset):
    if offset == 0:
        return x
    frames = x.shape[0]
    rows = lax.broadcasted_iota(jnp.int32, (frames, 1), 0)
    rolled = pltpu.roll(x, (-offset) % frames, 0)
    kept = rows < frames - offset if offset > 0 else rows >= -offset
    return jnp.where(kept, rolled, 0.0)


def wide(x, width):
    return jnp.concatenate([x] * (width // 128), axis=1)


def rowsum(x):
    return jnp.sum(x, axis=0, keepdims=True)


def normalize(x, small, clip):
    conv = small[CONV : CONV + 1] + x * small[3:4]
    for k in range(7):
        if k != 3:
            conv = conv + shifted(x, k - 3) * small[k : k + 1]
    centred = conv - jnp.mean(conv, axis=-1, keepdims=True)
    inv = lax.rsqrt(jnp.mean(centred * centred, axis=-1, keepdims=True) + 1e-06)
    normed = centred * inv
    scale = small[pl.ds(SCALE + clip, 1)]
    shift = small[pl.ds(SHIFT + clip, 1)]
    adapted = (normed * scale + shift).astype(BF16)
    return adapted, normed.astype(BF16), jnp.broadcast_to(inv, (x.shape[0], 128))


def prep_body(sec, speaker, taps, conv, upb, downb, gain, scale_hbm, shift_hbm, own, other, sems):
    width = own.shape[1]
    half = SMALL - SHIFT
    copies = []
    for side, out in enumerate((own, other)):
        first = (sec[0] if side == 0 else 1 - sec[0]) * half
        for clip in range(half):
            row = speaker[first + clip]
            for kind, table in enumerate((scale_hbm, shift_hbm)):
                copies.append(
                    pltpu.make_async_copy(
                        table.at[0, pl.ds(row, 1)],
                        out.at[pl.ds((SCALE, SHIFT)[kind] + clip, 1)],
                        sems.at[side, kind, clip],
                    )
                )
    for copy in copies:
        copy.start()
    for out in (own, other):
        for k in range(7):
            out[TAPS + k : TAPS + k + 1] = taps[k]
        out[CONV : CONV + 1] = conv[...]
        for k in range(DOWNB - UPB):
            out[UPB + k : UPB + k + 1] = upb[:, k * width : (k + 1) * width]
        out[DOWNB : DOWNB + 1] = downb[...]
        out[GAIN : GAIN + 1] = gain[...]
        out[GAIN + 1 : SCALE] = jnp.zeros((SCALE - GAIN - 1, width), F32)
    for copy in copies:
        copy.wait()


def forward_tiles(adapted, up, down, small, act, slope, acc):
    clips = acc.shape[0] // 256
    for j in range(3):
        bias = small[UPB + j : UPB + j + 1]
        for r in range(clips):
            rows = slice(r * 256, (r + 1) * 256)
            pre = dot(adapted[rows], up[:, j * TILE : (j + 1) * TILE], NN) + bias
            phi = 0.5 * lax.erf(pre * HALF_ROOT) + 0.5
            low = (pre * phi).astype(BF16)
            act[j, rows] = low
            slope[j, rows] = (phi + pre * (DENSITY * jnp.exp(-0.5 * pre * pre))).astype(BF16)
            part = dot(low, down[j * TILE : (j + 1) * TILE], NN)
            if j == 0:
                acc[rows] = part
            else:
                acc[rows] = acc[rows] + part


def activation_tile(j, gb, down, slope, sums):
    total = jnp.zeros((1, TILE), F32)
    for r in range(gb.shape[0] // 256):
        rows = slice(r * 256, (r + 1) * 256)
        gact = dot(gb[rows], down[j * TILE : (j + 1) * TILE], NT)
        gpre = (gact * slope[j, rows].astype(F32)).astype(BF16)
        slope[j, rows] = gpre
        total = total + rowsum(gpre.astype(F32))
    sums[UPB + j : UPB + j + 1] = total


def weight_tile(j, gb, adapted, act, gpre, upd, dnd):
    gup = dot(adapted[...], gpre, TN).astype(BF16)
    share = TILE // BLOCKS
    for i in range(BLOCKS):
        upd[position(i, ORDERS[0]), j * share : (j + 1) * share] = gup[i * share : (i + 1) * share]
    gdn = dot(act, gb[...], TN).astype(BF16)
    share = 3 * TILE // BLOCKS
    at = j * TILE
    while at < (j + 1) * TILE:
        stop = min((at // share + 1) * share, (j + 1) * TILE)
        first = at % share
        dnd[position(at // share, ORDERS[1]), first : first + stop - at] = gdn[
            at - j * TILE : stop - j * TILE
        ]
        at = stop


def norm_backward(gad, normed, inv, small, clip, grad_out, v):
    n = normed.astype(F32)
    width = n.shape[1]
    scale = small[pl.ds(SCALE + clip, 1)]
    g_shift = rowsum(gad)
    g_scale = rowsum(gad * n)
    gn = gad * scale
    m1 = jnp.mean(gn, axis=-1, keepdims=True)
    m2 = jnp.mean(gn * n, axis=-1, keepdims=True)
    gc = (gn - m1 - n * m2) * wide(inv, width)
    g_conv = rowsum(gc)
    total = grad_out
    g_taps = []
    for k in range(7):
        moved = shifted(gc, 3 - k)
        total = total + moved * small[k : k + 1]
        g_taps.append(rowsum(moved * v))
    return total.astype(BF16), jnp.concatenate(g_taps + [g_conv], axis=0), g_scale, g_shift


def place_weights(sec, block, up_own, up_got, down_own, down_got, up, down, sems, start):
    def go(up_from, down_from):
        for source, target, sem in ((up_from, up, sems.at[0]), (down_from, down, sems.at[1])):
            copy = pltpu.make_async_copy(source, target, sem)
            copy.start() if start else copy.wait()

    if not start:
        go(up_own, down_own)
        return

    @pl.when(sec[0] == block)
    def _():
        go(up_own, down_own)

    @pl.when(sec[0] != block)
    def _():
        go(up_got, down_got)


def route(sec, upd, dnd, keep, send, sems, start):
    def go(kept, sent):
        for source, target, sem in ((kept, keep, sems.at[0]), (sent, send, sems.at[1])):
            copy = pltpu.make_async_copy(source, target, sem)
            copy.start() if start else copy.wait()

    if not start:
        go(upd, dnd)
        return

    @pl.when(sec[0] == 0)
    def _():
        go(upd, dnd)

    @pl.when(sec[0] != 0)
    def _():
        go(dnd, upd)


def main_body(
    sec, valid, own_small, got_small, tokens, cot, up_own, up_got, down_own, down_got,
    sums0, sums1, gin1, gb0_hbm, adapted_hbm, normed_hbm, inv_hbm, out_own, out_send, act_hbm,
    gpre_hbm, keep, send, small0_out,
    up0, down0, up1, down1, act0, slope0, act1, slope1, acc, adapted0, normed, inv, adapted1, branch0,
    gb, v, grad, out0, out1, small0, small1, upd, dnd, sems, pieces,
):
    clips = acc.shape[0] // 256
    mine = pl.ds(sec[0] * clips, clips)
    loads = (
        pltpu.make_async_copy(tokens.at[mine], v, sems.at[6, 0]),
        pltpu.make_async_copy(cot.at[mine], grad, sems.at[6, 1]),
    )
    loads[0].start()
    weights = (up_own, up_got, down_own, down_got)
    place_weights(sec, 0, *weights, up0, down0, sems.at[0], True)
    place_weights(sec, 1, *weights, up1, down1, sems.at[1], True)
    loads[1].start()
    first = sec[0] == 0
    small0[...] = pick(first, own_small[...], got_small[...])
    small1[...] = pick(first, got_small[...], own_small[...])
    small0_out[...] = small0[...]
    sums0[...] = jnp.zeros_like(sums0)
    sums1[...] = jnp.zeros_like(sums1)
    loads[0].wait()

    def begin(r):
        rows = pl.ds(pl.multiple_of(r * 256, 256), 256)
        adapted0[rows], normed[rows], inv[rows] = normalize(v[r].astype(F32), small0, r)

    pl.loop(0, clips)(begin)
    saves = [
        pltpu.make_async_copy(source, target, sems.at[7 + n // 2, n % 2])
        for n, (source, target) in enumerate(
            ((normed, normed_hbm), (inv, inv_hbm), (adapted0, adapted_hbm), (act0, act_hbm))
        )
    ]
    for copy in saves[:3]:
        copy.start()
    place_weights(sec, 0, *weights, up0, down0, sems.at[0], False)
    forward_tiles(adapted0, up0, down0, small0, act0, slope0, acc)
    saves[3].start()
    saves[0].wait()
    saves[1].wait()

    def between(r):
        rows = pl.ds(pl.multiple_of(r * 256, 256), 256)
        branch = acc[rows] + small0[DOWNB : DOWNB + 1]
        branch0[rows] = branch
        result = (v[r].astype(F32) + small0[GAIN : GAIN + 1] * branch).astype(BF16)
        out0[r] = result
        adapted1[rows], normed[rows], inv[rows] = normalize(result.astype(F32), small1, r)

    pl.loop(0, clips)(between)
    place_weights(sec, 1, *weights, up1, down1, sems.at[1], False)
    forward_tiles(adapted1, up1, down1, small1, act1, slope1, acc)
    loads[1].wait()

    def top(r):
        rows = pl.ds(pl.multiple_of(r * 256, 256), 256)
        branch = acc[rows] + small1[DOWNB : DOWNB + 1]
        gain = small1[GAIN : GAIN + 1]
        out1[r] = (out0[r].astype(F32) + gain * branch).astype(BF16)
        above = grad[r].astype(F32) * valid[sec[0] * clips + r].astype(F32)
        low = (above * gain).astype(BF16)
        gb[rows] = low
        sums1[GAIN : GAIN + 1] += rowsum(above * branch)
        sums1[DOWNB : DOWNB + 1] += rowsum(low.astype(F32))

    pl.loop(0, clips)(top)
    half_own = out_own.at[mine]
    route(sec, out0, out1, half_own, out_send, sems.at[4], True)
    for j in range(3):
        activation_tile(j, gb, down1, slope1, sums1)
        for r in range(clips):
            rows = slice(r * 256, (r + 1) * 256)
            part = dot(slope1[j, rows], up1[:, j * TILE : (j + 1) * TILE], NT)
            acc[rows] = part if j == 0 else acc[rows] + part
        weight_tile(j, gb, adapted1, act1[j], slope1[j], upd, dnd)
    route(sec, upd, dnd, keep, send, sems.at[3], True)

    def move(r):
        rows = pl.ds(pl.multiple_of(r * 256, 256), 256)
        return (
            pltpu.make_async_copy(grad.at[r], gin1.at[r], pieces.at[0, r]),
            pltpu.make_async_copy(gb.at[rows], gb0_hbm.at[rows], pieces.at[1, r]),
        )

    def under(r):
        rows = pl.ds(pl.multiple_of(r * 256, 256), 256)
        above = grad[r].astype(F32) * valid[sec[0] * clips + r].astype(F32)
        gin, smalls, g_scale, g_shift = norm_backward(
            acc[rows], normed[rows], inv[rows], small1, r, above, out0[r].astype(F32)
        )
        grad[r] = gin
        sums1[TAPS : TAPS + 8] += smalls
        sums1[pl.ds(SCALE + r, 1)] = g_scale
        sums1[pl.ds(SHIFT + r, 1)] = g_shift
        grad0 = gin.astype(F32)
        low = (grad0 * small0[GAIN : GAIN + 1]).astype(BF16)
        gb[rows] = low
        for copy in move(r):
            copy.start()
        sums0[GAIN : GAIN + 1] += rowsum(grad0 * branch0[rows])
        sums0[DOWNB : DOWNB + 1] += rowsum(low.astype(F32))

    pl.loop(0, clips)(under)
    tiles = []
    for j in range(3):
        activation_tile(j, gb, down0, slope0, sums0)
        tiles.append(pltpu.make_async_copy(slope0.at[j], gpre_hbm.at[j], sems.at[5 + j // 2 * 4, j % 2]))
        tiles[-1].start()
    route(sec, out0, out1, half_own, out_send, sems.at[4], False)
    route(sec, upd, dnd, keep, send, sems.at[3], False)
    for copy in saves[2:] + tiles:
        copy.wait()
    for r in range(clips):
        for copy in move(r):
            copy.wait()


def weights_body(sec, gb, adapted, act, gpre, keep, send, upd, dnd, sems):
    step = pl.program_id(0)
    for j in range(3):

        @pl.when(step == j)
        def _():
            weight_tile(j, gb, adapted, act[0], gpre[0], upd, dnd)

    @pl.when(step == 2)
    def _():
        route(sec, upd, dnd, keep, send, sems, True)
        route(sec, upd, dnd, keep, send, sems, False)


def last_body(
    first, sec, gpre, up_own, up_got, normed, inv, small, grad_out, tokens, sums_in, *rest
):
    gin, away, sums, up, sem = rest[-5:]
    step = pl.program_id(0)
    clip = first + step

    @pl.when(step == 0)
    def _():
        sums[...] = sums_in[...]

        @pl.when(sec[0] == 0)
        def _():
            pltpu.make_async_copy(up_own, up, sem).start()

        @pl.when(sec[0] != 0)
        def _():
            pltpu.make_async_copy(up_got, up, sem).start()

        pltpu.make_async_copy(up_own, up, sem).wait()

    gad = dot(gpre[0], up[:, :TILE], NT)
    for j in range(1, 3):
        gad = gad + dot(gpre[j], up[:, j * TILE : (j + 1) * TILE], NT)
    above = grad_out[0]
    out, smalls, g_scale, g_shift = norm_backward(
        gad, normed[...], inv[...], small, clip, above.astype(F32), tokens[0].astype(F32)
    )
    gin[0] = jnp.where(sec[0] == 0, out, above)
    away[0] = jnp.where(sec[0] == 0, above, out)
    sums[TAPS : TAPS + 8] += smalls
    sums[pl.ds(SCALE + clip, 1)] = g_scale
    sums[pl.ds(SHIFT + clip, 1)] = g_shift


def pick(first, a, b):
    return jnp.where(first, a, b)


def bit_of(spot, step):
    low, high = ORDERS[0][step], ORDERS[1][step]
    return (spot[1] >> (low if low == high else pick(spot[0] == 0, low, high))) & 1


def region(spot, level, step):
    start = 0
    for i in range(level, min(step, 4)):
        start = start + bit_of(spot, i) * (8 >> i)
    if step < 4:
        start = start + (1 - bit_of(spot, step)) * (8 >> step)
    return start


GATHER = (1, 2, 3, 0)


def gather_slot(spot):
    slot = 0
    for i, step in enumerate(GATHER):
        slot = slot + bit_of(spot, step) * (1 << i)
    return slot


def fetch(copies, source, first, rows, target, sem):
    copies.append(pltpu.make_async_copy(source.at[pl.ds(first, rows)], target, sem))
    copies[-1].start()


def add_up(buffers, rows):
    total = buffers[0][:rows].astype(F32)
    for buffer in buffers[1:]:
        total = total + buffer[:rows].astype(F32)
    return total


def pack_body(step, blocks, bases, share, extras, sec, place, speaker, *refs):
    spot = (sec[0], place[0])
    levels = step + 2
    sources = [refs[b * levels : (b + 1) * levels] for b in range(blocks)]
    refs = refs[blocks * levels :]
    count = 1 if step == 4 else 8 >> step
    rows = count * share
    extra_in, refs = refs[: 3 * extras], refs[3 * extras :]
    packet, refs = (refs[0], refs[1:]) if step < 4 or extras else (None, refs)
    if extras:
        smalls_out, refs = refs[0], refs[1:]
    if step == 4:
        mine, away, refs = refs[0], refs[1], refs[2:]
    buffers, tail, sems = refs
    copies = []
    for b in range(blocks):
        for n in range(levels):
            level = max(n - 1, 0)
            base = bases[b][level]
            first = pl.multiple_of((region(spot, level, step)) * share + base, 32)
            fetch(copies, sources[b][n], first, rows, buffers.at[b, n], sems.at[b, n])
    head = blocks * rows if step < 4 else 0
    if extras and step == 1:
        sums0, sums1, got = extra_in
        own = pick(spot[0] == 0, sums0[...], sums1[...])
        other = got[...]
        low = pick(spot[0] == 0, own[SCALE:], other[SCALE:])
        high = pick(spot[0] == 0, other[SCALE:], own[SCALE:])
        packet[head : head + 16] = jnp.concatenate([low, high], axis=0).astype(BF16)
        width = own.shape[1]
        lane = lax.broadcasted_iota(jnp.int32, (1, width), 1)
        mine_lane = (lane >> 4) == gather_slot(spot)
        which = ((lane >> 3) & 1) * 4 + (lane & 3)
        code = jnp.zeros((1, width), jnp.int32)
        for c in range(8):
            code = jnp.where(mine_lane & (which == c), speaker[c], code)
        smalls_out[...] = own[:SCALE] + other[:SCALE]
        smalls_out[13:14] = (code >> 6).astype(F32)
        smalls_out[14:15] = (code & 63).astype(F32)
        packet[head + 16 : head + 32] = smalls_out[...].astype(BF16)
    elif extras:
        before, after, smalls_in = extra_in
        size = 16 << (step - 2)
        old_head = blocks * (8 >> (step - 1)) * share
        bit = bit_of(spot, GATHER[step - 2])
        for n, (source, spot_bit) in enumerate(((before, bit), (after, 1 - bit))):
            target = packet.at[pl.ds(pl.multiple_of(head + spot_bit * size, 16), size)]
            fetch(copies, source, old_head, size, target, sems.at[2, n])
        fetch(copies, after, old_head + size, 16, tail, sems.at[2, 2])
    for b in range(blocks):
        for n in range(levels):
            copies[b * levels + n].wait()
        total = add_up([buffers.at[b, n] for n in range(levels)], rows)
        if step < 4:
            packet[b * rows : (b + 1) * rows] = total.astype(BF16)
        else:
            @pl.when(spot[0] == b)
            def _():
                mine[...] = total

            @pl.when(spot[0] != b)
            def _():
                away[...] = total
    if extras and step > 1:
        for copy in copies[blocks * levels :]:
            copy.wait()
        smalls_out[...] = smalls_in[...] + tail[...].astype(F32)
        packet[head + 2 * size : head + 2 * size + 16] = smalls_out[...].astype(BF16)


def finish_body(
    sec, place, before, after, smalls_in, mine, got, scale, shift, up, down, taps, conv, upb, downb, gain,
    rows_of, tail, sems,
):
    spot = (sec[0], place[0])
    size = rows_of.shape[0] // 2
    bit = bit_of(spot, GATHER[3])
    copies = []
    for n, (source, spot_bit) in enumerate(((before, bit), (after, 1 - bit))):
        target = rows_of.at[pl.ds(pl.multiple_of(spot_bit * size, 16), size)]
        fetch(copies, source, 0, size, target, sems.at[n])
    fetch(copies, after, size, 16, tail, sems.at[2])
    first = spot[0] == 0
    one, two = mine[...], got[...]
    up_rows = up.shape[0]
    ups = pick(first, one, two)
    for j in range(3):
        up[:, j * TILE : (j + 1) * TILE] = ups[j * up_rows : (j + 1) * up_rows]
    down[...] = pick(first, two, one)
    for copy in copies:
        copy.wait()
    total = smalls_in[...] + tail[...].astype(F32)
    owned = scale.shape[0]
    count = 2 * size
    who = total[13:14, :count] * 64.0 + total[14:15, :count]
    wanted = lax.broadcasted_iota(jnp.int32, (owned, count), 0) + spot[1] * owned
    hit = who == wanted.astype(F32)
    kind = (lax.broadcasted_iota(jnp.int32, (owned, count), 1) >> 2) & 1
    for k, out in enumerate((scale, shift)):
        out[...] = dot(jnp.where(hit & (kind == k), 1.0, 0.0).astype(BF16), rows_of[...], NN)
    width = total.shape[1]
    lanes = width // BLOCKS
    turn = lax.rem(BLOCKS - spot[1], BLOCKS)
    cut = pltpu.roll(total, turn * lanes, 1)[:, :lanes]
    for k in range(7):
        taps[k] = cut[k : k + 1]
    conv[...] = cut[CONV : CONV + 1]
    downb[...] = cut[DOWNB : DOWNB + 1]
    gain[...] = cut[GAIN : GAIN + 1]
    line = jnp.concatenate([total[UPB + k : UPB + k + 1] for k in range(3)], axis=1)
    upb[...] = pltpu.roll(line, turn * 3 * lanes, 1)[:, : 3 * lanes]


def struct(shape, dtype):
    return jax.ShapeDtypeStruct(shape, dtype)


def params(limit):
    return pltpu.CompilerParams(vmem_limit_bytes=limit * 1024 * 1024)


def cost(flops, moved):
    return pl.CostEstimate(flops=int(flops), bytes_accessed=int(moved), transcendentals=0)


def local(
    tokens, out_cotangent, speaker, valid, conv_weight, conv_bias, scale_table, shift_table,
    up_weight, up_bias, down_weight, down_bias, layer_scale,
):
    section = lax.axis_index("section").astype(jnp.int32)
    place = lax.axis_index("dp").astype(jnp.int32)
    devices = lax.axis_size("dp")
    first_section = section == 0
    clips, frames, width = tokens.shape
    hidden = up_weight.shape[2]
    table_rows = scale_table.shape[1]
    half = clips // 2
    rows = half * frames
    sec = section[None]
    swap = [(0, 1), (1, 0)]

    own_small, other_small = pl.pallas_call(
        prep_body,
        out_shape=[struct((SMALL, width), F32)] * 2,
        in_specs=[SMEM, SMEM] + [VMEM] * 5 + [ANY] * 2,
        out_specs=[VMEM] * 2,
        scratch_shapes=[pltpu.SemaphoreType.DMA((2, 2, half))],
        name="prep",
    )(
        sec, speaker, conv_weight.transpose(1, 0, 2), conv_bias, up_bias, down_bias, layer_scale,
        scale_table, shift_table,
    )
    got_small = lax.ppermute(other_small, "section", swap)
    up_own, down_own = up_weight[0], down_weight[0]
    up_got = lax.ppermute(up_own, "section", swap)
    down_got = lax.ppermute(down_own, "section", swap)
    clip_block = (1, frames, width)
    whole_small = pl.BlockSpec((SMALL, width), lambda c, sec: (0, 0))
    half_struct = struct((half, frames, width), BF16)
    whole_struct = struct((clips, frames, width), BF16)
    small_struct = struct((SMALL, width), F32)
    flat_struct = struct((rows, width), BF16)
    tiles = hidden // TILE
    tiled = (tiles, rows, TILE)
    share = hidden // BLOCKS
    gradient = (BLOCKS, share, width)
    gradient_struct = struct(gradient, BF16)
    product = 2 * rows * width * hidden

    def full(*shape):
        return pl.BlockSpec(shape, lambda i, *_: (0,) * len(shape))

    (
        sums0, sums1, gin1, gb0, adapted0, normed0, inv0, out_own, out_send, act0, gpre0, keep1, send1,
        small0,
    ) = pl.pallas_call(
        main_body,
        out_shape=[
            small_struct, small_struct, half_struct, flat_struct, flat_struct, flat_struct,
            struct((rows, 128), F32), whole_struct, half_struct, struct(tiled, BF16),
            struct(tiled, BF16), gradient_struct, gradient_struct, small_struct,
        ],
        in_specs=[SMEM, SMEM, VMEM, VMEM] + [ANY] * 6,
        out_specs=[VMEM, VMEM] + [ANY] * 11 + [VMEM],
        scratch_shapes=[
            pltpu.VMEM((width, hidden), BF16),
            pltpu.VMEM((hidden, width), BF16),
            pltpu.VMEM((width, hidden), BF16),
            pltpu.VMEM((hidden, width), BF16),
            pltpu.VMEM(tiled, BF16),
            pltpu.VMEM(tiled, BF16),
            pltpu.VMEM(tiled, BF16),
            pltpu.VMEM(tiled, BF16),
            pltpu.VMEM((rows, width), F32),
            pltpu.VMEM((rows, width), BF16),
            pltpu.VMEM((rows, width), BF16),
            pltpu.VMEM((rows, 128), F32),
            pltpu.VMEM((rows, width), BF16),
            pltpu.VMEM((rows, width), F32),
            pltpu.VMEM((rows, width), BF16),
            pltpu.VMEM((half, frames, width), BF16),
            pltpu.VMEM((half, frames, width), BF16),
            pltpu.VMEM((half, frames, width), BF16),
            pltpu.VMEM((half, frames, width), BF16),
            pltpu.VMEM((SMALL, width), F32),
            pltpu.VMEM((SMALL, width), F32),
            pltpu.VMEM(gradient, BF16),
            pltpu.VMEM(gradient, BF16),
            pltpu.SemaphoreType.DMA((10, 2)),
            pltpu.SemaphoreType.DMA((2, half)),
        ],
        compiler_params=params(42),
        cost_estimate=cost(9 * product, 24 << 20),
        name="main",
    )(
        sec, valid, own_small, got_small, tokens, out_cotangent, up_own, up_got, down_own, down_got
    )
    got1 = lax.ppermute(send1, "section", swap)
    got_out = lax.ppermute(out_send, "section", swap)

    tile_spec = pl.BlockSpec((1, rows, TILE), lambda j, *_: (j, 0, 0))
    keep0, send0 = pl.pallas_call(
        weights_body,
        grid_spec=pltpu.PrefetchScalarGridSpec(
            num_scalar_prefetch=1,
            grid=(tiles,),
            in_specs=[full(rows, width), full(rows, width), tile_spec, tile_spec],
            out_specs=[ANY, ANY],
            scratch_shapes=[
                pltpu.VMEM(gradient, BF16),
                pltpu.VMEM(gradient, BF16),
                pltpu.SemaphoreType.DMA((2,)),
            ],
        ),
        out_shape=[gradient_struct, gradient_struct],
        compiler_params=params(20),
        cost_estimate=cost(2 * product, 12 << 20),
        name="weights",
    )(sec, gb0, adapted0, act0, gpre0)
    got0 = lax.ppermute(send0, "section", swap)

    def last(first, count, sums, *others):
        def at(c):
            return first + c

        return pl.pallas_call(
            functools.partial(last_body, first),
            grid_spec=pltpu.PrefetchScalarGridSpec(
                num_scalar_prefetch=1,
                grid=(count,),
                in_specs=[
                    pl.BlockSpec((tiles, frames, TILE), lambda c, sec: (0, at(c), 0)),
                    ANY,
                    ANY,
                    pl.BlockSpec((frames, width), lambda c, sec: (at(c), 0)),
                    pl.BlockSpec((frames, 128), lambda c, sec: (at(c), 0)),
                    whole_small,
                    pl.BlockSpec(clip_block, lambda c, sec: (at(c), 0, 0)),
                    pl.BlockSpec(clip_block, lambda c, sec: (sec[0] * half + at(c), 0, 0)),
                    whole_small,
                ]
                + [ANY] * len(others),
                out_specs=[
                    pl.BlockSpec(clip_block, lambda c, sec: (sec[0] * half + at(c), 0, 0)),
                    pl.BlockSpec(clip_block, lambda c, sec: (at(c), 0, 0)),
                    whole_small,
                ],
                scratch_shapes=[pltpu.VMEM((width, hidden), BF16), pltpu.SemaphoreType.DMA],
            ),
            out_shape=[whole_struct, half_struct, small_struct],
            input_output_aliases={10 + i: i for i in range(len(others))},
            compiler_params=params(14),
            cost_estimate=cost(8 * product, 12 << 20),
            name="last",
        )(sec, gpre0, up_own, up_got, normed0, inv0, small0, gin1, tokens, sums, *others)

    gin_own, gin_send, sums0 = last(0, half, sums0)
    got_gin = lax.ppermute(gin_send, "section", swap)
    got_sums = lax.ppermute(pick(first_section, sums1, sums0), "section", swap)

    def joined(whole, got):
        return lax.dynamic_update_slice(whole, got, ((1 - section) * half, 0, 0))[None]

    block_outputs = joined(out_own, got_out)
    input_grads = joined(gin_own, got_gin)
    pairs = [[keep0, got0], [keep1, got1]]
    if devices == BLOCKS:
        outs = halved(sec, place[None], speaker, pairs, sums0, sums1, got_sums, table_rows)
    else:
        outs = scattered(section, place, devices, speaker, pairs, sums0, sums1, got_sums, table_rows)
    return (block_outputs, input_grads) + outs


def exchanged(packet, step):
    devices = lax.axis_size("dp")
    moves = [
        (s * devices + i, s * devices + (i ^ (1 << ORDERS[s][step])))
        for s in range(2)
        for i in range(devices)
    ]
    return lax.ppermute(packet, PAIR, moves)


def halved(sec, place, speaker, pairs, sums0, sums1, got_sums, table_rows):
    _, share, width = pairs[0][0].shape
    pairs = [[piece.reshape(-1, width) for piece in pair] for pair in pairs]

    def pack(step, block_sources, bases, extra_in):
        blocks = len(block_sources)
        levels = step + 2
        count = 1 if step == 4 else 8 >> step
        rows = count * share
        extras = len(extra_in) > 0
        outs = []
        size = (8 << step) if extras else 0
        length = (blocks * rows if step < 4 else 0) + (size + 16 if extras else 0)
        outs.append(struct((length, width), BF16))
        if extras:
            outs.append(struct((SCALE, width), F32))
        if step == 4:
            outs += [struct((share, width), F32)] * 2
        if extras and step == 1:
            extra_specs = [VMEM] * 3
        elif extras:
            extra_specs = [ANY, ANY, VMEM]
        else:
            extra_specs = []
        return pl.pallas_call(
            functools.partial(pack_body, step, blocks, bases, share, int(extras)),
            out_shape=outs,
            in_specs=[SMEM, SMEM, SMEM] + [ANY] * (blocks * levels) + extra_specs,
            out_specs=[VMEM] * len(outs),
            scratch_shapes=[
                pltpu.VMEM((blocks, levels, rows, width), BF16),
                pltpu.VMEM((16, width), BF16),
                pltpu.SemaphoreType.DMA((3, max(levels, 3))),
            ],
            compiler_params=params(8),
            cost_estimate=cost(0, 4 << 20),
        )(sec, place, speaker, *[x for sources in block_sources for x in sources], *extra_in)

    for b in (1, 0):
        (packet,) = pack(0, [pairs[b]], [[0]], [])
        pairs[b].append(exchanged(packet, 0))
    bases = [[0, 0], [0, 0]]
    extra_in = [sums0, sums1, got_sums]
    for step in range(1, 4):
        packet, smalls = pack(step, pairs, bases, extra_in)
        got = exchanged(packet, step)
        rows = (8 >> step) * share
        for b in range(2):
            pairs[b].append(got)
            bases[b].append(b * rows)
        bases = [list(x) for x in bases]
        extra_in = [packet, got, smalls]
    packet, smalls, mine, away = pack(4, pairs, bases, extra_in)
    got = exchanged(packet, 0)
    got_share = lax.ppermute(away, "section", [(0, 1), (1, 0)])
    owned = table_rows // BLOCKS
    up_rows = width // BLOCKS
    lanes = width // BLOCKS
    one = struct((1, lanes), F32)
    scale, shift, up, down, taps, conv, upb, downb, gain = pl.pallas_call(
        finish_body,
        out_shape=[
            struct((owned, width), F32),
            struct((owned, width), F32),
            struct((up_rows, 3 * TILE), F32),
            struct((share, width), F32),
            struct((7, 1, lanes), F32),
            one,
            struct((1, 3 * lanes), F32),
            one,
            one,
        ],
        in_specs=[SMEM, SMEM, ANY, ANY, VMEM, VMEM, VMEM],
        out_specs=[VMEM] * 9,
        scratch_shapes=[
            pltpu.VMEM((16 * BLOCKS, width), BF16),
            pltpu.VMEM((16, width), BF16),
            pltpu.SemaphoreType.DMA((3,)),
        ],
        compiler_params=params(8),
        name="finish",
    )(sec, place, packet, got, smalls, mine, got_share)
    return (
        taps.transpose(1, 0, 2), conv, scale[None], shift[None], up[None], upb, down[None], downb, gain
    )


def scattered(section, place, devices, speaker, pairs, sums0, sums1, got_sums, table_rows):
    first_section = section == 0
    own_sums = pick(first_section, sums0, sums1)
    smalls = lax.psum(own_sums[:SCALE] + got_sums[:SCALE], "dp")
    clip_rows = jnp.stack([own_sums[SCALE:], got_sums[SCALE:]])
    clip_rows = pick(first_section, clip_rows, clip_rows[::-1]).astype(BF16)
    clips = speaker.shape[0]
    width = clip_rows.shape[-1]
    clip_rows = clip_rows.reshape(2, 2, clips // 2, width).transpose(1, 0, 2, 3).reshape(2, clips, width)
    gathered = lax.all_gather(clip_rows, "dp", axis=1, tiled=True)
    who = lax.all_gather(speaker, "dp", tiled=True)
    owned = table_rows // devices
    wanted = place * owned + jnp.arange(owned, dtype=jnp.int32)
    chosen = (who[None, :] == wanted[:, None]).astype(BF16)
    tables = [jnp.dot(chosen, gathered[k], preferred_element_type=F32) for k in range(2)]
    natural = []
    for order in ORDERS:
        natural.append(
            jnp.stack(
                [
                    jnp.stack([pair[0][position(i, order)].astype(F32) + pair[1][position(i, order)].astype(F32) for i in range(BLOCKS)])
                    for pair in pairs
                ]
            )
        )
    blocks, _, rows, width = natural[0].shape
    tiles = rows * BLOCKS // TILE
    up = natural[0].reshape(blocks, BLOCKS, tiles, rows // tiles, TILE).transpose(0, 1, 3, 2, 4)
    flat = pick(
        first_section, up.reshape(blocks, devices, -1), natural[1].reshape(blocks, devices, -1)
    )
    share = lax.psum_scatter(flat, "dp", scatter_dimension=1, tiled=True)[:, 0]
    own_share = lax.dynamic_index_in_dim(share, section, 0, keepdims=False)
    got_share = lax.ppermute(
        lax.dynamic_index_in_dim(share, 1 - section, 0, keepdims=False), "section", [(0, 1), (1, 0)]
    )
    up_share = pick(first_section, own_share, got_share).reshape(width // devices, -1)
    down_share = pick(first_section, got_share, own_share).reshape(-1, width)
    lanes = width // devices
    own_lanes = lax.dynamic_slice_in_dim(smalls, place * lanes, lanes, 1)
    upb = lax.dynamic_slice_in_dim(smalls[UPB : UPB + 3].reshape(-1), place * 3 * lanes, 3 * lanes, 0)
    return (
        own_lanes[TAPS : TAPS + 7][None],
        own_lanes[CONV : CONV + 1],
        tables[0][None],
        tables[1][None],
        up_share[None],
        upb[None],
        down_share[None],
        own_lanes[DOWNB : DOWNB + 1],
        own_lanes[GAIN : GAIN + 1],
    )


def solution(mesh):
    placed = (
        P("dp", None, None),
        P("dp", None, None),
        P("dp"),
        P("dp"),
        P("section", None, None),
        P("section", None),
        P("section", None, None),
        P("section", None, None),
        P("section", None, None),
        P("section", None),
        P("section", None, None),
        P("section", None),
        P("section", None),
    )

    return jax.shard_map(
        local,
        mesh=mesh,
        in_specs=placed,
        out_specs=(
            P("section", "dp", None, None),
            P("section", "dp", None, None),
            P("section", None, "dp"),
            P("section", "dp"),
            P("section", "dp", None),
            P("section", "dp", None),
            P("section", "dp", None),
            P("section", "dp"),
            P("section", "dp", None),
            P("section", "dp"),
            P("section", "dp"),
        ),
        check_vma=False,
    )
```

```python
import functools

import jax
import jax.numpy as jnp
from jax import lax
from jax.experimental import pallas as pl
from jax.experimental.pallas import tpu as pltpu
from jax.sharding import PartitionSpec as P


F32 = jnp.float32
BF16 = jnp.bfloat16
PAIR = ("section", "dp")
TILE = 512
LAST_MIB = 48
HALF_ROOT = 0.7071067811865476
DENSITY = 0.3989422804014327
BLOCKS = 16
ORDERS = ((0, 1, 2, 3), (2, 0, 1, 3))
ANY = pl.BlockSpec(memory_space=pl.ANY)
HBM = pl.BlockSpec(memory_space=pltpu.HBM)
VMEM = pl.BlockSpec(memory_space=pltpu.VMEM)
SMEM = pl.BlockSpec(memory_space=pltpu.SMEM)

TAPS, CONV, UPB, DOWNB, GAIN, SCALE, SHIFT, SMALL = 0, 7, 8, 11, 12, 16, 20, 24


def position(block, order):
    place = 0
    for bit in order:
        place = 2 * place + ((block >> bit) & 1)
    return place


def dot(a, b, dims):
    return lax.dot_general(a, b, (dims, ((), ())), preferred_element_type=F32)


NN = ((1,), (0,))
NT = ((1,), (1,))
TN = ((0,), (0,))


OFFSETS = (-3, -2, -1, 1, 2, 3)


def set_shifts(shifts):
    frames = shifts.shape[1]
    row = lax.broadcasted_iota(jnp.int32, (frames, frames), 0)
    col = lax.broadcasted_iota(jnp.int32, (frames, frames), 1)
    for n, offset in enumerate(OFFSETS):
        shifts[n * frames : (n + 1) * frames] = jnp.where(col == row + offset, 1.0, 0.0).astype(BF16)


def shifted(shifts, x, offset):
    frames = x.shape[0]
    n = OFFSETS.index(offset)
    return dot(shifts[n * frames : (n + 1) * frames], x, NN)


def wide(x, width):
    return jnp.concatenate([x] * (width // 128), axis=1)


def rowsum(x):
    return jnp.sum(x, axis=0, keepdims=True)


def normalize(x, small, clip, shifts):
    conv = small[CONV : CONV + 1] + x.astype(F32) * small[3:4]
    for offset in OFFSETS:
        conv = conv + shifted(shifts, x, offset) * small[offset + 3 : offset + 4]
    centred = conv - jnp.mean(conv, axis=-1, keepdims=True)
    inv = lax.rsqrt(jnp.mean(centred * centred, axis=-1, keepdims=True) + 1e-06)
    normed = centred * inv
    scale = small[pl.ds(SCALE + clip, 1)]
    shift = small[pl.ds(SHIFT + clip, 1)]
    adapted = (normed * scale + shift).astype(BF16)
    return adapted, normed.astype(BF16), jnp.broadcast_to(inv, (x.shape[0], 128))


def prep_body(sec, speaker, taps, conv, upb, downb, gain, scale_hbm, shift_hbm, own, other, sems):
    width = own.shape[1]
    half = SMALL - SHIFT
    copies = []
    for side, out in enumerate((own, other)):
        first = (sec[0] if side == 0 else 1 - sec[0]) * half
        for clip in range(half):
            row = speaker[first + clip]
            for kind, table in enumerate((scale_hbm, shift_hbm)):
                copies.append(
                    pltpu.make_async_copy(
                        table.at[0, pl.ds(row, 1)],
                        out.at[pl.ds((SCALE, SHIFT)[kind] + clip, 1)],
                        sems.at[side, kind, clip],
                    )
                )
    for copy in copies:
        copy.start()
    for out in (own, other):
        for k in range(7):
            out[TAPS + k : TAPS + k + 1] = taps[k]
        out[CONV : CONV + 1] = conv[...]
        for k in range(DOWNB - UPB):
            out[UPB + k : UPB + k + 1] = upb[:, k * width : (k + 1) * width]
        out[DOWNB : DOWNB + 1] = downb[...]
        out[GAIN : GAIN + 1] = gain[...]
        out[GAIN + 1 : SCALE] = jnp.zeros((SCALE - GAIN - 1, width), F32)
    for copy in copies:
        copy.wait()


def forward_tiles(adapted, up, down, small, act, slope, acc):
    steps = [(j, r) for j in range(3) for r in range(acc.shape[0] // 256)]

    def hidden(j, r):
        part = dot(adapted[r * 256 : (r + 1) * 256], up[:, j * TILE : (j + 1) * TILE], NN)
        return part + small[UPB + j : UPB + j + 1]

    ahead = hidden(*steps[0])
    for n, (j, r) in enumerate(steps):
        rows = slice(r * 256, (r + 1) * 256)
        pre = ahead
        if n + 1 < len(steps):
            ahead = hidden(*steps[n + 1])
        phi = 0.5 * lax.erf(pre * HALF_ROOT) + 0.5
        low = (pre * phi).astype(BF16)
        act[j, rows] = low
        slope[j, rows] = (phi + pre * (DENSITY * jnp.exp(-0.5 * pre * pre))).astype(BF16)
        part = dot(low, down[j * TILE : (j + 1) * TILE], NN)
        acc[rows] = part if j == 0 else acc[rows] + part


def activation_tile(j, gb, down, slope, sums):
    total = jnp.zeros((1, TILE), F32)
    for r in range(gb.shape[0] // 256):
        rows = slice(r * 256, (r + 1) * 256)
        gact = dot(gb[rows], down[j * TILE : (j + 1) * TILE], NT)
        gpre = (gact * slope[j, rows].astype(F32)).astype(BF16)
        slope[j, rows] = gpre
        total = total + rowsum(gpre.astype(F32))
    sums[UPB + j : UPB + j + 1] = total


def down_pieces(j):
    share = 3 * TILE // BLOCKS
    at, pieces = j * TILE, []
    while at < (j + 1) * TILE:
        stop = min((at // share + 1) * share, (j + 1) * TILE)
        pieces.append((position(at // share, ORDERS[1]), at % share, stop - at, at - j * TILE))
        at = stop
    return pieces


def weight_tile(j, gb, adapted, act, gpre, upd, dnd):
    gup = dot(adapted[...], gpre, TN).astype(BF16)
    share = TILE // BLOCKS
    for i in range(BLOCKS):
        upd[position(i, ORDERS[0]), j * share : (j + 1) * share] = gup[i * share : (i + 1) * share]
    gdn = dot(act, gb[...], TN).astype(BF16)
    for block, first, rows, at in down_pieces(j):
        dnd[block, first : first + rows] = gdn[at : at + rows]


def norm_backward(gad, normed, inv, small, clip, grad_out, v, shifts):
    n = normed.astype(F32)
    width = n.shape[1]
    scale = small[pl.ds(SCALE + clip, 1)]
    g_shift = rowsum(gad)
    g_scale = rowsum(gad * n)
    gn = gad * scale
    m1 = jnp.mean(gn, axis=-1, keepdims=True)
    m2 = jnp.mean(gn * n, axis=-1, keepdims=True)
    gc = (gn - m1 - n * m2) * wide(inv, width)
    low = gc.astype(BF16)
    total = grad_out + gc * small[3:4]
    v = v.astype(F32)
    g_taps = []
    for k in range(7):
        if k == 3:
            g_taps.append(rowsum(gc * v))
            continue
        moved = shifted(shifts, low, 3 - k)
        total = total + moved * small[k : k + 1]
        g_taps.append(rowsum(moved * v))
    return total.astype(BF16), jnp.concatenate(g_taps + [rowsum(gc)], axis=0), g_scale, g_shift


def place_weights(sec, block, up_own, up_got, down_own, down_got, up, down, sems, start):
    def go(up_from, down_from):
        for source, target, sem in ((up_from, up, sems.at[0]), (down_from, down, sems.at[1])):
            copy = pltpu.make_async_copy(source, target, sem)
            copy.start() if start else copy.wait()

    if not start:
        go(up_own, down_own)
        return

    @pl.when(sec[0] == block)
    def _():
        go(up_own, down_own)

    @pl.when(sec[0] != block)
    def _():
        go(up_got, down_got)


def route(sec, upd, dnd, keep, send, sems, start):
    def go(kept, sent):
        for source, target, sem in ((kept, keep, sems.at[0]), (sent, send, sems.at[1])):
            copy = pltpu.make_async_copy(source, target, sem)
            copy.start() if start else copy.wait()

    if not start:
        go(upd, dnd)
        return

    @pl.when(sec[0] == 0)
    def _():
        go(upd, dnd)

    @pl.when(sec[0] != 0)
    def _():
        go(dnd, upd)


def main_body(
    sec, valid, own_small, got_small, tokens, cot, up_own, up_got, down_own, down_got,
    sums0, sums1, gin1, gb0_hbm, adapted_hbm, normed_hbm, inv_hbm, out_own, out_send, act_hbm,
    gpre_hbm, keep, send, small0_out,
    up0, down0, up1, down1, act0, slope0, act1, slope1, acc, adapted0, normed, inv, adapted1, branch0,
    gb, v, grad, out0, out1, small0, small1, shifts, upd, dnd, sems, pieces,
):
    clips = acc.shape[0] // 256
    mine = pl.ds(sec[0] * clips, clips)
    loads = (
        pltpu.make_async_copy(tokens.at[mine], v, sems.at[6, 0]),
        pltpu.make_async_copy(cot.at[mine], grad, sems.at[6, 1]),
    )
    loads[0].start()
    weights = (up_own, up_got, down_own, down_got)
    place_weights(sec, 0, *weights, up0, down0, sems.at[0], True)
    place_weights(sec, 1, *weights, up1, down1, sems.at[1], True)
    loads[1].start()
    first = sec[0] == 0
    small0[...] = pick(first, own_small[...], got_small[...])
    small1[...] = pick(first, got_small[...], own_small[...])
    small0_out[...] = small0[...]
    sums0[...] = jnp.zeros_like(sums0)
    sums1[...] = jnp.zeros_like(sums1)
    set_shifts(shifts)
    loads[0].wait()

    def begin(r):
        rows = pl.ds(pl.multiple_of(r * 256, 256), 256)
        adapted0[rows], normed[rows], inv[rows] = normalize(v[r], small0, r, shifts)

    pl.loop(0, clips, unroll=True)(begin)
    saves = [
        pltpu.make_async_copy(source, target, sems.at[7 + n // 2, n % 2])
        for n, (source, target) in enumerate(
            ((normed, normed_hbm), (inv, inv_hbm), (adapted0, adapted_hbm), (act0, act_hbm))
        )
    ]
    for copy in saves[:3]:
        copy.start()
    place_weights(sec, 0, *weights, up0, down0, sems.at[0], False)
    forward_tiles(adapted0, up0, down0, small0, act0, slope0, acc)
    saves[3].start()
    saves[0].wait()
    saves[1].wait()

    def between(r):
        rows = pl.ds(pl.multiple_of(r * 256, 256), 256)
        branch = acc[rows] + small0[DOWNB : DOWNB + 1]
        branch0[rows] = branch
        result = (v[r].astype(F32) + small0[GAIN : GAIN + 1] * branch).astype(BF16)
        out0[r] = result
        adapted1[rows], normed[rows], inv[rows] = normalize(result, small1, r, shifts)

    pl.loop(0, clips, unroll=True)(between)
    place_weights(sec, 1, *weights, up1, down1, sems.at[1], False)
    forward_tiles(adapted1, up1, down1, small1, act1, slope1, acc)
    loads[1].wait()

    def top(r):
        rows = pl.ds(pl.multiple_of(r * 256, 256), 256)
        branch = acc[rows] + small1[DOWNB : DOWNB + 1]
        gain = small1[GAIN : GAIN + 1]
        out1[r] = (out0[r].astype(F32) + gain * branch).astype(BF16)
        above = grad[r].astype(F32) * valid[sec[0] * clips + r].astype(F32)
        low = (above * gain).astype(BF16)
        gb[rows] = low
        sums1[GAIN : GAIN + 1] += rowsum(above * branch)
        sums1[DOWNB : DOWNB + 1] += rowsum(low.astype(F32))

    pl.loop(0, clips)(top)
    half_own = out_own.at[mine]
    route(sec, out0, out1, half_own, out_send, sems.at[4], True)
    for j in range(3):
        activation_tile(j, gb, down1, slope1, sums1)
        for r in range(clips):
            rows = slice(r * 256, (r + 1) * 256)
            part = dot(slope1[j, rows], up1[:, j * TILE : (j + 1) * TILE], NT)
            acc[rows] = part if j == 0 else acc[rows] + part
        weight_tile(j, gb, adapted1, act1[j], slope1[j], upd, dnd)
    route(sec, upd, dnd, keep, send, sems.at[3], True)

    def move(r):
        rows = pl.ds(pl.multiple_of(r * 256, 256), 256)
        return (
            pltpu.make_async_copy(grad.at[r], gin1.at[r], pieces.at[0, r]),
            pltpu.make_async_copy(gb.at[rows], gb0_hbm.at[rows], pieces.at[1, r]),
        )

    def under(r):
        rows = pl.ds(pl.multiple_of(r * 256, 256), 256)
        above = grad[r].astype(F32) * valid[sec[0] * clips + r].astype(F32)
        gin, smalls, g_scale, g_shift = norm_backward(
            acc[rows], normed[rows], inv[rows], small1, r, above, out0[r], shifts
        )
        grad[r] = gin
        sums1[TAPS : TAPS + 8] += smalls
        sums1[pl.ds(SCALE + r, 1)] = g_scale
        sums1[pl.ds(SHIFT + r, 1)] = g_shift
        grad0 = gin.astype(F32)
        low = (grad0 * small0[GAIN : GAIN + 1]).astype(BF16)
        gb[rows] = low
        for copy in move(r):
            copy.start()
        sums0[GAIN : GAIN + 1] += rowsum(grad0 * branch0[rows])
        sums0[DOWNB : DOWNB + 1] += rowsum(low.astype(F32))

    pl.loop(0, clips)(under)
    tiles = []
    for j in range(3):
        activation_tile(j, gb, down0, slope0, sums0)
        tiles.append(pltpu.make_async_copy(slope0.at[j], gpre_hbm.at[j], sems.at[5 + j // 2 * 4, j % 2]))
        tiles[-1].start()
    route(sec, out0, out1, half_own, out_send, sems.at[4], False)
    route(sec, upd, dnd, keep, send, sems.at[3], False)
    for copy in saves[2:] + tiles:
        copy.wait()
    for r in range(clips):
        for copy in move(r):
            copy.wait()


def weights_body(sec, gb, adapted, act, gpre, keep, send, upd, dnd, sems):
    step = pl.program_id(0)
    share = TILE // BLOCKS

    def copies(j, up_to, down_to):
        part = pl.ds(j * share, share)
        moves = [pltpu.make_async_copy(upd.at[:, part], up_to.at[:, part], sems.at[j, 0])]
        for n, (block, first, rows, _) in enumerate(down_pieces(j)):
            part = pl.ds(first, rows)
            moves.append(
                pltpu.make_async_copy(dnd.at[block, part], down_to.at[block, part], sems.at[j, 1 + n])
            )
        return moves

    for j in range(3):

        @pl.when(step == j)
        def _():
            weight_tile(j, gb, adapted, act[0], gpre[0], upd, dnd)

            @pl.when(sec[0] == 0)
            def _():
                for copy in copies(j, keep, send):
                    copy.start()

            @pl.when(sec[0] != 0)
            def _():
                for copy in copies(j, send, keep):
                    copy.start()

    @pl.when(step == 2)
    def _():
        for j in range(3):
            for copy in copies(j, keep, send):
                copy.wait()


def last_body(
    first, sec, gpre, up_own, up_got, normed, inv, small, grad_out, tokens, sums_in, *rest
):
    gin, away, sums, up, shifts, sem = rest[-6:]
    step = pl.program_id(0)
    clip = first + step

    @pl.when(step == 0)
    def _():
        sums[...] = sums_in[...]

        @pl.when(sec[0] == 0)
        def _():
            pltpu.make_async_copy(up_own, up, sem).start()

        @pl.when(sec[0] != 0)
        def _():
            pltpu.make_async_copy(up_got, up, sem).start()

        set_shifts(shifts)
        pltpu.make_async_copy(up_own, up, sem).wait()

    gad = dot(gpre[0], up[:, :TILE], NT)
    for j in range(1, 3):
        gad = gad + dot(gpre[j], up[:, j * TILE : (j + 1) * TILE], NT)
    above = grad_out[0]
    out, smalls, g_scale, g_shift = norm_backward(
        gad, normed[...], inv[...], small, clip, above.astype(F32), tokens[0], shifts
    )
    gin[0] = jnp.where(sec[0] == 0, out, above)
    away[0] = jnp.where(sec[0] == 0, above, out)
    sums[TAPS : TAPS + 8] += smalls
    sums[pl.ds(SCALE + clip, 1)] = g_scale
    sums[pl.ds(SHIFT + clip, 1)] = g_shift


def pick(first, a, b):
    return jnp.where(first, a, b)


def bit_of(spot, step):
    low, high = ORDERS[0][step], ORDERS[1][step]
    return (spot[1] >> (low if low == high else pick(spot[0] == 0, low, high))) & 1


GATHER = (1, 2, 3, 0)


def gather_slot(spot):
    slot = 0
    for i, step in enumerate(GATHER):
        slot = slot + bit_of(spot, step) * (1 << i)
    return slot


def fetch(copies, source, first, rows, target, sem):
    copies.append(pltpu.make_async_copy(source.at[pl.ds(first, rows)], target, sem))
    copies[-1].start()


def split_body(share, sec, place, keep, got, packet, kept, came, sems):
    rows = 8 * share
    first = pl.multiple_of((1 - bit_of((sec[0], place[0]), 0)) * rows, rows)
    pieces = 4
    size = rows // pieces
    copies = []
    for n in range(pieces):
        for m, (source, target) in enumerate(((keep, kept), (got, came))):
            fetch(
                copies, source, first + n * size, size, target.at[pl.ds(n * size, size)], sems.at[n, m]
            )
    for n in range(pieces):
        copies[2 * n].wait()
        copies[2 * n + 1].wait()
        part = slice(n * size, (n + 1) * size)
        packet[part] = (kept[part].astype(F32) + came[part].astype(F32)).astype(BF16)


def pack_body(step, share, sec, place, speaker, total0, total1, *refs):
    spot = (sec[0], place[0])
    count = 8 >> step
    rows = max(count, 1) * share
    head = 2 * count * share
    totals = (total0, total1)
    if step == 1:
        latest = [(refs[0], 0), (refs[1], 0)]
        refs = refs[2:]
    else:
        latest = [(refs[0], 0), (refs[0], (16 >> step) * share)]
    extra_in, refs = refs[:3], refs[3:]
    packet, smalls_out = refs[:2]
    for b in range(2):
        source, base = latest[b]
        if step < 4:
            first = pl.multiple_of((1 - bit_of(spot, step)) * rows, 32)
            away = totals[b][pl.ds(first, rows)] + source[pl.ds(base + first, rows)].astype(F32)
            packet[b * rows : (b + 1) * rows] = away.astype(BF16)
        else:
            whole = totals[b][...] + source[base : base + rows].astype(F32)
            for target, mine in ((refs[2], True), (refs[3], False)):

                @pl.when((spot[0] == b) == mine)
                def _():
                    target[...] = whole

    if step == 1:
        sums0, sums1, got = extra_in
        own = pick(spot[0] == 0, sums0[...], sums1[...])
        other = got[...]
        low = pick(spot[0] == 0, own[SCALE:], other[SCALE:])
        high = pick(spot[0] == 0, other[SCALE:], own[SCALE:])
        packet[head : head + 16] = jnp.concatenate([low, high], axis=0).astype(BF16)
        width = own.shape[1]
        lane = lax.broadcasted_iota(jnp.int32, (1, width), 1)
        mine_lane = (lane >> 4) == gather_slot(spot)
        which = ((lane >> 3) & 1) * 4 + (lane & 3)
        code = jnp.zeros((1, width), jnp.int32)
        for c in range(8):
            code = jnp.where(mine_lane & (which == c), speaker[c], code)
        smalls_out[...] = own[:SCALE] + other[:SCALE]
        smalls_out[13:14] = (code >> 6).astype(F32)
        smalls_out[14:15] = (code & 63).astype(F32)
        tail = head + 16
    else:
        after, before, smalls_in = extra_in
        size = 16 << (step - 2)
        old_head = (16 >> step) * 2 * share
        bit = bit_of(spot, GATHER[step - 2])
        for source, side in ((before, bit), (after, 1 - bit)):
            packet[pl.ds(pl.multiple_of(head + side * size, 16), size)] = source[
                old_head : old_head + size
            ]
        smalls_out[...] = smalls_in[...] + after[old_head + size : old_head + size + 16].astype(F32)
        tail = head + 2 * size
    packet[tail : tail + 16] = smalls_out[...].astype(BF16)


def finish_body(
    sec, place, before, after, smalls_in, mine, got, scale, shift, up, down, taps, conv, upb, downb, gain,
    rows_of,
):
    spot = (sec[0], place[0])
    size = rows_of.shape[0] // 2
    bit = bit_of(spot, GATHER[3])
    for source, side in ((before, bit), (after, 1 - bit)):
        rows_of[pl.ds(pl.multiple_of(side * size, 16), size)] = source[:size]
    first = spot[0] == 0
    one, two = mine[...], got[...]
    up_rows = up.shape[0]
    ups = pick(first, one, two)
    for j in range(3):
        up[:, j * TILE : (j + 1) * TILE] = ups[j * up_rows : (j + 1) * up_rows]
    down[...] = pick(first, two, one)
    total = smalls_in[...] + after[size:].astype(F32)
    owned = scale.shape[0]
    count = 2 * size
    who = total[13:14, :count] * 64.0 + total[14:15, :count]
    wanted = lax.broadcasted_iota(jnp.int32, (owned, count), 0) + spot[1] * owned
    hit = who == wanted.astype(F32)
    kind = (lax.broadcasted_iota(jnp.int32, (owned, count), 1) >> 2) & 1
    for k, out in enumerate((scale, shift)):
        out[...] = dot(jnp.where(hit & (kind == k), 1.0, 0.0).astype(BF16), rows_of[...], NN)
    width = total.shape[1]
    lanes = width // BLOCKS
    turn = lax.rem(BLOCKS - spot[1], BLOCKS)
    cut = pltpu.roll(total, turn * lanes, 1)[:, :lanes]
    for k in range(7):
        taps[k] = cut[k : k + 1]
    conv[...] = cut[CONV : CONV + 1]
    downb[...] = cut[DOWNB : DOWNB + 1]
    gain[...] = cut[GAIN : GAIN + 1]
    line = jnp.concatenate([total[UPB + k : UPB + k + 1] for k in range(3)], axis=1)
    upb[...] = pltpu.roll(line, turn * 3 * lanes, 1)[:, : 3 * lanes]


def struct(shape, dtype):
    return jax.ShapeDtypeStruct(shape, dtype)


def params(limit):
    return pltpu.CompilerParams(vmem_limit_bytes=limit * 1024 * 1024)


def cost(flops, moved):
    return pl.CostEstimate(flops=int(flops), bytes_accessed=int(moved), transcendentals=0)


def local(
    tokens, out_cotangent, speaker, valid, conv_weight, conv_bias, scale_table, shift_table,
    up_weight, up_bias, down_weight, down_bias, layer_scale,
):
    section = lax.axis_index("section").astype(jnp.int32)
    place = lax.axis_index("dp").astype(jnp.int32)
    devices = lax.axis_size("dp")
    first_section = section == 0
    clips, frames, width = tokens.shape
    hidden = up_weight.shape[2]
    table_rows = scale_table.shape[1]
    half = clips // 2
    rows = half * frames
    sec = section[None]
    swap = [(0, 1), (1, 0)]

    own_small, other_small = pl.pallas_call(
        prep_body,
        out_shape=[struct((SMALL, width), F32)] * 2,
        in_specs=[SMEM, SMEM] + [VMEM] * 5 + [ANY] * 2,
        out_specs=[VMEM] * 2,
        scratch_shapes=[pltpu.SemaphoreType.DMA((2, 2, half))],
        name="prep",
    )(
        sec, speaker, conv_weight.transpose(1, 0, 2), conv_bias, up_bias, down_bias, layer_scale,
        scale_table, shift_table,
    )
    got_small = lax.ppermute(other_small, "section", swap)
    up_own, down_own = up_weight[0], down_weight[0]
    up_got = lax.ppermute(up_own, "section", swap)
    down_got = lax.ppermute(down_own, "section", swap)
    clip_block = (1, frames, width)
    whole_small = pl.BlockSpec((SMALL, width), lambda c, sec: (0, 0))
    half_struct = struct((half, frames, width), BF16)
    whole_struct = struct((clips, frames, width), BF16)
    small_struct = struct((SMALL, width), F32)
    flat_struct = struct((rows, width), BF16)
    tiles = hidden // TILE
    tiled = (tiles, rows, TILE)
    share = hidden // BLOCKS
    gradient = (BLOCKS, share, width)
    gradient_struct = struct(gradient, BF16)
    product = 2 * rows * width * hidden

    def full(*shape):
        return pl.BlockSpec(shape, lambda i, *_: (0,) * len(shape))

    (
        sums0, sums1, gin1, gb0, adapted0, normed0, inv0, out_own, out_send, act0, gpre0, keep1, send1,
        small0,
    ) = pl.pallas_call(
        main_body,
        out_shape=[
            small_struct, small_struct, half_struct, flat_struct, flat_struct, flat_struct,
            struct((rows, 128), F32), whole_struct, half_struct, struct(tiled, BF16),
            struct(tiled, BF16), gradient_struct, gradient_struct, small_struct,
        ],
        in_specs=[SMEM, SMEM, VMEM, VMEM, HBM, HBM, HBM, ANY, HBM, ANY],
        out_specs=[VMEM, VMEM] + [HBM] * 11 + [VMEM],
        scratch_shapes=[
            pltpu.VMEM((width, hidden), BF16),
            pltpu.VMEM((hidden, width), BF16),
            pltpu.VMEM((width, hidden), BF16),
            pltpu.VMEM((hidden, width), BF16),
            pltpu.VMEM(tiled, BF16),
            pltpu.VMEM(tiled, BF16),
            pltpu.VMEM(tiled, BF16),
            pltpu.VMEM(tiled, BF16),
            pltpu.VMEM((rows, width), F32),
            pltpu.VMEM((rows, width), BF16),
            pltpu.VMEM((rows, width), BF16),
            pltpu.VMEM((rows, 128), F32),
            pltpu.VMEM((rows, width), BF16),
            pltpu.VMEM((rows, width), F32),
            pltpu.VMEM((rows, width), BF16),
            pltpu.VMEM((half, frames, width), BF16),
            pltpu.VMEM((half, frames, width), BF16),
            pltpu.VMEM((half, frames, width), BF16),
            pltpu.VMEM((half, frames, width), BF16),
            pltpu.VMEM((SMALL, width), F32),
            pltpu.VMEM((SMALL, width), F32),
            pltpu.VMEM((len(OFFSETS) * frames, frames), BF16),
            pltpu.VMEM(gradient, BF16),
            pltpu.VMEM(gradient, BF16),
            pltpu.SemaphoreType.DMA((10, 2)),
            pltpu.SemaphoreType.DMA((2, half)),
        ],
        compiler_params=params(46),
        cost_estimate=cost(9 * product, 24 << 20),
        name="main",
    )(
        sec, valid, own_small, got_small, tokens, out_cotangent, up_own, up_got, down_own, down_got
    )
    got1 = lax.ppermute(send1, "section", swap)
    got_out = lax.ppermute(out_send, "section", swap)

    tile_spec = pl.BlockSpec((1, rows, TILE), lambda j, *_: (j, 0, 0))
    keep0, send0 = pl.pallas_call(
        weights_body,
        grid_spec=pltpu.PrefetchScalarGridSpec(
            num_scalar_prefetch=1,
            grid=(tiles,),
            in_specs=[full(rows, width), full(rows, width), tile_spec, tile_spec],
            out_specs=[HBM, HBM],
            scratch_shapes=[
                pltpu.VMEM(gradient, BF16),
                pltpu.VMEM(gradient, BF16),
                pltpu.SemaphoreType.DMA((3, 8)),
            ],
        ),
        out_shape=[gradient_struct, gradient_struct],
        compiler_params=params(60),
        cost_estimate=cost(2 * product, 12 << 20),
        name="weights",
    )(sec, gb0, adapted0, act0, gpre0)
    got0 = lax.ppermute(send0, "section", swap)

    def last(first, count, sums, *others):
        def at(c):
            return first + c

        return pl.pallas_call(
            functools.partial(last_body, first),
            grid_spec=pltpu.PrefetchScalarGridSpec(
                num_scalar_prefetch=1,
                grid=(count,),
                in_specs=[
                    pl.BlockSpec((tiles, frames, TILE), lambda c, sec: (0, at(c), 0)),
                    HBM,
                    ANY,
                    pl.BlockSpec((frames, width), lambda c, sec: (at(c), 0)),
                    pl.BlockSpec((frames, 128), lambda c, sec: (at(c), 0)),
                    whole_small,
                    pl.BlockSpec(clip_block, lambda c, sec: (at(c), 0, 0)),
                    pl.BlockSpec(clip_block, lambda c, sec: (sec[0] * half + at(c), 0, 0)),
                    whole_small,
                ]
                + [ANY] * len(others),
                out_specs=[
                    pl.BlockSpec(clip_block, lambda c, sec: (sec[0] * half + at(c), 0, 0)),
                    pl.BlockSpec(clip_block, lambda c, sec: (at(c), 0, 0)),
                    whole_small,
                ],
                scratch_shapes=[
                    pltpu.VMEM((width, hidden), BF16),
                    pltpu.VMEM((len(OFFSETS) * frames, frames), BF16),
                    pltpu.SemaphoreType.DMA,
                ],
            ),
            out_shape=[whole_struct, half_struct, small_struct],
            input_output_aliases={10 + i: i for i in range(len(others))},
            compiler_params=params(LAST_MIB),
            cost_estimate=cost(8 * product, 12 << 20),
            name="last",
        )(sec, gpre0, up_own, up_got, normed0, inv0, small0, gin1, tokens, sums, *others)

    gin_own, gin_send, sums0 = last(0, half, sums0)
    got_gin = lax.ppermute(gin_send, "section", swap)
    got_sums = lax.ppermute(pick(first_section, sums1, sums0), "section", swap)

    def joined(whole, got):
        return lax.dynamic_update_slice(whole, got, ((1 - section) * half, 0, 0))[None]

    block_outputs = joined(out_own, got_out)
    input_grads = joined(gin_own, got_gin)
    pairs = [[keep0, got0], [keep1, got1]]
    if devices == BLOCKS:
        outs = halved(sec, place[None], speaker, pairs, sums0, sums1, got_sums, table_rows)
    else:
        outs = scattered(section, place, devices, speaker, pairs, sums0, sums1, got_sums, table_rows)
    return (block_outputs, input_grads) + outs


def exchanged(packet, step):
    devices = lax.axis_size("dp")
    moves = [
        (s * devices + i, s * devices + (i ^ (1 << ORDERS[s][step])))
        for s in range(2)
        for i in range(devices)
    ]
    return lax.ppermute(packet, PAIR, moves)


def halved(sec, place, speaker, pairs, sums0, sums1, got_sums, table_rows):
    _, share, width = pairs[0][0].shape
    pairs = [[piece.reshape(-1, width) for piece in pair] for pair in pairs]
    spot = (sec[0], place[0])
    rows = 8 * share

    def split(b):
        return pl.pallas_call(
            functools.partial(split_body, share),
            out_shape=struct((rows, width), BF16),
            in_specs=[SMEM, SMEM, HBM, ANY],
            out_specs=VMEM,
            scratch_shapes=[
                pltpu.VMEM((rows, width), BF16),
                pltpu.VMEM((rows, width), BF16),
                pltpu.SemaphoreType.DMA((4, 2)),
            ],
            compiler_params=params(6),
            cost_estimate=cost(0, 4 << 20),
        )(sec, place, *pairs[b])

    def part(array, first, count):
        return lax.dynamic_slice_in_dim(array, first, count, 0).astype(F32)

    latest, totals = [None, None], [None, None]
    for b in (1, 0):
        packet = split(b)
        latest[b] = exchanged(packet, 0)
    for b in (1, 0):
        totals[b] = sum(part(piece, bit_of(spot, 0) * rows, rows) for piece in pairs[b])

    def pack(step, extra_in):
        count = 8 >> step
        length = 2 * count * share + (8 << step) + 16
        outs = [struct((length, width), BF16), struct((SCALE, width), F32)]
        if step == 4:
            outs += [struct((share, width), F32)] * 2
        operands = list(totals) + (latest if step == 1 else []) + extra_in
        return pl.pallas_call(
            functools.partial(pack_body, step, share),
            out_shape=outs,
            in_specs=[SMEM, SMEM, SMEM] + [VMEM] * len(operands),
            out_specs=[VMEM] * len(outs),
            compiler_params=params(8),
            cost_estimate=cost(0, 2 << 20),
        )(sec, place, speaker, *operands)

    packet, smalls = pack(1, [sums0, sums1, got_sums])
    for step in range(1, 4):
        got = exchanged(packet, step)
        rows = (8 >> step) * share
        first = bit_of(spot, step) * rows
        bases = (0, 0) if step == 1 else (0, 2 * rows)
        totals = [
            part(totals[b], first, rows) + part(latest[b], bases[b] + first, rows) for b in range(2)
        ]
        latest = [got, got]
        packet, smalls, *shares = pack(step + 1, [got, packet, smalls])
    mine, away = shares
    got = exchanged(packet, 0)
    got_share = lax.ppermute(away, "section", [(0, 1), (1, 0)])
    owned = table_rows // BLOCKS
    up_rows = width // BLOCKS
    lanes = width // BLOCKS
    one = struct((1, lanes), F32)
    scale, shift, up, down, taps, conv, upb, downb, gain = pl.pallas_call(
        finish_body,
        out_shape=[
            struct((owned, width), F32),
            struct((owned, width), F32),
            struct((up_rows, 3 * TILE), F32),
            struct((share, width), F32),
            struct((7, 1, lanes), F32),
            one,
            struct((1, 3 * lanes), F32),
            one,
            one,
        ],
        in_specs=[SMEM, SMEM] + [VMEM] * 5,
        out_specs=[VMEM] * 9,
        scratch_shapes=[pltpu.VMEM((16 * BLOCKS, width), BF16)],
        compiler_params=params(8),
        name="finish",
    )(sec, place, packet, got, smalls, mine, got_share)
    return (
        taps.transpose(1, 0, 2), conv, scale[None], shift[None], up[None], upb, down[None], downb, gain
    )


def scattered(section, place, devices, speaker, pairs, sums0, sums1, got_sums, table_rows):
    first_section = section == 0
    own_sums = pick(first_section, sums0, sums1)
    smalls = lax.psum(own_sums[:SCALE] + got_sums[:SCALE], "dp")
    clip_rows = jnp.stack([own_sums[SCALE:], got_sums[SCALE:]])
    clip_rows = pick(first_section, clip_rows, clip_rows[::-1]).astype(BF16)
    clips = speaker.shape[0]
    width = clip_rows.shape[-1]
    clip_rows = clip_rows.reshape(2, 2, clips // 2, width).transpose(1, 0, 2, 3).reshape(2, clips, width)
    gathered = lax.all_gather(clip_rows, "dp", axis=1, tiled=True)
    who = lax.all_gather(speaker, "dp", tiled=True)
    owned = table_rows // devices
    wanted = place * owned + jnp.arange(owned, dtype=jnp.int32)
    chosen = (who[None, :] == wanted[:, None]).astype(BF16)
    tables = [jnp.dot(chosen, gathered[k], preferred_element_type=F32) for k in range(2)]
    natural = []
    for order in ORDERS:
        natural.append(
            jnp.stack(
                [
                    jnp.stack([pair[0][position(i, order)].astype(F32) + pair[1][position(i, order)].astype(F32) for i in range(BLOCKS)])
                    for pair in pairs
                ]
            )
        )
    blocks, _, rows, width = natural[0].shape
    tiles = rows * BLOCKS // TILE
    up = natural[0].reshape(blocks, BLOCKS, tiles, rows // tiles, TILE).transpose(0, 1, 3, 2, 4)
    flat = pick(
        first_section, up.reshape(blocks, devices, -1), natural[1].reshape(blocks, devices, -1)
    )
    share = lax.psum_scatter(flat, "dp", scatter_dimension=1, tiled=True)[:, 0]
    own_share = lax.dynamic_index_in_dim(share, section, 0, keepdims=False)
    got_share = lax.ppermute(
        lax.dynamic_index_in_dim(share, 1 - section, 0, keepdims=False), "section", [(0, 1), (1, 0)]
    )
    up_share = pick(first_section, own_share, got_share).reshape(width // devices, -1)
    down_share = pick(first_section, got_share, own_share).reshape(-1, width)
    lanes = width // devices
    own_lanes = lax.dynamic_slice_in_dim(smalls, place * lanes, lanes, 1)
    upb = lax.dynamic_slice_in_dim(smalls[UPB : UPB + 3].reshape(-1), place * 3 * lanes, 3 * lanes, 0)
    return (
        own_lanes[TAPS : TAPS + 7][None],
        own_lanes[CONV : CONV + 1],
        tables[0][None],
        tables[1][None],
        up_share[None],
        upb[None],
        down_share[None],
        own_lanes[DOWNB : DOWNB + 1],
        own_lanes[GAIN : GAIN + 1],
    )


def solution(mesh):
    placed = (
        P("dp", None, None),
        P("dp", None, None),
        P("dp"),
        P("dp"),
        P("section", None, None),
        P("section", None),
        P("section", None, None),
        P("section", None, None),
        P("section", None, None),
        P("section", None),
        P("section", None, None),
        P("section", None),
        P("section", None),
    )

    return jax.shard_map(
        local,
        mesh=mesh,
        in_specs=placed,
        out_specs=(
            P("section", "dp", None, None),
            P("section", "dp", None, None),
            P("section", None, "dp"),
            P("section", "dp"),
            P("section", "dp", None),
            P("section", "dp", None),
            P("section", "dp", None),
            P("section", "dp"),
            P("section", "dp", None),
            P("section", "dp"),
            P("section", "dp"),
        ),
        check_vma=False,
    )
```

```python
import functools

import jax
import jax.numpy as jnp
from jax import lax
from jax.experimental import pallas as pl
from jax.experimental.pallas import tpu as pltpu
from jax.sharding import PartitionSpec as P


F32 = jnp.float32
BF16 = jnp.bfloat16
PAIR = ("section", "dp")
TILE = 512
ALL_VMEM = 67043328
HALF_ROOT = 0.7071067811865476
DENSITY = 0.3989422804014327
BLOCKS = 16
ORDERS = ((0, 1, 2, 3), (2, 0, 1, 3))
ANY = pl.BlockSpec(memory_space=pl.ANY)
HBM = pl.BlockSpec(memory_space=pltpu.HBM)
VMEM = pl.BlockSpec(memory_space=pltpu.VMEM)
SMEM = pl.BlockSpec(memory_space=pltpu.SMEM)

TAPS, CONV, UPB, DOWNB, GAIN, SCALE, SHIFT, SMALL = 0, 7, 8, 11, 12, 16, 20, 24


def position(block, order):
    place = 0
    for bit in order:
        place = 2 * place + ((block >> bit) & 1)
    return place


def dot(a, b, dims):
    return lax.dot_general(a, b, (dims, ((), ())), preferred_element_type=F32)


NN = ((1,), (0,))
NT = ((1,), (1,))
TN = ((0,), (0,))


OFFSETS = (-3, -2, -1, 1, 2, 3)


def set_shifts(shifts):
    frames = shifts.shape[1]
    row = lax.broadcasted_iota(jnp.int32, (frames, frames), 0)
    col = lax.broadcasted_iota(jnp.int32, (frames, frames), 1)
    for n, offset in enumerate(OFFSETS):
        shifts[n * frames : (n + 1) * frames] = jnp.where(col == row + offset, 1.0, 0.0).astype(BF16)


def shifted(shifts, x, offset):
    frames = x.shape[0]
    n = OFFSETS.index(offset)
    return dot(shifts[n * frames : (n + 1) * frames], x, NN)


def wide(x, width):
    return jnp.concatenate([x] * (width // 128), axis=1)


def rowsum(x):
    return jnp.sum(x, axis=0, keepdims=True)


def normalize(x, small, clip, shifts):
    conv = small[CONV : CONV + 1] + x.astype(F32) * small[3:4]
    for offset in OFFSETS:
        conv = conv + shifted(shifts, x, offset) * small[offset + 3 : offset + 4]
    centred = conv - jnp.mean(conv, axis=-1, keepdims=True)
    inv = lax.rsqrt(jnp.mean(centred * centred, axis=-1, keepdims=True) + 1e-06)
    normed = centred * inv
    scale = small[pl.ds(SCALE + clip, 1)]
    shift = small[pl.ds(SHIFT + clip, 1)]
    adapted = (normed * scale + shift).astype(BF16)
    return adapted, normed.astype(BF16), jnp.broadcast_to(inv, (x.shape[0], 128))


def prep_body(sec, speaker, taps, conv, upb, downb, gain, scale_hbm, shift_hbm, own, other, sems):
    width = own.shape[1]
    half = SMALL - SHIFT
    copies = []
    for side, out in enumerate((own, other)):
        first = (sec[0] if side == 0 else 1 - sec[0]) * half
        for clip in range(half):
            row = speaker[first + clip]
            for kind, table in enumerate((scale_hbm, shift_hbm)):
                copies.append(
                    pltpu.make_async_copy(
                        table.at[0, pl.ds(row, 1)],
                        out.at[pl.ds((SCALE, SHIFT)[kind] + clip, 1)],
                        sems.at[side, kind, clip],
                    )
                )
    for copy in copies:
        copy.start()
    for out in (own, other):
        for k in range(7):
            out[TAPS + k : TAPS + k + 1] = taps[k]
        out[CONV : CONV + 1] = conv[...]
        for k in range(DOWNB - UPB):
            out[UPB + k : UPB + k + 1] = upb[:, k * width : (k + 1) * width]
        out[DOWNB : DOWNB + 1] = downb[...]
        out[GAIN : GAIN + 1] = gain[...]
        out[GAIN + 1 : SCALE] = jnp.zeros((SCALE - GAIN - 1, width), F32)
    for copy in copies:
        copy.wait()


def forward_tiles(adapted, up, down, small, act, slope, acc):
    steps = [(j, r) for j in range(3) for r in range(acc.shape[0] // 256)]

    def hidden(j, r):
        part = dot(adapted[r * 256 : (r + 1) * 256], up[:, j * TILE : (j + 1) * TILE], NN)
        return part + small[UPB + j : UPB + j + 1]

    ahead = hidden(*steps[0])
    for n, (j, r) in enumerate(steps):
        rows = slice(r * 256, (r + 1) * 256)
        pre = ahead
        if n + 1 < len(steps):
            ahead = hidden(*steps[n + 1])
        phi = 0.5 * lax.erf(pre * HALF_ROOT) + 0.5
        low = (pre * phi).astype(BF16)
        act[j, rows] = low
        slope[j, rows] = (phi + pre * (DENSITY * jnp.exp(-0.5 * pre * pre))).astype(BF16)
        part = dot(low, down[j * TILE : (j + 1) * TILE], NN)
        acc[rows] = part if j == 0 else acc[rows] + part


def activation_tile(j, gb, down, slope, sums):
    total = jnp.zeros((1, TILE), F32)
    for r in range(gb.shape[0] // 256):
        rows = slice(r * 256, (r + 1) * 256)
        gact = dot(gb[rows], down[j * TILE : (j + 1) * TILE], NT)
        gpre = (gact * slope[j, rows].astype(F32)).astype(BF16)
        slope[j, rows] = gpre
        total = total + rowsum(gpre.astype(F32))
    sums[UPB + j : UPB + j + 1] = total


def down_pieces(j):
    share = 3 * TILE // BLOCKS
    at, pieces = j * TILE, []
    while at < (j + 1) * TILE:
        stop = min((at // share + 1) * share, (j + 1) * TILE)
        pieces.append((position(at // share, ORDERS[1]), at % share, stop - at, at - j * TILE))
        at = stop
    return pieces


def weight_tile(j, gb, adapted, act, gpre, upd, dnd):
    gup = dot(adapted[...], gpre, TN).astype(BF16)
    share = TILE // BLOCKS
    for i in range(BLOCKS):
        upd[position(i, ORDERS[0]), j * share : (j + 1) * share] = gup[i * share : (i + 1) * share]
    gdn = dot(act, gb[...], TN).astype(BF16)
    for block, first, rows, at in down_pieces(j):
        dnd[block, first : first + rows] = gdn[at : at + rows]


def norm_backward(gad, normed, inv, small, clip, grad_out, v, shifts):
    n = normed.astype(F32)
    width = n.shape[1]
    scale = small[pl.ds(SCALE + clip, 1)]
    g_shift = rowsum(gad)
    g_scale = rowsum(gad * n)
    gn = gad * scale
    m1 = jnp.mean(gn, axis=-1, keepdims=True)
    m2 = jnp.mean(gn * n, axis=-1, keepdims=True)
    gc = (gn - m1 - n * m2) * wide(inv, width)
    low = gc.astype(BF16)
    total = grad_out + gc * small[3:4]
    v = v.astype(F32)
    g_taps = []
    for k in range(7):
        if k == 3:
            g_taps.append(rowsum(gc * v))
            continue
        moved = shifted(shifts, low, 3 - k)
        total = total + moved * small[k : k + 1]
        g_taps.append(rowsum(moved * v))
    return total.astype(BF16), jnp.concatenate(g_taps + [rowsum(gc)], axis=0), g_scale, g_shift


def place_weights(sec, block, up_own, up_got, down_own, down_got, up, down, sems, start):
    def go(up_from, down_from):
        for source, target, sem in ((up_from, up, sems.at[0]), (down_from, down, sems.at[1])):
            copy = pltpu.make_async_copy(source, target, sem)
            copy.start() if start else copy.wait()

    if not start:
        go(up_own, down_own)
        return

    @pl.when(sec[0] == block)
    def _():
        go(up_own, down_own)

    @pl.when(sec[0] != block)
    def _():
        go(up_got, down_got)


def route_tile(sec, j, upd, dnd, keep, send, sems, start):
    share = TILE // BLOCKS

    def go(up_to, down_to):
        part = pl.ds(j * share, share)
        copies = [pltpu.make_async_copy(upd.at[:, part], up_to.at[:, part], sems.at[j, 0])]
        for n, (block, first, rows, _) in enumerate(down_pieces(j)):
            part = pl.ds(first, rows)
            copies.append(
                pltpu.make_async_copy(dnd.at[block, part], down_to.at[block, part], sems.at[j, 1 + n])
            )
        for copy in copies:
            copy.start() if start else copy.wait()

    if not start:
        go(keep, send)
        return

    @pl.when(sec[0] == 0)
    def _():
        go(keep, send)

    @pl.when(sec[0] != 0)
    def _():
        go(send, keep)


def route(sec, upd, dnd, keep, send, sems, start):
    def go(kept, sent):
        for source, target, sem in ((kept, keep, sems.at[0]), (sent, send, sems.at[1])):
            copy = pltpu.make_async_copy(source, target, sem)
            copy.start() if start else copy.wait()

    if not start:
        go(upd, dnd)
        return

    @pl.when(sec[0] == 0)
    def _():
        go(upd, dnd)

    @pl.when(sec[0] != 0)
    def _():
        go(dnd, upd)


def main_body(
    sec, valid, own_small, got_small, tokens, cot, up_own, up_got, down_own, down_got,
    sums0, sums1, gin1, normed_hbm, inv_hbm, out_own, out_send, gpre_hbm, keep1, send1, keep0, send0,
    small0_out,
    up0, down0, up1, down1, act0, slope0, act1, slope1, acc, adapted0, normed, inv, adapted1, branch0,
    gb, v, grad, out0, out1, small0, small1, shifts, upd, dnd, upd0, dnd0, sems, pieces, parts,
):
    clips = acc.shape[0] // 256
    mine = pl.ds(sec[0] * clips, clips)
    loads = (
        pltpu.make_async_copy(tokens.at[mine], v, sems.at[6, 0]),
        pltpu.make_async_copy(cot.at[mine], grad, sems.at[6, 1]),
    )
    loads[0].start()
    weights = (up_own, up_got, down_own, down_got)
    place_weights(sec, 0, *weights, up0, down0, sems.at[0], True)
    place_weights(sec, 1, *weights, up1, down1, sems.at[1], True)
    loads[1].start()
    first = sec[0] == 0
    small0[...] = pick(first, own_small[...], got_small[...])
    small1[...] = pick(first, got_small[...], own_small[...])
    small0_out[...] = small0[...]
    sums0[...] = jnp.zeros_like(sums0)
    sums1[...] = jnp.zeros_like(sums1)
    set_shifts(shifts)
    loads[0].wait()

    def begin(r):
        rows = pl.ds(pl.multiple_of(r * 256, 256), 256)
        adapted0[rows], normed[rows], inv[rows] = normalize(v[r], small0, r, shifts)

    pl.loop(0, clips, unroll=True)(begin)
    saves = [
        pltpu.make_async_copy(source, target, sems.at[7 + n // 2, n % 2])
        for n, (source, target) in enumerate(
            ((normed, normed_hbm), (inv, inv_hbm))
        )
    ]
    for copy in saves:
        copy.start()
    place_weights(sec, 0, *weights, up0, down0, sems.at[0], False)
    forward_tiles(adapted0, up0, down0, small0, act0, slope0, acc)
    for copy in saves:
        copy.wait()

    def between(r):
        rows = pl.ds(pl.multiple_of(r * 256, 256), 256)
        branch = acc[rows] + small0[DOWNB : DOWNB + 1]
        branch0[rows] = branch
        result = (v[r].astype(F32) + small0[GAIN : GAIN + 1] * branch).astype(BF16)
        out0[r] = result
        adapted1[rows], normed[rows], inv[rows] = normalize(result, small1, r, shifts)

    pl.loop(0, clips, unroll=True)(between)
    place_weights(sec, 1, *weights, up1, down1, sems.at[1], False)
    forward_tiles(adapted1, up1, down1, small1, act1, slope1, acc)
    loads[1].wait()

    def top(r):
        rows = pl.ds(pl.multiple_of(r * 256, 256), 256)
        branch = acc[rows] + small1[DOWNB : DOWNB + 1]
        gain = small1[GAIN : GAIN + 1]
        out1[r] = (out0[r].astype(F32) + gain * branch).astype(BF16)
        above = grad[r].astype(F32) * valid[sec[0] * clips + r].astype(F32)
        low = (above * gain).astype(BF16)
        gb[rows] = low
        sums1[GAIN : GAIN + 1] += rowsum(above * branch)
        sums1[DOWNB : DOWNB + 1] += rowsum(low.astype(F32))

    pl.loop(0, clips)(top)
    half_own = out_own.at[mine]
    route(sec, out0, out1, half_own, out_send, sems.at[4], True)
    for j in range(3):
        activation_tile(j, gb, down1, slope1, sums1)
        for r in range(clips):
            rows = slice(r * 256, (r + 1) * 256)
            part = dot(slope1[j, rows], up1[:, j * TILE : (j + 1) * TILE], NT)
            acc[rows] = part if j == 0 else acc[rows] + part
        weight_tile(j, gb, adapted1, act1[j], slope1[j], upd, dnd)
    route(sec, upd, dnd, keep1, send1, sems.at[3], True)

    def move(r):
        return pltpu.make_async_copy(grad.at[r], gin1.at[r], pieces.at[r])

    def under(r):
        rows = pl.ds(pl.multiple_of(r * 256, 256), 256)
        above = grad[r].astype(F32) * valid[sec[0] * clips + r].astype(F32)
        gin, smalls, g_scale, g_shift = norm_backward(
            acc[rows], normed[rows], inv[rows], small1, r, above, out0[r], shifts
        )
        grad[r] = gin
        sums1[TAPS : TAPS + 8] += smalls
        sums1[pl.ds(SCALE + r, 1)] = g_scale
        sums1[pl.ds(SHIFT + r, 1)] = g_shift
        grad0 = gin.astype(F32)
        low = (grad0 * small0[GAIN : GAIN + 1]).astype(BF16)
        gb[rows] = low
        move(r).start()
        sums0[GAIN : GAIN + 1] += rowsum(grad0 * branch0[rows])
        sums0[DOWNB : DOWNB + 1] += rowsum(low.astype(F32))

    pl.loop(0, clips)(under)
    tiles = []
    for j in range(3):
        activation_tile(j, gb, down0, slope0, sums0)
        tiles.append(pltpu.make_async_copy(slope0.at[j], gpre_hbm.at[j], sems.at[5 + j // 2 * 3, j % 2]))
        tiles[-1].start()
        weight_tile(j, gb, adapted0, act0[j], slope0[j], upd0, dnd0)
        route_tile(sec, j, upd0, dnd0, keep0, send0, parts, True)
    route(sec, out0, out1, half_own, out_send, sems.at[4], False)
    route(sec, upd, dnd, keep1, send1, sems.at[3], False)
    for copy in tiles + [move(r) for r in range(clips)]:
        copy.wait()
    for j in range(3):
        route_tile(sec, j, upd0, dnd0, keep0, send0, parts, False)


def last_body(
    first, sec, gpre, up_own, up_got, normed, inv, small, grad_out, tokens, sums_in, *rest
):
    gin, away, sums, up, shifts, sem = rest[-6:]
    step = pl.program_id(0)
    clip = first + step

    @pl.when(step == 0)
    def _():
        sums[...] = sums_in[...]

        @pl.when(sec[0] == 0)
        def _():
            pltpu.make_async_copy(up_own, up, sem).start()

        @pl.when(sec[0] != 0)
        def _():
            pltpu.make_async_copy(up_got, up, sem).start()

        set_shifts(shifts)
        pltpu.make_async_copy(up_own, up, sem).wait()

    gad = dot(gpre[0], up[:, :TILE], NT)
    for j in range(1, 3):
        gad = gad + dot(gpre[j], up[:, j * TILE : (j + 1) * TILE], NT)
    above = grad_out[0]
    out, smalls, g_scale, g_shift = norm_backward(
        gad, normed[...], inv[...], small, clip, above.astype(F32), tokens[0], shifts
    )
    gin[0] = jnp.where(sec[0] == 0, out, above)
    away[0] = jnp.where(sec[0] == 0, above, out)
    sums[TAPS : TAPS + 8] += smalls
    sums[pl.ds(SCALE + clip, 1)] = g_scale
    sums[pl.ds(SHIFT + clip, 1)] = g_shift


def pick(first, a, b):
    return jnp.where(first, a, b)


def bit_of(spot, step):
    low, high = ORDERS[0][step], ORDERS[1][step]
    return (spot[1] >> (low if low == high else pick(spot[0] == 0, low, high))) & 1


GATHER = (1, 2, 3, 0)


def gather_slot(spot):
    slot = 0
    for i, step in enumerate(GATHER):
        slot = slot + bit_of(spot, step) * (1 << i)
    return slot


def fetch(copies, source, first, rows, target, sem):
    copies.append(pltpu.make_async_copy(source.at[pl.ds(first, rows)], target, sem))
    copies[-1].start()


def split_body(share, sec, place, keep, got, packet, kept, came, sems):
    rows = 8 * share
    first = pl.multiple_of((1 - bit_of((sec[0], place[0]), 0)) * rows, rows)
    pieces = 4
    size = rows // pieces
    copies = []
    for n in range(pieces):
        for m, (source, target) in enumerate(((keep, kept), (got, came))):
            fetch(
                copies, source, first + n * size, size, target.at[pl.ds(n * size, size)], sems.at[n, m]
            )
    for n in range(pieces):
        copies[2 * n].wait()
        copies[2 * n + 1].wait()
        part = slice(n * size, (n + 1) * size)
        packet[part] = (kept[part].astype(F32) + came[part].astype(F32)).astype(BF16)


def pack_body(step, share, sec, place, speaker, total0, total1, *refs):
    spot = (sec[0], place[0])
    count = 8 >> step
    rows = max(count, 1) * share
    head = 2 * count * share
    totals = (total0, total1)
    if step == 1:
        latest = [(refs[0], 0), (refs[1], 0)]
        refs = refs[2:]
    else:
        latest = [(refs[0], 0), (refs[0], (16 >> step) * share)]
    extra_in, refs = refs[:3], refs[3:]
    packet, smalls_out = refs[:2]
    for b in range(2):
        source, base = latest[b]
        if step < 4:
            first = pl.multiple_of((1 - bit_of(spot, step)) * rows, 32)
            away = totals[b][pl.ds(first, rows)] + source[pl.ds(base + first, rows)].astype(F32)
            packet[b * rows : (b + 1) * rows] = away.astype(BF16)
        else:
            whole = totals[b][...] + source[base : base + rows].astype(F32)
            for target, mine in ((refs[2], True), (refs[3], False)):

                @pl.when((spot[0] == b) == mine)
                def _():
                    target[...] = whole

    if step == 1:
        sums0, sums1, got = extra_in
        own = pick(spot[0] == 0, sums0[...], sums1[...])
        other = got[...]
        low = pick(spot[0] == 0, own[SCALE:], other[SCALE:])
        high = pick(spot[0] == 0, other[SCALE:], own[SCALE:])
        packet[head : head + 16] = jnp.concatenate([low, high], axis=0).astype(BF16)
        width = own.shape[1]
        lane = lax.broadcasted_iota(jnp.int32, (1, width), 1)
        mine_lane = (lane >> 4) == gather_slot(spot)
        which = ((lane >> 3) & 1) * 4 + (lane & 3)
        code = jnp.zeros((1, width), jnp.int32)
        for c in range(8):
            code = jnp.where(mine_lane & (which == c), speaker[c], code)
        smalls_out[...] = own[:SCALE] + other[:SCALE]
        smalls_out[13:14] = (code >> 6).astype(F32)
        smalls_out[14:15] = (code & 63).astype(F32)
        tail = head + 16
    else:
        after, before, smalls_in = extra_in
        size = 16 << (step - 2)
        old_head = (16 >> step) * 2 * share
        bit = bit_of(spot, GATHER[step - 2])
        for source, side in ((before, bit), (after, 1 - bit)):
            packet[pl.ds(pl.multiple_of(head + side * size, 16), size)] = source[
                old_head : old_head + size
            ]
        smalls_out[...] = smalls_in[...] + after[old_head + size : old_head + size + 16].astype(F32)
        tail = head + 2 * size
    packet[tail : tail + 16] = smalls_out[...].astype(BF16)


def finish_body(
    sec, place, before, after, smalls_in, mine, got, scale, shift, up, down, taps, conv, upb, downb, gain,
    rows_of,
):
    spot = (sec[0], place[0])
    size = rows_of.shape[0] // 2
    bit = bit_of(spot, GATHER[3])
    for source, side in ((before, bit), (after, 1 - bit)):
        rows_of[pl.ds(pl.multiple_of(side * size, 16), size)] = source[:size]
    first = spot[0] == 0
    one, two = mine[...], got[...]
    up_rows = up.shape[0]
    ups = pick(first, one, two)
    for j in range(3):
        up[:, j * TILE : (j + 1) * TILE] = ups[j * up_rows : (j + 1) * up_rows]
    down[...] = pick(first, two, one)
    total = smalls_in[...] + after[size:].astype(F32)
    owned = scale.shape[0]
    count = 2 * size
    who = total[13:14, :count] * 64.0 + total[14:15, :count]
    wanted = lax.broadcasted_iota(jnp.int32, (owned, count), 0) + spot[1] * owned
    hit = who == wanted.astype(F32)
    kind = (lax.broadcasted_iota(jnp.int32, (owned, count), 1) >> 2) & 1
    for k, out in enumerate((scale, shift)):
        out[...] = dot(jnp.where(hit & (kind == k), 1.0, 0.0).astype(BF16), rows_of[...], NN)
    width = total.shape[1]
    lanes = width // BLOCKS
    turn = lax.rem(BLOCKS - spot[1], BLOCKS)
    cut = pltpu.roll(total, turn * lanes, 1)[:, :lanes]
    for k in range(7):
        taps[k] = cut[k : k + 1]
    conv[...] = cut[CONV : CONV + 1]
    downb[...] = cut[DOWNB : DOWNB + 1]
    gain[...] = cut[GAIN : GAIN + 1]
    line = jnp.concatenate([total[UPB + k : UPB + k + 1] for k in range(3)], axis=1)
    upb[...] = pltpu.roll(line, turn * 3 * lanes, 1)[:, : 3 * lanes]


def struct(shape, dtype):
    return jax.ShapeDtypeStruct(shape, dtype)


def params(limit=None):
    return pltpu.CompilerParams(vmem_limit_bytes=limit * 1024 * 1024 if limit else ALL_VMEM)


def cost(flops, moved):
    return pl.CostEstimate(flops=int(flops), bytes_accessed=int(moved), transcendentals=0)


def local(
    tokens, out_cotangent, speaker, valid, conv_weight, conv_bias, scale_table, shift_table,
    up_weight, up_bias, down_weight, down_bias, layer_scale,
):
    section = lax.axis_index("section").astype(jnp.int32)
    place = lax.axis_index("dp").astype(jnp.int32)
    devices = lax.axis_size("dp")
    first_section = section == 0
    clips, frames, width = tokens.shape
    hidden = up_weight.shape[2]
    table_rows = scale_table.shape[1]
    half = clips // 2
    rows = half * frames
    sec = section[None]
    swap = [(0, 1), (1, 0)]

    own_small, other_small = pl.pallas_call(
        prep_body,
        out_shape=[struct((SMALL, width), F32)] * 2,
        in_specs=[SMEM, SMEM] + [VMEM] * 5 + [ANY] * 2,
        out_specs=[VMEM] * 2,
        scratch_shapes=[pltpu.SemaphoreType.DMA((2, 2, half))],
        compiler_params=params(),
        name="prep",
    )(
        sec, speaker, conv_weight.transpose(1, 0, 2), conv_bias, up_bias, down_bias, layer_scale,
        scale_table, shift_table,
    )
    got_small = lax.ppermute(other_small, "section", swap)
    up_own, down_own = up_weight[0], down_weight[0]
    up_got = lax.ppermute(up_own, "section", swap)
    down_got = lax.ppermute(down_own, "section", swap)
    clip_block = (1, frames, width)
    whole_small = pl.BlockSpec((SMALL, width), lambda c, sec: (0, 0))
    half_struct = struct((half, frames, width), BF16)
    whole_struct = struct((clips, frames, width), BF16)
    small_struct = struct((SMALL, width), F32)
    flat_struct = struct((rows, width), BF16)
    tiles = hidden // TILE
    tiled = (tiles, rows, TILE)
    share = hidden // BLOCKS
    gradient = (BLOCKS, share, width)
    gradient_struct = struct(gradient, BF16)
    product = 2 * rows * width * hidden

    (
        sums0, sums1, gin1, normed0, inv0, out_own, out_send, gpre0, keep1, send1, keep0, send0, small0,
    ) = pl.pallas_call(
        main_body,
        out_shape=[
            small_struct, small_struct, half_struct, flat_struct, struct((rows, 128), F32),
            whole_struct, half_struct, struct(tiled, BF16), gradient_struct, gradient_struct,
            gradient_struct, gradient_struct, small_struct,
        ],
        in_specs=[SMEM, SMEM, VMEM, VMEM, HBM, HBM, HBM, ANY, HBM, ANY],
        out_specs=[VMEM, VMEM] + [HBM] * 10 + [VMEM],
        scratch_shapes=[
            pltpu.VMEM((width, hidden), BF16),
            pltpu.VMEM((hidden, width), BF16),
            pltpu.VMEM((width, hidden), BF16),
            pltpu.VMEM((hidden, width), BF16),
            pltpu.VMEM(tiled, BF16),
            pltpu.VMEM(tiled, BF16),
            pltpu.VMEM(tiled, BF16),
            pltpu.VMEM(tiled, BF16),
            pltpu.VMEM((rows, width), F32),
            pltpu.VMEM((rows, width), BF16),
            pltpu.VMEM((rows, width), BF16),
            pltpu.VMEM((rows, 128), F32),
            pltpu.VMEM((rows, width), BF16),
            pltpu.VMEM((rows, width), F32),
            pltpu.VMEM((rows, width), BF16),
            pltpu.VMEM((half, frames, width), BF16),
            pltpu.VMEM((half, frames, width), BF16),
            pltpu.VMEM((half, frames, width), BF16),
            pltpu.VMEM((half, frames, width), BF16),
            pltpu.VMEM((SMALL, width), F32),
            pltpu.VMEM((SMALL, width), F32),
            pltpu.VMEM((len(OFFSETS) * frames, frames), BF16),
            pltpu.VMEM(gradient, BF16),
            pltpu.VMEM(gradient, BF16),
            pltpu.VMEM(gradient, BF16),
            pltpu.VMEM(gradient, BF16),
            pltpu.SemaphoreType.DMA((9, 2)),
            pltpu.SemaphoreType.DMA((half,)),
            pltpu.SemaphoreType.DMA((3, 8)),
        ],
        compiler_params=params(),
        cost_estimate=cost(11 * product, 24 << 20),
        name="main",
    )(
        sec, valid, own_small, got_small, tokens, out_cotangent, up_own, up_got, down_own, down_got
    )
    got1 = lax.ppermute(send1, "section", swap)
    got0 = lax.ppermute(send0, "section", swap)
    got_out = lax.ppermute(out_send, "section", swap)

    def last(first, count, sums, *others):
        def at(c):
            return first + c

        return pl.pallas_call(
            functools.partial(last_body, first),
            grid_spec=pltpu.PrefetchScalarGridSpec(
                num_scalar_prefetch=1,
                grid=(count,),
                in_specs=[
                    pl.BlockSpec((tiles, frames, TILE), lambda c, sec: (0, at(c), 0)),
                    HBM,
                    ANY,
                    pl.BlockSpec((frames, width), lambda c, sec: (at(c), 0)),
                    pl.BlockSpec((frames, 128), lambda c, sec: (at(c), 0)),
                    whole_small,
                    pl.BlockSpec(clip_block, lambda c, sec: (at(c), 0, 0)),
                    pl.BlockSpec(clip_block, lambda c, sec: (sec[0] * half + at(c), 0, 0)),
                    whole_small,
                ]
                + [ANY] * len(others),
                out_specs=[
                    pl.BlockSpec(clip_block, lambda c, sec: (sec[0] * half + at(c), 0, 0)),
                    pl.BlockSpec(clip_block, lambda c, sec: (at(c), 0, 0)),
                    whole_small,
                ],
                scratch_shapes=[
                    pltpu.VMEM((width, hidden), BF16),
                    pltpu.VMEM((len(OFFSETS) * frames, frames), BF16),
                    pltpu.SemaphoreType.DMA,
                ],
            ),
            out_shape=[whole_struct, half_struct, small_struct],
            input_output_aliases={10 + i: i for i in range(len(others))},
            compiler_params=params(),
            cost_estimate=cost(2 * count * product, 12 << 20),
        )(sec, gpre0, up_own, up_got, normed0, inv0, small0, gin1, tokens, sums, *others)

    gin_own, gin_send, sums0 = last(0, 1, sums0)
    gin_own, gin_send, sums0 = last(1, half - 1, sums0, gin_own, gin_send)
    got_gin = lax.ppermute(gin_send, "section", swap)
    got_sums = lax.ppermute(pick(first_section, sums1, sums0), "section", swap)

    def joined(whole, got):
        return lax.dynamic_update_slice(whole, got, ((1 - section) * half, 0, 0))[None]

    block_outputs = joined(out_own, got_out)
    input_grads = joined(gin_own, got_gin)
    pairs = [[keep0, got0], [keep1, got1]]
    if devices == BLOCKS:
        outs = halved(sec, place[None], speaker, pairs, sums0, sums1, got_sums, table_rows)
    else:
        outs = scattered(section, place, devices, speaker, pairs, sums0, sums1, got_sums, table_rows)
    return (block_outputs, input_grads) + outs


def exchanged(packet, step):
    devices = lax.axis_size("dp")
    moves = [
        (s * devices + i, s * devices + (i ^ (1 << ORDERS[s][step])))
        for s in range(2)
        for i in range(devices)
    ]
    return lax.ppermute(packet, PAIR, moves)


def halved(sec, place, speaker, pairs, sums0, sums1, got_sums, table_rows):
    _, share, width = pairs[0][0].shape
    pairs = [[piece.reshape(-1, width) for piece in pair] for pair in pairs]
    spot = (sec[0], place[0])
    rows = 8 * share

    def split(b):
        return pl.pallas_call(
            functools.partial(split_body, share),
            out_shape=struct((rows, width), BF16),
            in_specs=[SMEM, SMEM, HBM, ANY],
            out_specs=VMEM,
            scratch_shapes=[
                pltpu.VMEM((rows, width), BF16),
                pltpu.VMEM((rows, width), BF16),
                pltpu.SemaphoreType.DMA((4, 2)),
            ],
            compiler_params=params(6),
            cost_estimate=cost(0, 4 << 20),
        )(sec, place, *pairs[b])

    def part(array, first, count):
        return lax.dynamic_slice_in_dim(array, first, count, 0).astype(F32)

    latest, totals = [None, None], [None, None]
    for b in (1, 0):
        packet = split(b)
        latest[b] = exchanged(packet, 0)
    for b in (1, 0):
        totals[b] = sum(part(piece, bit_of(spot, 0) * rows, rows) for piece in pairs[b])

    def pack(step, extra_in):
        count = 8 >> step
        length = 2 * count * share + (8 << step) + 16
        outs = [struct((length, width), BF16), struct((SCALE, width), F32)]
        if step == 4:
            outs += [struct((share, width), F32)] * 2
        operands = list(totals) + (latest if step == 1 else []) + extra_in
        return pl.pallas_call(
            functools.partial(pack_body, step, share),
            out_shape=outs,
            in_specs=[SMEM, SMEM, SMEM] + [VMEM] * len(operands),
            out_specs=[VMEM] * len(outs),
            compiler_params=params(8),
            cost_estimate=cost(0, 2 << 20),
        )(sec, place, speaker, *operands)

    packet, smalls = pack(1, [sums0, sums1, got_sums])
    for step in range(1, 4):
        got = exchanged(packet, step)
        rows = (8 >> step) * share
        first = bit_of(spot, step) * rows
        bases = (0, 0) if step == 1 else (0, 2 * rows)
        totals = [
            part(totals[b], first, rows) + part(latest[b], bases[b] + first, rows) for b in range(2)
        ]
        latest = [got, got]
        packet, smalls, *shares = pack(step + 1, [got, packet, smalls])
    mine, away = shares
    got = exchanged(packet, 0)
    got_share = lax.ppermute(away, "section", [(0, 1), (1, 0)])
    owned = table_rows // BLOCKS
    up_rows = width // BLOCKS
    lanes = width // BLOCKS
    one = struct((1, lanes), F32)
    scale, shift, up, down, taps, conv, upb, downb, gain = pl.pallas_call(
        finish_body,
        out_shape=[
            struct((owned, width), F32),
            struct((owned, width), F32),
            struct((up_rows, 3 * TILE), F32),
            struct((share, width), F32),
            struct((7, 1, lanes), F32),
            one,
            struct((1, 3 * lanes), F32),
            one,
            one,
        ],
        in_specs=[SMEM, SMEM] + [VMEM] * 5,
        out_specs=[VMEM] * 9,
        scratch_shapes=[pltpu.VMEM((16 * BLOCKS, width), BF16)],
        compiler_params=params(8),
        name="finish",
    )(sec, place, packet, got, smalls, mine, got_share)
    return (
        taps.transpose(1, 0, 2), conv, scale[None], shift[None], up[None], upb, down[None], downb, gain
    )


def scattered(section, place, devices, speaker, pairs, sums0, sums1, got_sums, table_rows):
    first_section = section == 0
    own_sums = pick(first_section, sums0, sums1)
    smalls = lax.psum(own_sums[:SCALE] + got_sums[:SCALE], "dp")
    clip_rows = jnp.stack([own_sums[SCALE:], got_sums[SCALE:]])
    clip_rows = pick(first_section, clip_rows, clip_rows[::-1]).astype(BF16)
    clips = speaker.shape[0]
    width = clip_rows.shape[-1]
    clip_rows = clip_rows.reshape(2, 2, clips // 2, width).transpose(1, 0, 2, 3).reshape(2, clips, width)
    gathered = lax.all_gather(clip_rows, "dp", axis=1, tiled=True)
    who = lax.all_gather(speaker, "dp", tiled=True)
    owned = table_rows // devices
    wanted = place * owned + jnp.arange(owned, dtype=jnp.int32)
    chosen = (who[None, :] == wanted[:, None]).astype(BF16)
    tables = [jnp.dot(chosen, gathered[k], preferred_element_type=F32) for k in range(2)]
    natural = []
    for order in ORDERS:
        natural.append(
            jnp.stack(
                [
                    jnp.stack([pair[0][position(i, order)].astype(F32) + pair[1][position(i, order)].astype(F32) for i in range(BLOCKS)])
                    for pair in pairs
                ]
            )
        )
    blocks, _, rows, width = natural[0].shape
    tiles = rows * BLOCKS // TILE
    up = natural[0].reshape(blocks, BLOCKS, tiles, rows // tiles, TILE).transpose(0, 1, 3, 2, 4)
    flat = pick(
        first_section, up.reshape(blocks, devices, -1), natural[1].reshape(blocks, devices, -1)
    )
    share = lax.psum_scatter(flat, "dp", scatter_dimension=1, tiled=True)[:, 0]
    own_share = lax.dynamic_index_in_dim(share, section, 0, keepdims=False)
    got_share = lax.ppermute(
        lax.dynamic_index_in_dim(share, 1 - section, 0, keepdims=False), "section", [(0, 1), (1, 0)]
    )
    up_share = pick(first_section, own_share, got_share).reshape(width // devices, -1)
    down_share = pick(first_section, got_share, own_share).reshape(-1, width)
    lanes = width // devices
    own_lanes = lax.dynamic_slice_in_dim(smalls, place * lanes, lanes, 1)
    upb = lax.dynamic_slice_in_dim(smalls[UPB : UPB + 3].reshape(-1), place * 3 * lanes, 3 * lanes, 0)
    return (
        own_lanes[TAPS : TAPS + 7][None],
        own_lanes[CONV : CONV + 1],
        tables[0][None],
        tables[1][None],
        up_share[None],
        upb[None],
        down_share[None],
        own_lanes[DOWNB : DOWNB + 1],
        own_lanes[GAIN : GAIN + 1],
    )


def solution(mesh):
    placed = (
        P("dp", None, None),
        P("dp", None, None),
        P("dp"),
        P("dp"),
        P("section", None, None),
        P("section", None),
        P("section", None, None),
        P("section", None, None),
        P("section", None, None),
        P("section", None),
        P("section", None, None),
        P("section", None),
        P("section", None),
    )

    return jax.shard_map(
        local,
        mesh=mesh,
        in_specs=placed,
        out_specs=(
            P("section", "dp", None, None),
            P("section", "dp", None, None),
            P("section", None, "dp"),
            P("section", "dp"),
            P("section", "dp", None),
            P("section", "dp", None),
            P("section", "dp", None),
            P("section", "dp"),
            P("section", "dp", None),
            P("section", "dp"),
            P("section", "dp"),
        ),
        check_vma=False,
    )
```

```python
import functools

import jax
import jax.numpy as jnp
from jax import lax
from jax.experimental import pallas as pl
from jax.experimental.pallas import tpu as pltpu
from jax.sharding import PartitionSpec as P


F32 = jnp.float32
BF16 = jnp.bfloat16
PAIR = ("section", "dp")
TILE = 512
ALL_VMEM = 67043328
HALF_ROOT = 0.7071067811865476
DENSITY = 0.3989422804014327
BLOCKS = 16
ORDERS = ((0, 1, 2, 3), (2, 0, 1, 3))
ANY = pl.BlockSpec(memory_space=pl.ANY)
HBM = pl.BlockSpec(memory_space=pltpu.HBM)
VMEM = pl.BlockSpec(memory_space=pltpu.VMEM)
SMEM = pl.BlockSpec(memory_space=pltpu.SMEM)

TAPS, CONV, UPB, DOWNB, GAIN, SCALE, SHIFT, SMALL = 0, 7, 8, 11, 12, 16, 20, 24


def position(block, order):
    place = 0
    for bit in order:
        place = 2 * place + ((block >> bit) & 1)
    return place


def dot(a, b, dims):
    return lax.dot_general(a, b, (dims, ((), ())), preferred_element_type=F32)


NN = ((1,), (0,))
NT = ((1,), (1,))
TN = ((0,), (0,))


OFFSETS = (-3, -2, -1, 1, 2, 3)


def set_shifts(shifts):
    frames = shifts.shape[1]
    row = lax.broadcasted_iota(jnp.int32, (frames, frames), 0)
    col = lax.broadcasted_iota(jnp.int32, (frames, frames), 1)
    for n, offset in enumerate(OFFSETS):
        shifts[n * frames : (n + 1) * frames] = jnp.where(col == row + offset, 1.0, 0.0).astype(BF16)


def shifted(shifts, x, offset):
    frames = x.shape[0]
    n = OFFSETS.index(offset)
    return dot(shifts[n * frames : (n + 1) * frames], x, NN)


def wide(x, width):
    return jnp.concatenate([x] * (width // 128), axis=1)


def rowsum(x):
    return jnp.sum(x, axis=0, keepdims=True)


def normalize(x, small, clip, shifts):
    conv = small[CONV : CONV + 1] + x.astype(F32) * small[3:4]
    for offset in OFFSETS:
        conv = conv + shifted(shifts, x, offset) * small[offset + 3 : offset + 4]
    centred = conv - jnp.mean(conv, axis=-1, keepdims=True)
    inv = lax.rsqrt(jnp.mean(centred * centred, axis=-1, keepdims=True) + 1e-06)
    normed = centred * inv
    scale = small[pl.ds(SCALE + clip, 1)]
    shift = small[pl.ds(SHIFT + clip, 1)]
    adapted = (normed * scale + shift).astype(BF16)
    return adapted, normed.astype(BF16), jnp.broadcast_to(inv, (x.shape[0], 128))


def prep_body(sec, speaker, taps, conv, upb, downb, gain, scale_hbm, shift_hbm, own, other, sems):
    width = own.shape[1]
    half = SMALL - SHIFT
    copies = []
    for side, out in enumerate((own, other)):
        first = (sec[0] if side == 0 else 1 - sec[0]) * half
        for clip in range(half):
            row = speaker[first + clip]
            for kind, table in enumerate((scale_hbm, shift_hbm)):
                copies.append(
                    pltpu.make_async_copy(
                        table.at[0, pl.ds(row, 1)],
                        out.at[pl.ds((SCALE, SHIFT)[kind] + clip, 1)],
                        sems.at[side, kind, clip],
                    )
                )
    for copy in copies:
        copy.start()
    for out in (own, other):
        for k in range(7):
            out[TAPS + k : TAPS + k + 1] = taps[k]
        out[CONV : CONV + 1] = conv[...]
        for k in range(DOWNB - UPB):
            out[UPB + k : UPB + k + 1] = upb[:, k * width : (k + 1) * width]
        out[DOWNB : DOWNB + 1] = downb[...]
        out[GAIN : GAIN + 1] = gain[...]
        out[GAIN + 1 : SCALE] = jnp.zeros((SCALE - GAIN - 1, width), F32)
    for copy in copies:
        copy.wait()


def forward_tiles(adapted, up, down, small, act, slope, acc):
    steps = [(j, r) for j in range(3) for r in range(acc.shape[0] // 256)]

    def hidden(j, r):
        part = dot(adapted[r * 256 : (r + 1) * 256], up[:, j * TILE : (j + 1) * TILE], NN)
        return part + small[UPB + j : UPB + j + 1]

    ahead = hidden(*steps[0])
    for n, (j, r) in enumerate(steps):
        rows = slice(r * 256, (r + 1) * 256)
        pre = ahead
        if n + 1 < len(steps):
            ahead = hidden(*steps[n + 1])
        phi = 0.5 * lax.erf(pre * HALF_ROOT) + 0.5
        low = (pre * phi).astype(BF16)
        act[j, rows] = low
        slope[j, rows] = (phi + pre * (DENSITY * jnp.exp(-0.5 * pre * pre))).astype(BF16)
        part = dot(low, down[j * TILE : (j + 1) * TILE], NN)
        acc[rows] = part if j == 0 else acc[rows] + part


def activation_tile(j, gb, down, slope, sums):
    total = jnp.zeros((1, TILE), F32)
    for r in range(gb.shape[0] // 256):
        rows = slice(r * 256, (r + 1) * 256)
        gact = dot(gb[rows], down[j * TILE : (j + 1) * TILE], NT)
        gpre = (gact * slope[j, rows].astype(F32)).astype(BF16)
        slope[j, rows] = gpre
        total = total + rowsum(gpre.astype(F32))
    sums[UPB + j : UPB + j + 1] = total


def down_pieces(j):
    share = 3 * TILE // BLOCKS
    at, pieces = j * TILE, []
    while at < (j + 1) * TILE:
        stop = min((at // share + 1) * share, (j + 1) * TILE)
        pieces.append((position(at // share, ORDERS[1]), at % share, stop - at, at - j * TILE))
        at = stop
    return pieces


def weight_tile(j, gb, adapted, act, gpre, upd, dnd):
    gup = dot(adapted[...], gpre, TN).astype(BF16)
    share = TILE // BLOCKS
    for i in range(BLOCKS):
        upd[position(i, ORDERS[0]), j * share : (j + 1) * share] = gup[i * share : (i + 1) * share]
    gdn = dot(act, gb[...], TN).astype(BF16)
    for block, first, rows, at in down_pieces(j):
        dnd[block, first : first + rows] = gdn[at : at + rows]


def norm_backward(gad, normed, inv, small, clip, grad_out, v, shifts):
    n = normed.astype(F32)
    width = n.shape[1]
    scale = small[pl.ds(SCALE + clip, 1)]
    g_shift = rowsum(gad)
    g_scale = rowsum(gad * n)
    gn = gad * scale
    m1 = jnp.mean(gn, axis=-1, keepdims=True)
    m2 = jnp.mean(gn * n, axis=-1, keepdims=True)
    gc = (gn - m1 - n * m2) * wide(inv, width)
    low = gc.astype(BF16)
    total = grad_out + gc * small[3:4]
    v = v.astype(F32)
    g_taps = []
    for k in range(7):
        if k == 3:
            g_taps.append(rowsum(gc * v))
            continue
        moved = shifted(shifts, low, 3 - k)
        total = total + moved * small[k : k + 1]
        g_taps.append(rowsum(moved * v))
    return total.astype(BF16), jnp.concatenate(g_taps + [rowsum(gc)], axis=0), g_scale, g_shift


def place_weights(sec, block, up_own, up_got, down_own, down_got, up, down, sems, start):
    def go(up_from, down_from):
        for source, target, sem in ((up_from, up, sems.at[0]), (down_from, down, sems.at[1])):
            copy = pltpu.make_async_copy(source, target, sem)
            copy.start() if start else copy.wait()

    if not start:
        go(up_own, down_own)
        return

    @pl.when(sec[0] == block)
    def _():
        go(up_own, down_own)

    @pl.when(sec[0] != block)
    def _():
        go(up_got, down_got)


def route_tile(sec, j, upd, dnd, keep, send, sems, start):
    share = TILE // BLOCKS

    def go(up_to, down_to):
        part = pl.ds(j * share, share)
        copies = [pltpu.make_async_copy(upd.at[:, part], up_to.at[:, part], sems.at[j, 0])]
        for n, (block, first, rows, _) in enumerate(down_pieces(j)):
            part = pl.ds(first, rows)
            copies.append(
                pltpu.make_async_copy(dnd.at[block, part], down_to.at[block, part], sems.at[j, 1 + n])
            )
        for copy in copies:
            copy.start() if start else copy.wait()

    if not start:
        go(keep, send)
        return

    @pl.when(sec[0] == 0)
    def _():
        go(keep, send)

    @pl.when(sec[0] != 0)
    def _():
        go(send, keep)


def route(sec, upd, dnd, keep, send, sems, start):
    def go(kept, sent):
        for source, target, sem in ((kept, keep, sems.at[0]), (sent, send, sems.at[1])):
            copy = pltpu.make_async_copy(source, target, sem)
            copy.start() if start else copy.wait()

    if not start:
        go(upd, dnd)
        return

    @pl.when(sec[0] == 0)
    def _():
        go(upd, dnd)

    @pl.when(sec[0] != 0)
    def _():
        go(dnd, upd)


def main_body(
    sec, valid, own_small, got_small, tokens, cot, up_own, up_got, down_own, down_got,
    sums0, sums1, gin1, normed_hbm, inv_hbm, out_own, out_send, gpre_hbm, keep1, send1, keep0, send0,
    small0_out,
    up0, down0, up1, down1, act0, slope0, act1, slope1, acc, adapted0, normed, inv, adapted1, branch0,
    gb, v, grad, out0, out1, small0, small1, shifts, upd, dnd, upd0, dnd0, sems, pieces, parts,
):
    clips = acc.shape[0] // 256
    mine = pl.ds(sec[0] * clips, clips)
    loads = (
        pltpu.make_async_copy(tokens.at[mine], v, sems.at[6, 0]),
        pltpu.make_async_copy(cot.at[mine], grad, sems.at[6, 1]),
    )
    loads[0].start()
    weights = (up_own, up_got, down_own, down_got)
    place_weights(sec, 0, *weights, up0, down0, sems.at[0], True)
    place_weights(sec, 1, *weights, up1, down1, sems.at[1], True)
    loads[1].start()
    first = sec[0] == 0
    small0[...] = pick(first, own_small[...], got_small[...])
    small1[...] = pick(first, got_small[...], own_small[...])
    small0_out[...] = small0[...]
    sums0[...] = jnp.zeros_like(sums0)
    sums1[...] = jnp.zeros_like(sums1)
    set_shifts(shifts)
    loads[0].wait()

    def begin(r):
        rows = pl.ds(pl.multiple_of(r * 256, 256), 256)
        adapted0[rows], normed[rows], inv[rows] = normalize(v[r], small0, r, shifts)

    pl.loop(0, clips, unroll=True)(begin)
    saves = [
        pltpu.make_async_copy(source, target, sems.at[7 + n // 2, n % 2])
        for n, (source, target) in enumerate(
            ((normed, normed_hbm), (inv, inv_hbm))
        )
    ]
    for copy in saves:
        copy.start()
    place_weights(sec, 0, *weights, up0, down0, sems.at[0], False)
    forward_tiles(adapted0, up0, down0, small0, act0, slope0, acc)
    for copy in saves:
        copy.wait()

    def between(r):
        rows = pl.ds(pl.multiple_of(r * 256, 256), 256)
        branch = acc[rows] + small0[DOWNB : DOWNB + 1]
        branch0[rows] = branch
        result = (v[r].astype(F32) + small0[GAIN : GAIN + 1] * branch).astype(BF16)
        out0[r] = result
        adapted1[rows], normed[rows], inv[rows] = normalize(result, small1, r, shifts)

    pl.loop(0, clips, unroll=True)(between)
    place_weights(sec, 1, *weights, up1, down1, sems.at[1], False)
    forward_tiles(adapted1, up1, down1, small1, act1, slope1, acc)
    loads[1].wait()

    def top(r):
        rows = pl.ds(pl.multiple_of(r * 256, 256), 256)
        branch = acc[rows] + small1[DOWNB : DOWNB + 1]
        gain = small1[GAIN : GAIN + 1]
        out1[r] = (out0[r].astype(F32) + gain * branch).astype(BF16)
        above = grad[r].astype(F32) * valid[sec[0] * clips + r].astype(F32)
        low = (above * gain).astype(BF16)
        gb[rows] = low
        sums1[GAIN : GAIN + 1] += rowsum(above * branch)
        sums1[DOWNB : DOWNB + 1] += rowsum(low.astype(F32))

    pl.loop(0, clips)(top)
    half_own = out_own.at[mine]
    route(sec, out0, out1, half_own, out_send, sems.at[4], True)
    for j in range(3):
        activation_tile(j, gb, down1, slope1, sums1)
        for r in range(clips):
            rows = slice(r * 256, (r + 1) * 256)
            part = dot(slope1[j, rows], up1[:, j * TILE : (j + 1) * TILE], NT)
            acc[rows] = part if j == 0 else acc[rows] + part
        weight_tile(j, gb, adapted1, act1[j], slope1[j], upd, dnd)
    route(sec, upd, dnd, keep1, send1, sems.at[3], True)

    def move(r):
        return pltpu.make_async_copy(grad.at[r], gin1.at[r], pieces.at[r])

    def under(r):
        rows = pl.ds(pl.multiple_of(r * 256, 256), 256)
        above = grad[r].astype(F32) * valid[sec[0] * clips + r].astype(F32)
        gin, smalls, g_scale, g_shift = norm_backward(
            acc[rows], normed[rows], inv[rows], small1, r, above, out0[r], shifts
        )
        grad[r] = gin
        sums1[TAPS : TAPS + 8] += smalls
        sums1[pl.ds(SCALE + r, 1)] = g_scale
        sums1[pl.ds(SHIFT + r, 1)] = g_shift
        grad0 = gin.astype(F32)
        low = (grad0 * small0[GAIN : GAIN + 1]).astype(BF16)
        gb[rows] = low
        move(r).start()
        sums0[GAIN : GAIN + 1] += rowsum(grad0 * branch0[rows])
        sums0[DOWNB : DOWNB + 1] += rowsum(low.astype(F32))

    pl.loop(0, clips)(under)
    tiles = []
    for j in range(3):
        activation_tile(j, gb, down0, slope0, sums0)
        tiles.append(pltpu.make_async_copy(slope0.at[j], gpre_hbm.at[j], sems.at[5 + j // 2 * 3, j % 2]))
        tiles[-1].start()
        weight_tile(j, gb, adapted0, act0[j], slope0[j], upd0, dnd0)
        route_tile(sec, j, upd0, dnd0, keep0, send0, parts, True)
    route(sec, out0, out1, half_own, out_send, sems.at[4], False)
    route(sec, upd, dnd, keep1, send1, sems.at[3], False)
    for copy in tiles + [move(r) for r in range(clips)]:
        copy.wait()
    for j in range(3):
        route_tile(sec, j, upd0, dnd0, keep0, send0, parts, False)


def last_body(
    first, sec, gpre, up_own, up_got, normed, inv, small, grad_out, tokens, sums_in, *rest
):
    gin, away, sums, up, shifts, sem = rest[-6:]
    step = pl.program_id(0)
    clip = first + step

    @pl.when(step == 0)
    def _():
        sums[...] = sums_in[...]

        @pl.when(sec[0] == 0)
        def _():
            pltpu.make_async_copy(up_own, up, sem).start()

        @pl.when(sec[0] != 0)
        def _():
            pltpu.make_async_copy(up_got, up, sem).start()

        set_shifts(shifts)
        pltpu.make_async_copy(up_own, up, sem).wait()

    gad = dot(gpre[0], up[:, :TILE], NT)
    for j in range(1, 3):
        gad = gad + dot(gpre[j], up[:, j * TILE : (j + 1) * TILE], NT)
    above = grad_out[0]
    out, smalls, g_scale, g_shift = norm_backward(
        gad, normed[...], inv[...], small, clip, above.astype(F32), tokens[0], shifts
    )
    gin[0] = jnp.where(sec[0] == 0, out, above)
    away[0] = jnp.where(sec[0] == 0, above, out)
    sums[TAPS : TAPS + 8] += smalls
    sums[pl.ds(SCALE + clip, 1)] = g_scale
    sums[pl.ds(SHIFT + clip, 1)] = g_shift


def pick(first, a, b):
    return jnp.where(first, a, b)


def bit_of(spot, step):
    low, high = ORDERS[0][step], ORDERS[1][step]
    return (spot[1] >> (low if low == high else pick(spot[0] == 0, low, high))) & 1


GATHER = (3, 2, 0, 1)


def gather_bit(spot, hop):
    return (spot[1] >> GATHER[hop]) & 1


def gather_slot(spot):
    slot = 0
    for hop in range(len(GATHER)):
        slot = slot + gather_bit(spot, hop) * (1 << hop)
    return slot


def fetch(copies, source, first, rows, target, sem):
    copies.append(pltpu.make_async_copy(source.at[pl.ds(first, rows)], target, sem))
    copies[-1].start()


def split_body(share, sec, place, keep, got, packet, kept, came, sems):
    rows = 8 * share
    first = pl.multiple_of((1 - bit_of((sec[0], place[0]), 0)) * rows, rows)
    pieces = 4
    size = rows // pieces
    copies = []
    for n in range(pieces):
        for m, (source, target) in enumerate(((keep, kept), (got, came))):
            fetch(
                copies, source, first + n * size, size, target.at[pl.ds(n * size, size)], sems.at[n, m]
            )
    for n in range(pieces):
        copies[2 * n].wait()
        copies[2 * n + 1].wait()
        part = slice(n * size, (n + 1) * size)
        packet[part] = (kept[part].astype(F32) + came[part].astype(F32)).astype(BF16)


def second_body(share, sec, place, *refs):
    spot = (sec[0], place[0])
    sources, (packet, buffer, sems) = refs[:6], refs[6:]
    rows = 4 * share
    away = (1 - bit_of(spot, 1)) * rows
    copies = []
    for n, source in enumerate(sources):
        first = away if n % 3 == 2 else away + bit_of(spot, 0) * 2 * rows
        fetch(copies, source, pl.multiple_of(first, 32), rows, buffer.at[n], sems.at[n])
    for b in range(2):
        total = 0.0
        for n in range(3 * b, 3 * b + 3):
            copies[n].wait()
            total = total + buffer[n].astype(F32)
        packet[b * rows : (b + 1) * rows] = total.astype(BF16)


def pack_body(step, share, sec, place, total0, total1, came, packet):
    rows = (8 >> step) * share
    first = pl.multiple_of((1 - bit_of((sec[0], place[0]), step)) * rows, 32)
    for b, total in enumerate((total0, total1)):
        latest = came[pl.ds(b * 2 * rows + first, rows)]
        packet[b * rows : (b + 1) * rows] = (total[pl.ds(first, rows)] + latest.astype(F32)).astype(BF16)


def share_body(share, sec, total0, total1, came, mine, away):
    for b, total in enumerate((total0, total1)):
        whole = total[...] + came[b * share : (b + 1) * share].astype(F32)
        for target, stays in ((mine, True), (away, False)):

            @pl.when((sec[0] == b) == stays)
            def _():
                target[...] = whole


def begin_rows_body(sec, place, speaker, sums0, sums1, got, packet, smalls):
    spot = (sec[0], place[0])
    first = spot[0] == 0
    own = pick(first, sums0[...], sums1[...])
    other = got[...]
    low = pick(first, own[SCALE:], other[SCALE:])
    high = pick(first, other[SCALE:], own[SCALE:])
    packet[:16] = jnp.concatenate([low, high], axis=0).astype(BF16)
    lane = lax.broadcasted_iota(jnp.int32, (1, own.shape[1]), 1)
    here = (lane >> 4) == gather_slot(spot)
    which = ((lane >> 3) & 1) * 4 + (lane & 3)
    code = jnp.zeros(lane.shape, jnp.int32)
    for c in range(8):
        code = jnp.where(here & (which == c), speaker[c], code)
    smalls[...] = own[:SCALE] + other[:SCALE]
    smalls[13:14] = (code >> 6).astype(F32)
    smalls[14:15] = (code & 63).astype(F32)
    packet[16:32] = smalls[...].astype(BF16)


def more_rows_body(hop, place, before, after, smalls_in, packet, smalls):
    size = 16 << (hop - 1)
    bit = gather_bit((0, place[0]), hop - 1)
    for source, side in ((before, bit), (after, 1 - bit)):
        packet[pl.ds(pl.multiple_of(side * size, 16), size)] = source[:size]
    smalls[...] = smalls_in[...] + after[size:].astype(F32)
    packet[2 * size :] = smalls[...].astype(BF16)


def tables_body(place, before, after, smalls_in, scale, shift, taps, conv, upb, downb, gain, rows_of):
    size = rows_of.shape[0] // 2
    bit = gather_bit((0, place[0]), len(GATHER) - 1)
    for source, side in ((before, bit), (after, 1 - bit)):
        rows_of[pl.ds(pl.multiple_of(side * size, 16), size)] = source[:size]
    total = smalls_in[...] + after[size:].astype(F32)
    owned = scale.shape[0]
    count = 2 * size
    who = total[13:14, :count] * 64.0 + total[14:15, :count]
    wanted = lax.broadcasted_iota(jnp.int32, (owned, count), 0) + place[0] * owned
    hit = who == wanted.astype(F32)
    kind = (lax.broadcasted_iota(jnp.int32, (owned, count), 1) >> 2) & 1
    for k, out in enumerate((scale, shift)):
        out[...] = dot(jnp.where(hit & (kind == k), 1.0, 0.0).astype(BF16), rows_of[...], NN)
    lanes = total.shape[1] // BLOCKS
    turn = lax.rem(BLOCKS - place[0], BLOCKS)
    cut = pltpu.roll(total, turn * lanes, 1)[:, :lanes]
    for k in range(7):
        taps[k] = cut[k : k + 1]
    conv[...] = cut[CONV : CONV + 1]
    downb[...] = cut[DOWNB : DOWNB + 1]
    gain[...] = cut[GAIN : GAIN + 1]
    line = jnp.concatenate([total[UPB + k : UPB + k + 1] for k in range(3)], axis=1)
    upb[...] = pltpu.roll(line, turn * 3 * lanes, 1)[:, : 3 * lanes]


def finish_body(sec, mine, got, up, down):
    first = sec[0] == 0
    rows = up.shape[0]
    ups = pick(first, mine[...], got[...])
    for j in range(3):
        up[:, j * TILE : (j + 1) * TILE] = ups[j * rows : (j + 1) * rows]
    down[...] = pick(first, got[...], mine[...])


def struct(shape, dtype):
    return jax.ShapeDtypeStruct(shape, dtype)


def params(limit=None):
    return pltpu.CompilerParams(vmem_limit_bytes=limit * 1024 * 1024 if limit else ALL_VMEM)


def cost(flops, moved):
    return pl.CostEstimate(flops=int(flops), bytes_accessed=int(moved), transcendentals=0)


def local(
    tokens, out_cotangent, speaker, valid, conv_weight, conv_bias, scale_table, shift_table,
    up_weight, up_bias, down_weight, down_bias, layer_scale,
):
    section = lax.axis_index("section").astype(jnp.int32)
    place = lax.axis_index("dp").astype(jnp.int32)
    devices = lax.axis_size("dp")
    first_section = section == 0
    clips, frames, width = tokens.shape
    hidden = up_weight.shape[2]
    table_rows = scale_table.shape[1]
    half = clips // 2
    rows = half * frames
    sec = section[None]
    swap = [(0, 1), (1, 0)]

    own_small, other_small = pl.pallas_call(
        prep_body,
        out_shape=[struct((SMALL, width), F32)] * 2,
        in_specs=[SMEM, SMEM] + [VMEM] * 5 + [ANY] * 2,
        out_specs=[VMEM] * 2,
        scratch_shapes=[pltpu.SemaphoreType.DMA((2, 2, half))],
        compiler_params=params(),
        name="prep",
    )(
        sec, speaker, conv_weight.transpose(1, 0, 2), conv_bias, up_bias, down_bias, layer_scale,
        scale_table, shift_table,
    )
    got_small = lax.ppermute(other_small, "section", swap)
    up_own, down_own = up_weight[0], down_weight[0]
    up_got = lax.ppermute(up_own, "section", swap)
    down_got = lax.ppermute(down_own, "section", swap)
    clip_block = (1, frames, width)
    whole_small = pl.BlockSpec((SMALL, width), lambda c, sec: (0, 0))
    half_struct = struct((half, frames, width), BF16)
    whole_struct = struct((clips, frames, width), BF16)
    small_struct = struct((SMALL, width), F32)
    flat_struct = struct((rows, width), BF16)
    tiles = hidden // TILE
    tiled = (tiles, rows, TILE)
    share = hidden // BLOCKS
    gradient = (BLOCKS, share, width)
    gradient_struct = struct(gradient, BF16)
    product = 2 * rows * width * hidden

    (
        sums0, sums1, gin1, normed0, inv0, out_own, out_send, gpre0, keep1, send1, keep0, send0, small0,
    ) = pl.pallas_call(
        main_body,
        out_shape=[
            small_struct, small_struct, half_struct, flat_struct, struct((rows, 128), F32),
            whole_struct, half_struct, struct(tiled, BF16), gradient_struct, gradient_struct,
            gradient_struct, gradient_struct, small_struct,
        ],
        in_specs=[SMEM, SMEM, VMEM, VMEM, HBM, HBM, HBM, ANY, HBM, ANY],
        out_specs=[VMEM, VMEM] + [HBM] * 10 + [VMEM],
        scratch_shapes=[
            pltpu.VMEM((width, hidden), BF16),
            pltpu.VMEM((hidden, width), BF16),
            pltpu.VMEM((width, hidden), BF16),
            pltpu.VMEM((hidden, width), BF16),
            pltpu.VMEM(tiled, BF16),
            pltpu.VMEM(tiled, BF16),
            pltpu.VMEM(tiled, BF16),
            pltpu.VMEM(tiled, BF16),
            pltpu.VMEM((rows, width), F32),
            pltpu.VMEM((rows, width), BF16),
            pltpu.VMEM((rows, width), BF16),
            pltpu.VMEM((rows, 128), F32),
            pltpu.VMEM((rows, width), BF16),
            pltpu.VMEM((rows, width), F32),
            pltpu.VMEM((rows, width), BF16),
            pltpu.VMEM((half, frames, width), BF16),
            pltpu.VMEM((half, frames, width), BF16),
            pltpu.VMEM((half, frames, width), BF16),
            pltpu.VMEM((half, frames, width), BF16),
            pltpu.VMEM((SMALL, width), F32),
            pltpu.VMEM((SMALL, width), F32),
            pltpu.VMEM((len(OFFSETS) * frames, frames), BF16),
            pltpu.VMEM(gradient, BF16),
            pltpu.VMEM(gradient, BF16),
            pltpu.VMEM(gradient, BF16),
            pltpu.VMEM(gradient, BF16),
            pltpu.SemaphoreType.DMA((9, 2)),
            pltpu.SemaphoreType.DMA((half,)),
            pltpu.SemaphoreType.DMA((3, 8)),
        ],
        compiler_params=params(),
        cost_estimate=cost(11 * product, 24 << 20),
        name="main",
    )(
        sec, valid, own_small, got_small, tokens, out_cotangent, up_own, up_got, down_own, down_got
    )
    got1 = lax.ppermute(send1, "section", swap)
    got0 = lax.ppermute(send0, "section", swap)
    got_out = lax.ppermute(out_send, "section", swap)

    def last(first, count, sums, *others):
        def at(c):
            return first + c

        return pl.pallas_call(
            functools.partial(last_body, first),
            grid_spec=pltpu.PrefetchScalarGridSpec(
                num_scalar_prefetch=1,
                grid=(count,),
                in_specs=[
                    pl.BlockSpec((tiles, frames, TILE), lambda c, sec: (0, at(c), 0)),
                    HBM,
                    ANY,
                    pl.BlockSpec((frames, width), lambda c, sec: (at(c), 0)),
                    pl.BlockSpec((frames, 128), lambda c, sec: (at(c), 0)),
                    whole_small,
                    pl.BlockSpec(clip_block, lambda c, sec: (at(c), 0, 0)),
                    pl.BlockSpec(clip_block, lambda c, sec: (sec[0] * half + at(c), 0, 0)),
                    whole_small,
                ]
                + [ANY] * len(others),
                out_specs=[
                    pl.BlockSpec(clip_block, lambda c, sec: (sec[0] * half + at(c), 0, 0)),
                    pl.BlockSpec(clip_block, lambda c, sec: (at(c), 0, 0)),
                    whole_small,
                ],
                scratch_shapes=[
                    pltpu.VMEM((width, hidden), BF16),
                    pltpu.VMEM((len(OFFSETS) * frames, frames), BF16),
                    pltpu.SemaphoreType.DMA,
                ],
            ),
            out_shape=[whole_struct, half_struct, small_struct],
            input_output_aliases={10 + i: i for i in range(len(others))},
            compiler_params=params(),
            cost_estimate=cost(2 * count * product, 12 << 20),
        )(sec, gpre0, up_own, up_got, normed0, inv0, small0, gin1, tokens, sums, *others)

    gin_own, gin_send, sums0 = last(0, half, sums0)
    got_gin = lax.ppermute(gin_send, "section", swap)
    got_sums = lax.ppermute(pick(first_section, sums1, sums0), "section", swap)

    def joined(whole, got):
        return lax.dynamic_update_slice(whole, got, ((1 - section) * half, 0, 0))[None]

    block_outputs = joined(out_own, got_out)
    input_grads = joined(gin_own, got_gin)
    pairs = [[keep0, got0], [keep1, got1]]
    if devices == BLOCKS:
        outs = halved(sec, place[None], speaker, pairs, sums0, sums1, got_sums, table_rows)
    else:
        outs = scattered(section, place, devices, speaker, pairs, sums0, sums1, got_sums, table_rows)
    return (block_outputs, input_grads) + outs


def exchanged(packet, step):
    devices = lax.axis_size("dp")
    moves = [
        (s * devices + i, s * devices + (i ^ (1 << ORDERS[s][step])))
        for s in range(2)
        for i in range(devices)
    ]
    return lax.ppermute(packet, PAIR, moves)


def halved(sec, place, speaker, pairs, sums0, sums1, got_sums, table_rows):
    _, share, width = pairs[0][0].shape
    pairs = [[piece.reshape(-1, width) for piece in pair] for pair in pairs]
    spot = (sec[0], place[0])
    half_rows = 8 * share

    def split(b):
        return pl.pallas_call(
            functools.partial(split_body, share),
            out_shape=struct((half_rows, width), BF16),
            in_specs=[SMEM, SMEM, HBM, HBM],
            out_specs=VMEM,
            scratch_shapes=[
                pltpu.VMEM((half_rows, width), BF16),
                pltpu.VMEM((half_rows, width), BF16),
                pltpu.SemaphoreType.DMA((4, 2)),
            ],
            compiler_params=params(),
            cost_estimate=cost(0, 4 << 20),
        )(sec, place, *pairs[b])

    def part(array, first, count):
        return lax.dynamic_slice_in_dim(array, first, count, 0).astype(F32)

    for b in (1, 0):
        packet = split(b)
        pairs[b].append(exchanged(packet, 0))

    def small_call(body, outs, scalars, operands, scratch=(), specs=None, limit=8):
        return pl.pallas_call(
            body,
            out_shape=outs,
            in_specs=[SMEM] * len(scalars) + (specs or [VMEM] * len(operands)),
            out_specs=[VMEM] * len(outs),
            scratch_shapes=scratch,
            compiler_params=params(limit),
            cost_estimate=cost(0, 2 << 20),
        )(*scalars, *operands)

    def row_outs(hop):
        return [struct(((16 << hop) + 16, width), BF16), struct((SCALE, width), F32)]

    rows_packet, smalls = small_call(begin_rows_body, row_outs(0), [sec, place, speaker], [sums0, sums1, got_sums])
    for hop in range(len(GATHER)):
        more = lax.ppermute(
            rows_packet, "dp", [(i, i ^ (1 << GATHER[hop])) for i in range(BLOCKS)]
        )
        operands = [rows_packet, more, smalls]
        if hop + 1 < len(GATHER):
            rows_packet, smalls = small_call(
                functools.partial(more_rows_body, hop + 1), row_outs(hop + 1), [place],
                operands,
            )
    owned = table_rows // BLOCKS
    lanes = width // BLOCKS
    one = struct((1, lanes), F32)
    scale, shift, taps, conv, upb, downb, gain = small_call(
        tables_body,
        [
            struct((owned, width), F32),
            struct((owned, width), F32),
            struct((7, 1, lanes), F32),
            one,
            struct((1, 3 * lanes), F32),
            one,
            one,
        ],
        [place],
        operands,
        [pltpu.VMEM((16 * BLOCKS, width), BF16)],
    )

    totals, latest = None, None
    for step in range(1, 4):
        rows = (8 >> step) * share
        first = bit_of(spot, step) * rows
        packet_struct = [struct((2 * rows, width), BF16)]
        if step == 1:
            (packet,) = small_call(
                functools.partial(second_body, share), packet_struct, [sec, place],
                pairs[0] + pairs[1],
                [pltpu.VMEM((6, rows, width), BF16), pltpu.SemaphoreType.DMA((6,))],
                [HBM] * 6,
                None,
            )
        else:
            (packet,) = small_call(
                functools.partial(pack_body, step, share), packet_struct, [sec, place],
                totals + [latest],
            )
        got = exchanged(packet, step)
        if step == 1:
            start = bit_of(spot, 0) * 2 * rows + first
            totals = [
                part(keep, start, rows) + part(swapped, start, rows) + part(came, first, rows)
                for keep, swapped, came in pairs
            ]
        else:
            totals = [
                part(totals[b], first, rows) + part(latest, 2 * b * rows + first, rows)
                for b in range(2)
            ]
        latest = got
    mine, away = small_call(
        functools.partial(share_body, share), [struct((share, width), F32)] * 2, [sec],
        totals + [latest],
    )
    got_share = lax.ppermute(away, "section", [(0, 1), (1, 0)])
    up, down = small_call(
        finish_body, [struct((width // BLOCKS, 3 * TILE), F32), struct((share, width), F32)], [sec], [mine, got_share]
    )
    return (
        taps.transpose(1, 0, 2), conv, scale[None], shift[None], up[None], upb, down[None], downb, gain
    )


def scattered(section, place, devices, speaker, pairs, sums0, sums1, got_sums, table_rows):
    first_section = section == 0
    own_sums = pick(first_section, sums0, sums1)
    smalls = lax.psum(own_sums[:SCALE] + got_sums[:SCALE], "dp")
    clip_rows = jnp.stack([own_sums[SCALE:], got_sums[SCALE:]])
    clip_rows = pick(first_section, clip_rows, clip_rows[::-1]).astype(BF16)
    clips = speaker.shape[0]
    width = clip_rows.shape[-1]
    clip_rows = clip_rows.reshape(2, 2, clips // 2, width).transpose(1, 0, 2, 3).reshape(2, clips, width)
    gathered = lax.all_gather(clip_rows, "dp", axis=1, tiled=True)
    who = lax.all_gather(speaker, "dp", tiled=True)
    owned = table_rows // devices
    wanted = place * owned + jnp.arange(owned, dtype=jnp.int32)
    chosen = (who[None, :] == wanted[:, None]).astype(BF16)
    tables = [jnp.dot(chosen, gathered[k], preferred_element_type=F32) for k in range(2)]
    natural = []
    for order in ORDERS:
        natural.append(
            jnp.stack(
                [
                    jnp.stack([pair[0][position(i, order)].astype(F32) + pair[1][position(i, order)].astype(F32) for i in range(BLOCKS)])
                    for pair in pairs
                ]
            )
        )
    blocks, _, rows, width = natural[0].shape
    tiles = rows * BLOCKS // TILE
    up = natural[0].reshape(blocks, BLOCKS, tiles, rows // tiles, TILE).transpose(0, 1, 3, 2, 4)
    flat = pick(
        first_section, up.reshape(blocks, devices, -1), natural[1].reshape(blocks, devices, -1)
    )
    share = lax.psum_scatter(flat, "dp", scatter_dimension=1, tiled=True)[:, 0]
    own_share = lax.dynamic_index_in_dim(share, section, 0, keepdims=False)
    got_share = lax.ppermute(
        lax.dynamic_index_in_dim(share, 1 - section, 0, keepdims=False), "section", [(0, 1), (1, 0)]
    )
    up_share = pick(first_section, own_share, got_share).reshape(width // devices, -1)
    down_share = pick(first_section, got_share, own_share).reshape(-1, width)
    lanes = width // devices
    own_lanes = lax.dynamic_slice_in_dim(smalls, place * lanes, lanes, 1)
    upb = lax.dynamic_slice_in_dim(smalls[UPB : UPB + 3].reshape(-1), place * 3 * lanes, 3 * lanes, 0)
    return (
        own_lanes[TAPS : TAPS + 7][None],
        own_lanes[CONV : CONV + 1],
        tables[0][None],
        tables[1][None],
        up_share[None],
        upb[None],
        down_share[None],
        own_lanes[DOWNB : DOWNB + 1],
        own_lanes[GAIN : GAIN + 1],
    )


def solution(mesh):
    placed = (
        P("dp", None, None),
        P("dp", None, None),
        P("dp"),
        P("dp"),
        P("section", None, None),
        P("section", None),
        P("section", None, None),
        P("section", None, None),
        P("section", None, None),
        P("section", None),
        P("section", None, None),
        P("section", None),
        P("section", None),
    )

    return jax.shard_map(
        local,
        mesh=mesh,
        in_specs=placed,
        out_specs=(
            P("section", "dp", None, None),
            P("section", "dp", None, None),
            P("section", None, "dp"),
            P("section", "dp"),
            P("section", "dp", None),
            P("section", "dp", None),
            P("section", "dp", None),
            P("section", "dp"),
            P("section", "dp", None),
            P("section", "dp"),
            P("section", "dp"),
        ),
        check_vma=False,
    )
```

```python
import functools

import jax
import jax.numpy as jnp
from jax import lax
from jax.experimental import pallas as pl
from jax.experimental.pallas import tpu as pltpu
from jax.sharding import PartitionSpec as P


F32 = jnp.float32
BF16 = jnp.bfloat16
PAIR = ("section", "dp")
TILE = 512
ALL_VMEM = 67043328
HALF_ROOT = 0.7071067811865476
DENSITY = 0.3989422804014327
BLOCKS = 16
ORDERS = ((0, 1, 2, 3), (2, 0, 1, 3))
ANY = pl.BlockSpec(memory_space=pl.ANY)
HBM = pl.BlockSpec(memory_space=pltpu.HBM)
VMEM = pl.BlockSpec(memory_space=pltpu.VMEM)
SMEM = pl.BlockSpec(memory_space=pltpu.SMEM)

TAPS, CONV, UPB, DOWNB, GAIN, SCALE, SHIFT, SMALL = 0, 7, 8, 11, 12, 16, 20, 24


def position(block, order):
    place = 0
    for bit in order:
        place = 2 * place + ((block >> bit) & 1)
    return place


def dot(a, b, dims):
    return lax.dot_general(a, b, (dims, ((), ())), preferred_element_type=F32)


NN = ((1,), (0,))
NT = ((1,), (1,))
TN = ((0,), (0,))


OFFSETS = (-3, -2, -1, 1, 2, 3)


def set_shifts(shifts):
    frames = shifts.shape[1]
    row = lax.broadcasted_iota(jnp.int32, (frames, frames), 0)
    col = lax.broadcasted_iota(jnp.int32, (frames, frames), 1)
    for n, offset in enumerate(OFFSETS):
        shifts[n * frames : (n + 1) * frames] = jnp.where(col == row + offset, 1.0, 0.0).astype(BF16)


def shifted(shifts, x, offset):
    frames = x.shape[0]
    n = OFFSETS.index(offset)
    return dot(shifts[n * frames : (n + 1) * frames], x, NN)


def wide(x, width):
    return jnp.concatenate([x] * (width // 128), axis=1)


def rowsum(x):
    return jnp.sum(x, axis=0, keepdims=True)


def normalize(x, small, clip, shifts):
    conv = small[CONV : CONV + 1] + x.astype(F32) * small[3:4]
    for offset in OFFSETS:
        conv = conv + shifted(shifts, x, offset) * small[offset + 3 : offset + 4]
    centred = conv - jnp.mean(conv, axis=-1, keepdims=True)
    inv = lax.rsqrt(jnp.mean(centred * centred, axis=-1, keepdims=True) + 1e-06)
    normed = centred * inv
    scale = small[pl.ds(SCALE + clip, 1)]
    shift = small[pl.ds(SHIFT + clip, 1)]
    adapted = (normed * scale + shift).astype(BF16)
    return adapted, normed.astype(BF16), jnp.broadcast_to(inv, (x.shape[0], 128))


def prep_body(sec, speaker, taps, conv, upb, downb, gain, scale_hbm, shift_hbm, own, other, sems):
    width = own.shape[1]
    half = SMALL - SHIFT
    copies = []
    for side, out in enumerate((own, other)):
        first = (sec[0] if side == 0 else 1 - sec[0]) * half
        for clip in range(half):
            row = speaker[first + clip]
            for kind, table in enumerate((scale_hbm, shift_hbm)):
                copies.append(
                    pltpu.make_async_copy(
                        table.at[0, pl.ds(row, 1)],
                        out.at[pl.ds((SCALE, SHIFT)[kind] + clip, 1)],
                        sems.at[side, kind, clip],
                    )
                )
    for copy in copies:
        copy.start()
    for out in (own, other):
        for k in range(7):
            out[TAPS + k : TAPS + k + 1] = taps[k]
        out[CONV : CONV + 1] = conv[...]
        for k in range(DOWNB - UPB):
            out[UPB + k : UPB + k + 1] = upb[:, k * width : (k + 1) * width]
        out[DOWNB : DOWNB + 1] = downb[...]
        out[GAIN : GAIN + 1] = gain[...]
        out[GAIN + 1 : SCALE] = jnp.zeros((SCALE - GAIN - 1, width), F32)
    for copy in copies:
        copy.wait()


def forward_tiles(adapted, up, down, small, act, slope, acc):
    steps = [(j, r) for j in range(3) for r in range(acc.shape[0] // 256)]

    def hidden(j, r):
        part = dot(adapted[r * 256 : (r + 1) * 256], up[:, j * TILE : (j + 1) * TILE], NN)
        return part + small[UPB + j : UPB + j + 1]

    ahead = hidden(*steps[0])
    for n, (j, r) in enumerate(steps):
        rows = slice(r * 256, (r + 1) * 256)
        pre = ahead
        if n + 1 < len(steps):
            ahead = hidden(*steps[n + 1])
        phi = 0.5 * lax.erf(pre * HALF_ROOT) + 0.5
        low = (pre * phi).astype(BF16)
        act[j, rows] = low
        slope[j, rows] = (phi + pre * (DENSITY * jnp.exp(-0.5 * pre * pre))).astype(BF16)
        part = dot(low, down[j * TILE : (j + 1) * TILE], NN)
        acc[rows] = part if j == 0 else acc[rows] + part


def activation_tile(j, gb, down, slope, sums):
    total = jnp.zeros((1, TILE), F32)
    for r in range(gb.shape[0] // 256):
        rows = slice(r * 256, (r + 1) * 256)
        gact = dot(gb[rows], down[j * TILE : (j + 1) * TILE], NT)
        gpre = (gact * slope[j, rows].astype(F32)).astype(BF16)
        slope[j, rows] = gpre
        total = total + rowsum(gpre.astype(F32))
    sums[UPB + j : UPB + j + 1] = total


def down_pieces(j):
    share = 3 * TILE // BLOCKS
    at, pieces = j * TILE, []
    while at < (j + 1) * TILE:
        stop = min((at // share + 1) * share, (j + 1) * TILE)
        pieces.append((position(at // share, ORDERS[1]), at % share, stop - at, at - j * TILE))
        at = stop
    return pieces


def weight_tile(j, gb, adapted, act, gpre, upd, dnd):
    gup = dot(adapted[...], gpre, TN).astype(BF16)
    share = TILE // BLOCKS
    for i in range(BLOCKS):
        upd[position(i, ORDERS[0]), j * share : (j + 1) * share] = gup[i * share : (i + 1) * share]
    gdn = dot(act, gb[...], TN).astype(BF16)
    for block, first, rows, at in down_pieces(j):
        dnd[block, first : first + rows] = gdn[at : at + rows]


def norm_backward(gad, normed, inv, small, clip, grad_out, v, shifts):
    n = normed.astype(F32)
    width = n.shape[1]
    scale = small[pl.ds(SCALE + clip, 1)]
    g_shift = rowsum(gad)
    g_scale = rowsum(gad * n)
    gn = gad * scale
    m1 = jnp.mean(gn, axis=-1, keepdims=True)
    m2 = jnp.mean(gn * n, axis=-1, keepdims=True)
    gc = (gn - m1 - n * m2) * wide(inv, width)
    low = gc.astype(BF16)
    total = grad_out + gc * small[3:4]
    v = v.astype(F32)
    g_taps = []
    for k in range(7):
        if k == 3:
            g_taps.append(rowsum(gc * v))
            continue
        moved = shifted(shifts, low, 3 - k)
        total = total + moved * small[k : k + 1]
        g_taps.append(rowsum(moved * v))
    return total.astype(BF16), jnp.concatenate(g_taps + [rowsum(gc)], axis=0), g_scale, g_shift


def place_weights(sec, block, up_own, up_got, down_own, down_got, up, down, sems, start):
    def go(up_from, down_from):
        for source, target, sem in ((up_from, up, sems.at[0]), (down_from, down, sems.at[1])):
            copy = pltpu.make_async_copy(source, target, sem)
            copy.start() if start else copy.wait()

    if not start:
        go(up_own, down_own)
        return

    @pl.when(sec[0] == block)
    def _():
        go(up_own, down_own)

    @pl.when(sec[0] != block)
    def _():
        go(up_got, down_got)


def leaving(sec, place):
    low, high = ORDERS[0][0], ORDERS[1][0]
    return 1 - ((place[0] >> pick(sec[0] == 0, high, low)) & 1)


def route_tile(sec, place, j, upd, dnd, keep, passed, stays, sems, start):
    share = TILE // BLOCKS
    part = pl.ds(j * share, share)
    half = BLOCKS // 2
    goes = leaving(sec, place)

    def run(copy):
        copy.start() if start else copy.wait()

    def up_copies(first, second):
        for n, (source, target) in enumerate(((goes, first), (1 - goes, second))):
            run(
                pltpu.make_async_copy(
                    upd.at[pl.ds(source * half, half), part], target.at[:, part], sems.at[j, n]
                )
            )

    def down_copies(pick_target):
        for n, (block, first, rows, _) in enumerate(down_pieces(j)):
            pick_target(n, block, pl.ds(first, rows))

    def down_to(target, n, source, block, rows):
        run(pltpu.make_async_copy(dnd.at[source, rows], target.at[block, rows], sems.at[j, 2 + n]))

    def down_kept(n, block, rows):
        down_to(keep, n, block, block, rows)

    def down_sent(n, block, rows):
        @pl.when(goes == block // half)
        def _():
            down_to(passed, n, block, block % half, rows)

        @pl.when(goes != block // half)
        def _():
            down_to(stays, n, block, block % half, rows)

    if not start:
        up_copies(passed, stays)
        down_copies(down_kept)
        return

    @pl.when(sec[0] == 0)
    def _():
        up_copies(keep.at[pl.ds(goes * half, half)], keep.at[pl.ds((1 - goes) * half, half)])
        down_copies(down_sent)

    @pl.when(sec[0] != 0)
    def _():
        up_copies(passed, stays)
        down_copies(down_kept)


def route_halves(sec, place, upd, dnd, keep, passed, stays, sems, start):
    half = BLOCKS // 2
    goes = leaving(sec, place)

    def go(kept, sent):
        for n, (source, target) in enumerate(
            (
                (kept, keep),
                (sent.at[pl.ds(goes * half, half)], passed),
                (sent.at[pl.ds((1 - goes) * half, half)], stays),
            )
        ):
            copy = pltpu.make_async_copy(source, target, sems.at[n])
            copy.start() if start else copy.wait()

    if not start:
        go(upd, dnd)
        return

    @pl.when(sec[0] == 0)
    def _():
        go(upd, dnd)

    @pl.when(sec[0] != 0)
    def _():
        go(dnd, upd)


def route(sec, upd, dnd, keep, send, sems, start):
    def go(kept, sent):
        for source, target, sem in ((kept, keep, sems.at[0]), (sent, send, sems.at[1])):
            copy = pltpu.make_async_copy(source, target, sem)
            copy.start() if start else copy.wait()

    if not start:
        go(upd, dnd)
        return

    @pl.when(sec[0] == 0)
    def _():
        go(upd, dnd)

    @pl.when(sec[0] != 0)
    def _():
        go(dnd, upd)


def main_body(
    sec, place, valid, own_small, got_small, tokens, cot, up_own, up_got, down_own, down_got,
    sums0, sums1, gin1, normed_hbm, inv_hbm, out_own, out_send, gpre_hbm, keep1, passed1, stays1, keep0, passed0,
    stays0, small0_out,
    up0, down0, up1, down1, act0, slope0, act1, slope1, acc, adapted0, normed, inv, adapted1, branch0,
    gb, v, grad, out0, out1, small0, small1, shifts, upd, dnd, upd0, dnd0, sems, pieces, parts, halves,
):
    clips = acc.shape[0] // 256
    mine = pl.ds(sec[0] * clips, clips)
    loads = (
        pltpu.make_async_copy(tokens.at[mine], v, sems.at[6, 0]),
        pltpu.make_async_copy(cot.at[mine], grad, sems.at[6, 1]),
    )
    loads[0].start()
    weights = (up_own, up_got, down_own, down_got)
    place_weights(sec, 0, *weights, up0, down0, sems.at[0], True)
    place_weights(sec, 1, *weights, up1, down1, sems.at[1], True)
    loads[1].start()
    first = sec[0] == 0
    small0[...] = pick(first, own_small[...], got_small[...])
    small1[...] = pick(first, got_small[...], own_small[...])
    small0_out[...] = small0[...]
    sums0[...] = jnp.zeros_like(sums0)
    sums1[...] = jnp.zeros_like(sums1)
    set_shifts(shifts)
    loads[0].wait()

    def begin(r):
        rows = pl.ds(pl.multiple_of(r * 256, 256), 256)
        adapted0[rows], normed[rows], inv[rows] = normalize(v[r], small0, r, shifts)

    pl.loop(0, clips, unroll=True)(begin)
    saves = [
        pltpu.make_async_copy(source, target, sems.at[7 + n // 2, n % 2])
        for n, (source, target) in enumerate(
            ((normed, normed_hbm), (inv, inv_hbm))
        )
    ]
    for copy in saves:
        copy.start()
    place_weights(sec, 0, *weights, up0, down0, sems.at[0], False)
    forward_tiles(adapted0, up0, down0, small0, act0, slope0, acc)
    for copy in saves:
        copy.wait()

    def between(r):
        rows = pl.ds(pl.multiple_of(r * 256, 256), 256)
        branch = acc[rows] + small0[DOWNB : DOWNB + 1]
        branch0[rows] = branch
        result = (v[r].astype(F32) + small0[GAIN : GAIN + 1] * branch).astype(BF16)
        out0[r] = result
        adapted1[rows], normed[rows], inv[rows] = normalize(result, small1, r, shifts)

    pl.loop(0, clips, unroll=True)(between)
    place_weights(sec, 1, *weights, up1, down1, sems.at[1], False)
    forward_tiles(adapted1, up1, down1, small1, act1, slope1, acc)
    loads[1].wait()

    def top(r):
        rows = pl.ds(pl.multiple_of(r * 256, 256), 256)
        branch = acc[rows] + small1[DOWNB : DOWNB + 1]
        gain = small1[GAIN : GAIN + 1]
        out1[r] = (out0[r].astype(F32) + gain * branch).astype(BF16)
        above = grad[r].astype(F32) * valid[sec[0] * clips + r].astype(F32)
        low = (above * gain).astype(BF16)
        gb[rows] = low
        sums1[GAIN : GAIN + 1] += rowsum(above * branch)
        sums1[DOWNB : DOWNB + 1] += rowsum(low.astype(F32))

    pl.loop(0, clips)(top)
    half_own = out_own.at[mine]
    route(sec, out0, out1, half_own, out_send, sems.at[4], True)
    for j in range(3):
        activation_tile(j, gb, down1, slope1, sums1)
        for r in range(clips):
            rows = slice(r * 256, (r + 1) * 256)
            part = dot(slope1[j, rows], up1[:, j * TILE : (j + 1) * TILE], NT)
            acc[rows] = part if j == 0 else acc[rows] + part
        weight_tile(j, gb, adapted1, act1[j], slope1[j], upd, dnd)
    route_halves(sec, place, upd, dnd, keep1, passed1, stays1, halves, True)

    def move(r):
        return pltpu.make_async_copy(grad.at[r], gin1.at[r], pieces.at[r])

    def under(r):
        rows = pl.ds(pl.multiple_of(r * 256, 256), 256)
        above = grad[r].astype(F32) * valid[sec[0] * clips + r].astype(F32)
        gin, smalls, g_scale, g_shift = norm_backward(
            acc[rows], normed[rows], inv[rows], small1, r, above, out0[r], shifts
        )
        grad[r] = gin
        sums1[TAPS : TAPS + 8] += smalls
        sums1[pl.ds(SCALE + r, 1)] = g_scale
        sums1[pl.ds(SHIFT + r, 1)] = g_shift
        grad0 = gin.astype(F32)
        low = (grad0 * small0[GAIN : GAIN + 1]).astype(BF16)
        gb[rows] = low
        move(r).start()
        sums0[GAIN : GAIN + 1] += rowsum(grad0 * branch0[rows])
        sums0[DOWNB : DOWNB + 1] += rowsum(low.astype(F32))

    pl.loop(0, clips)(under)
    tiles = []
    for j in range(3):
        activation_tile(j, gb, down0, slope0, sums0)
        tiles.append(pltpu.make_async_copy(slope0.at[j], gpre_hbm.at[j], sems.at[5 + j // 2 * 3, j % 2]))
        tiles[-1].start()
        weight_tile(j, gb, adapted0, act0[j], slope0[j], upd0, dnd0)
        route_tile(sec, place, j, upd0, dnd0, keep0, passed0, stays0, parts, True)
    route(sec, out0, out1, half_own, out_send, sems.at[4], False)
    route_halves(sec, place, upd, dnd, keep1, passed1, stays1, halves, False)
    for copy in tiles + [move(r) for r in range(clips)]:
        copy.wait()
    for j in range(3):
        route_tile(sec, place, j, upd0, dnd0, keep0, passed0, stays0, parts, False)


def last_body(
    sec, gpre, up_own, up_got, normed, inv, small, grad_out, tokens, sums0, sums1, gin, away, own, send,
    up, shifts, sums, sem,
):
    clip = pl.program_id(0)

    @pl.when(clip == 0)
    def _():
        sums[...] = sums0[...]

        @pl.when(sec[0] == 0)
        def _():
            pltpu.make_async_copy(up_own, up, sem).start()

        @pl.when(sec[0] != 0)
        def _():
            pltpu.make_async_copy(up_got, up, sem).start()

        set_shifts(shifts)
        pltpu.make_async_copy(up_own, up, sem).wait()

    gad = dot(gpre[0], up[:, :TILE], NT)
    for j in range(1, 3):
        gad = gad + dot(gpre[j], up[:, j * TILE : (j + 1) * TILE], NT)
    above = grad_out[0]
    out, smalls, g_scale, g_shift = norm_backward(
        gad, normed[...], inv[...], small, clip, above.astype(F32), tokens[0], shifts
    )
    gin[0] = jnp.where(sec[0] == 0, out, above)
    away[0] = jnp.where(sec[0] == 0, above, out)
    sums[TAPS : TAPS + 8] += smalls
    sums[pl.ds(SCALE + clip, 1)] = g_scale
    sums[pl.ds(SHIFT + clip, 1)] = g_shift

    @pl.when(clip == pl.num_programs(0) - 1)
    def _():
        own[...] = pick(sec[0] == 0, sums[...], sums1[...])
        send[...] = pick(sec[0] == 0, sums1[...], sums[...])


def pick(first, a, b):
    return jnp.where(first, a, b)


def bit_of(spot, step):
    low, high = ORDERS[0][step], ORDERS[1][step]
    return (spot[1] >> (low if low == high else pick(spot[0] == 0, low, high))) & 1


GATHER = (3, 2, 0, 1)


def gather_bit(spot, hop):
    return (spot[1] >> GATHER[hop]) & 1


def gather_slot(spot):
    slot = 0
    for hop in range(len(GATHER)):
        slot = slot + gather_bit(spot, hop) * (1 << hop)
    return slot


def fetch(copies, source, first, rows, target, sem):
    copies.append(pltpu.make_async_copy(source.at[pl.ds(first, rows)], target, sem))
    copies[-1].start()


def pack_body(step, share, sec, place, total0, total1, *refs):
    rows = (8 >> step) * share
    first = pl.multiple_of((1 - bit_of((sec[0], place[0]), step)) * rows, 32)
    if step == 1:
        came, (packet, buffer, sems) = refs[:2], refs[2:]
        copies = []
        for b in range(2):
            fetch(copies, came[b], first, rows, buffer.at[b], sems.at[b])
    else:
        came, packet = refs
    for b, total in enumerate((total0, total1)):
        if step == 1:
            copies[b].wait()
            latest = buffer[b]
        else:
            latest = came[pl.ds(b * 2 * rows + first, rows)]
        packet[b * rows : (b + 1) * rows] = (total[pl.ds(first, rows)] + latest.astype(F32)).astype(BF16)


def share_body(share, sec, total0, total1, came, mine, away):
    for b, total in enumerate((total0, total1)):
        whole = total[...] + came[b * share : (b + 1) * share].astype(F32)
        for target, stays in ((mine, True), (away, False)):

            @pl.when((sec[0] == b) == stays)
            def _():
                target[...] = whole


def begin_rows_body(sec, place, speaker, own_sums, got_sums, packet, smalls, held, sems):
    spot = (sec[0], place[0])
    first = spot[0] == 0
    copies = []
    for n, source in enumerate((own_sums, got_sums)):
        fetch(copies, source, 0, SMALL, held.at[n], sems.at[n])
    for copy in copies:
        copy.wait()
    own, other = held[0], held[1]
    low = pick(first, own[SCALE:], other[SCALE:])
    high = pick(first, other[SCALE:], own[SCALE:])
    packet[:16] = jnp.concatenate([low, high], axis=0).astype(BF16)
    lane = lax.broadcasted_iota(jnp.int32, (1, own.shape[1]), 1)
    here = (lane >> 4) == gather_slot(spot)
    which = ((lane >> 3) & 1) * 4 + (lane & 3)
    code = jnp.zeros(lane.shape, jnp.int32)
    for c in range(8):
        code = jnp.where(here & (which == c), speaker[c], code)
    smalls[...] = own[:SCALE] + other[:SCALE]
    smalls[13:14] = (code >> 6).astype(F32)
    smalls[14:15] = (code & 63).astype(F32)
    packet[16:32] = smalls[...].astype(BF16)


def more_rows_body(hop, place, before, after, smalls_in, packet, smalls):
    size = 16 << (hop - 1)
    bit = gather_bit((0, place[0]), hop - 1)
    for source, side in ((before, bit), (after, 1 - bit)):
        packet[pl.ds(pl.multiple_of(side * size, 16), size)] = source[:size]
    smalls[...] = smalls_in[...] + after[size:].astype(F32)
    packet[2 * size :] = smalls[...].astype(BF16)


def tables_body(place, before, after, smalls_in, scale, shift, taps, conv, upb, downb, gain, rows_of):
    size = rows_of.shape[0] // 2
    bit = gather_bit((0, place[0]), len(GATHER) - 1)
    for source, side in ((before, bit), (after, 1 - bit)):
        rows_of[pl.ds(pl.multiple_of(side * size, 16), size)] = source[:size]
    total = smalls_in[...] + after[size:].astype(F32)
    owned = scale.shape[0]
    count = 2 * size
    who = total[13:14, :count] * 64.0 + total[14:15, :count]
    wanted = lax.broadcasted_iota(jnp.int32, (owned, count), 0) + place[0] * owned
    hit = who == wanted.astype(F32)
    kind = (lax.broadcasted_iota(jnp.int32, (owned, count), 1) >> 2) & 1
    for k, out in enumerate((scale, shift)):
        out[...] = dot(jnp.where(hit & (kind == k), 1.0, 0.0).astype(BF16), rows_of[...], NN)
    lanes = total.shape[1] // BLOCKS
    turn = lax.rem(BLOCKS - place[0], BLOCKS)
    cut = pltpu.roll(total, turn * lanes, 1)[:, :lanes]
    for k in range(7):
        taps[k] = cut[k : k + 1]
    conv[...] = cut[CONV : CONV + 1]
    downb[...] = cut[DOWNB : DOWNB + 1]
    gain[...] = cut[GAIN : GAIN + 1]
    line = jnp.concatenate([total[UPB + k : UPB + k + 1] for k in range(3)], axis=1)
    upb[...] = pltpu.roll(line, turn * 3 * lanes, 1)[:, : 3 * lanes]


def finish_body(sec, mine, got, up, down):
    first = sec[0] == 0
    rows = up.shape[0]
    ups = pick(first, mine[...], got[...])
    for j in range(3):
        up[:, j * TILE : (j + 1) * TILE] = ups[j * rows : (j + 1) * rows]
    down[...] = pick(first, got[...], mine[...])


def struct(shape, dtype):
    return jax.ShapeDtypeStruct(shape, dtype)


def params(limit=None):
    return pltpu.CompilerParams(vmem_limit_bytes=limit * 1024 * 1024 if limit else ALL_VMEM)


def cost(flops, moved):
    return pl.CostEstimate(flops=int(flops), bytes_accessed=int(moved), transcendentals=0)


def local(
    tokens, out_cotangent, speaker, valid, conv_weight, conv_bias, scale_table, shift_table,
    up_weight, up_bias, down_weight, down_bias, layer_scale,
):
    section = lax.axis_index("section").astype(jnp.int32)
    place = lax.axis_index("dp").astype(jnp.int32)
    devices = lax.axis_size("dp")
    clips, frames, width = tokens.shape
    hidden = up_weight.shape[2]
    table_rows = scale_table.shape[1]
    half = clips // 2
    rows = half * frames
    sec = section[None]
    swap = [(0, 1), (1, 0)]

    own_small, other_small = pl.pallas_call(
        prep_body,
        out_shape=[struct((SMALL, width), F32)] * 2,
        in_specs=[SMEM, SMEM] + [VMEM] * 5 + [ANY] * 2,
        out_specs=[VMEM] * 2,
        scratch_shapes=[pltpu.SemaphoreType.DMA((2, 2, half))],
        compiler_params=params(),
        name="prep",
    )(
        sec, speaker, conv_weight.transpose(1, 0, 2), conv_bias, up_bias, down_bias, layer_scale,
        scale_table, shift_table,
    )
    got_small = lax.ppermute(other_small, "section", swap)
    up_own, down_own = up_weight[0], down_weight[0]
    up_got = lax.ppermute(up_own, "section", swap)
    down_got = lax.ppermute(down_own, "section", swap)
    clip_block = (1, frames, width)
    whole_small = pl.BlockSpec((SMALL, width), lambda c, sec: (0, 0))
    half_struct = struct((half, frames, width), BF16)
    whole_struct = struct((clips, frames, width), BF16)
    small_struct = struct((SMALL, width), F32)
    flat_struct = struct((rows, width), BF16)
    tiles = hidden // TILE
    tiled = (tiles, rows, TILE)
    share = hidden // BLOCKS
    gradient = (BLOCKS, share, width)
    gradient_struct = struct(gradient, BF16)
    piece_struct = struct((BLOCKS // 2, share, width), BF16)
    product = 2 * rows * width * hidden

    (
        sums0, sums1, gin1, normed0, inv0, out_own, out_send, gpre0, keep1, passed1,
        stays1, keep0, passed0, stays0, small0,
    ) = pl.pallas_call(
        main_body,
        out_shape=[
            small_struct, small_struct, half_struct, flat_struct, struct((rows, 128), F32),
            whole_struct, half_struct, struct(tiled, BF16), gradient_struct, piece_struct, piece_struct,
            gradient_struct, piece_struct, piece_struct, small_struct,
        ],
        in_specs=[SMEM, SMEM, SMEM, VMEM, VMEM, HBM, HBM, HBM, ANY, HBM, ANY],
        out_specs=[VMEM, VMEM] + [HBM] * 12 + [VMEM],
        scratch_shapes=[
            pltpu.VMEM((width, hidden), BF16),
            pltpu.VMEM((hidden, width), BF16),
            pltpu.VMEM((width, hidden), BF16),
            pltpu.VMEM((hidden, width), BF16),
            pltpu.VMEM(tiled, BF16),
            pltpu.VMEM(tiled, BF16),
            pltpu.VMEM(tiled, BF16),
            pltpu.VMEM(tiled, BF16),
            pltpu.VMEM((rows, width), F32),
            pltpu.VMEM((rows, width), BF16),
            pltpu.VMEM((rows, width), BF16),
            pltpu.VMEM((rows, 128), F32),
            pltpu.VMEM((rows, width), BF16),
            pltpu.VMEM((rows, width), F32),
            pltpu.VMEM((rows, width), BF16),
            pltpu.VMEM((half, frames, width), BF16),
            pltpu.VMEM((half, frames, width), BF16),
            pltpu.VMEM((half, frames, width), BF16),
            pltpu.VMEM((half, frames, width), BF16),
            pltpu.VMEM((SMALL, width), F32),
            pltpu.VMEM((SMALL, width), F32),
            pltpu.VMEM((len(OFFSETS) * frames, frames), BF16),
            pltpu.VMEM(gradient, BF16),
            pltpu.VMEM(gradient, BF16),
            pltpu.VMEM(gradient, BF16),
            pltpu.VMEM(gradient, BF16),
            pltpu.SemaphoreType.DMA((9, 2)),
            pltpu.SemaphoreType.DMA((half,)),
            pltpu.SemaphoreType.DMA((3, 9)),
            pltpu.SemaphoreType.DMA((3,)),
        ],
        compiler_params=params(),
        cost_estimate=cost(11 * product, 24 << 20),
        name="main",
    )(
        sec, place[None], valid, own_small, got_small, tokens, out_cotangent, up_own, up_got, down_own, down_got
    )
    swapped = []
    for piece in (passed1, passed0, stays1, stays0):
        swapped.append(lax.ppermute(piece, "section", swap))
    pairs = [[keep0, swapped[1], swapped[3]], [keep1, swapped[0], swapped[2]]]
    got_out = lax.ppermute(out_send, "section", swap)

    gin_own, gin_send, own_sums, sums_send = pl.pallas_call(
        last_body,
        grid_spec=pltpu.PrefetchScalarGridSpec(
            num_scalar_prefetch=1,
            grid=(half,),
            in_specs=[
                pl.BlockSpec((tiles, frames, TILE), lambda c, sec: (0, c, 0)),
                HBM,
                ANY,
                pl.BlockSpec((frames, width), lambda c, sec: (c, 0)),
                pl.BlockSpec((frames, 128), lambda c, sec: (c, 0)),
                whole_small,
                pl.BlockSpec(clip_block, lambda c, sec: (c, 0, 0)),
                pl.BlockSpec(clip_block, lambda c, sec: (sec[0] * half + c, 0, 0)),
                whole_small,
                whole_small,
            ],
            out_specs=[
                pl.BlockSpec(clip_block, lambda c, sec: (sec[0] * half + c, 0, 0)),
                pl.BlockSpec(clip_block, lambda c, sec: (c, 0, 0)),
                whole_small,
                whole_small,
            ],
            scratch_shapes=[
                pltpu.VMEM((width, hidden), BF16),
                pltpu.VMEM((len(OFFSETS) * frames, frames), BF16),
                pltpu.VMEM((SMALL, width), F32),
                pltpu.SemaphoreType.DMA,
            ],
        ),
        out_shape=[whole_struct, half_struct, small_struct, small_struct],
        compiler_params=params(),
        cost_estimate=cost(2 * half * product, 12 << 20),
        name="last",
    )(sec, gpre0, up_own, up_got, normed0, inv0, small0, gin1, tokens, sums0, sums1)
    got_gin = lax.ppermute(gin_send, "section", swap)
    got_sums = lax.ppermute(sums_send, "section", swap)

    def joined(whole, got):
        return lax.dynamic_update_slice(whole, got, ((1 - section) * half, 0, 0))[None]

    block_outputs = joined(out_own, got_out)
    input_grads = joined(gin_own, got_gin)
    if devices == BLOCKS:
        outs = halved(sec, place[None], speaker, pairs, own_sums, got_sums, table_rows)
    else:
        outs = scattered(section, place, devices, speaker, pairs, own_sums, got_sums, table_rows)
    return (block_outputs, input_grads) + outs


def exchanged(packet, step):
    devices = lax.axis_size("dp")
    moves = [
        (s * devices + i, s * devices + (i ^ (1 << ORDERS[s][step])))
        for s in range(2)
        for i in range(devices)
    ]
    return lax.ppermute(packet, PAIR, moves)


def halved(sec, place, speaker, pairs, own_sums, got_sums, table_rows):
    _, share, width = pairs[0][0].shape
    pairs = [[piece.reshape(-1, width) for piece in pair] for pair in pairs]
    spot = (sec[0], place[0])
    half_rows = 8 * share

    def part(array, first, count):
        return lax.dynamic_slice_in_dim(array, first, count, 0).astype(F32)

    bit = bit_of(spot, 0)
    latest, totals = [None, None], [None, None]
    for b in (1, 0):
        keep, passed, stays = pairs[b]
        packet = (part(keep, (1 - bit) * half_rows, half_rows) + passed.astype(F32)).astype(BF16)
        latest[b] = exchanged(packet, 0)
        keep, stays, _ = lax.optimization_barrier((keep, stays, own_sums))
        totals[b] = part(keep, bit * half_rows, half_rows) + stays.astype(F32)

    def small_call(body, outs, scalars, operands, scratch=(), specs=None, limit=8):
        return pl.pallas_call(
            body,
            out_shape=outs,
            in_specs=[SMEM] * len(scalars) + (specs or [VMEM] * len(operands)),
            out_specs=[VMEM] * len(outs),
            scratch_shapes=scratch,
            compiler_params=params(limit),
            cost_estimate=cost(0, 2 << 20),
        )(*scalars, *operands)

    def row_outs(hop):
        return [struct(((16 << hop) + 16, width), BF16), struct((SCALE, width), F32)]

    rows_packet, smalls = small_call(
        begin_rows_body, row_outs(0), [sec, place, speaker],
        [own_sums, got_sums],
        [pltpu.VMEM((2, SMALL, width), F32), pltpu.SemaphoreType.DMA((2,))], [HBM] * 2,
    )
    for hop in range(len(GATHER)):
        more = lax.ppermute(
            rows_packet, "dp", [(i, i ^ (1 << GATHER[hop])) for i in range(BLOCKS)]
        )
        operands = [rows_packet, more, smalls]
        if hop + 1 < len(GATHER):
            rows_packet, smalls = small_call(
                functools.partial(more_rows_body, hop + 1), row_outs(hop + 1), [place],
                operands,
            )
    owned = table_rows // BLOCKS
    lanes = width // BLOCKS
    one = struct((1, lanes), F32)
    scale, shift, taps, conv, upb, downb, gain = small_call(
        tables_body,
        [
            struct((owned, width), F32),
            struct((owned, width), F32),
            struct((7, 1, lanes), F32),
            one,
            struct((1, 3 * lanes), F32),
            one,
            one,
        ],
        [place],
        operands,
        [pltpu.VMEM((16 * BLOCKS, width), BF16)],
    )

    for step in range(1, 4):
        rows = (8 >> step) * share
        first = bit_of(spot, step) * rows
        packet_struct = [struct((2 * rows, width), BF16)]
        if step == 1:
            (packet,) = small_call(
                functools.partial(pack_body, step, share), packet_struct, [sec, place],
                totals + latest,
                [pltpu.VMEM((2, rows, width), BF16), pltpu.SemaphoreType.DMA((2,))],
                [VMEM] * 2 + [ANY] * 2,
            )
        else:
            (packet,) = small_call(
                functools.partial(pack_body, step, share), packet_struct, [sec, place],
                totals + latest[:1],
            )
        got = exchanged(packet, step)
        bases = (0, 0) if step == 1 else (0, 2 * rows)
        totals = [
            part(totals[b], first, rows) + part(latest[b], bases[b] + first, rows) for b in range(2)
        ]
        latest = [got, got]
    mine, away = small_call(
        functools.partial(share_body, share), [struct((share, width), F32)] * 2, [sec],
        totals + latest[:1],
    )
    got_share = lax.ppermute(away, "section", [(0, 1), (1, 0)])
    up, down = small_call(
        finish_body, [struct((width // BLOCKS, 3 * TILE), F32), struct((share, width), F32)], [sec], [mine, got_share]
    )
    return (
        taps.transpose(1, 0, 2), conv, scale[None], shift[None], up[None], upb, down[None], downb, gain
    )


def scattered(section, place, devices, speaker, pairs, own_sums, got_sums, table_rows):
    first_section = section == 0
    smalls = lax.psum(own_sums[:SCALE] + got_sums[:SCALE], "dp")
    clip_rows = jnp.stack([own_sums[SCALE:], got_sums[SCALE:]])
    clip_rows = pick(first_section, clip_rows, clip_rows[::-1]).astype(BF16)
    clips = speaker.shape[0]
    width = clip_rows.shape[-1]
    clip_rows = clip_rows.reshape(2, 2, clips // 2, width).transpose(1, 0, 2, 3).reshape(2, clips, width)
    gathered = lax.all_gather(clip_rows, "dp", axis=1, tiled=True)
    who = lax.all_gather(speaker, "dp", tiled=True)
    owned = table_rows // devices
    wanted = place * owned + jnp.arange(owned, dtype=jnp.int32)
    chosen = (who[None, :] == wanted[:, None]).astype(BF16)
    tables = [jnp.dot(chosen, gathered[k], preferred_element_type=F32) for k in range(2)]
    low, high = ORDERS[0][0], ORDERS[1][0]
    leaves = 1 - ((place >> pick(first_section, low, high)) & 1)
    whole = []
    for keep, gone, stay in pairs:
        other = pick(leaves == 0, jnp.concatenate([gone, stay]), jnp.concatenate([stay, gone]))
        whole.append(keep.astype(F32) + other.astype(F32))
    natural = []
    for order in ORDERS:
        natural.append(
            jnp.stack([jnp.stack([total[position(i, order)] for i in range(BLOCKS)]) for total in whole])
        )
    blocks, _, rows, width = natural[0].shape
    tiles = rows * BLOCKS // TILE
    up = natural[0].reshape(blocks, BLOCKS, tiles, rows // tiles, TILE).transpose(0, 1, 3, 2, 4)
    flat = pick(
        first_section, up.reshape(blocks, devices, -1), natural[1].reshape(blocks, devices, -1)
    )
    share = lax.psum_scatter(flat, "dp", scatter_dimension=1, tiled=True)[:, 0]
    own_share = lax.dynamic_index_in_dim(share, section, 0, keepdims=False)
    got_share = lax.ppermute(
        lax.dynamic_index_in_dim(share, 1 - section, 0, keepdims=False), "section", [(0, 1), (1, 0)]
    )
    up_share = pick(first_section, own_share, got_share).reshape(width // devices, -1)
    down_share = pick(first_section, got_share, own_share).reshape(-1, width)
    lanes = width // devices
    own_lanes = lax.dynamic_slice_in_dim(smalls, place * lanes, lanes, 1)
    upb = lax.dynamic_slice_in_dim(smalls[UPB : UPB + 3].reshape(-1), place * 3 * lanes, 3 * lanes, 0)
    return (
        own_lanes[TAPS : TAPS + 7][None],
        own_lanes[CONV : CONV + 1],
        tables[0][None],
        tables[1][None],
        up_share[None],
        upb[None],
        down_share[None],
        own_lanes[DOWNB : DOWNB + 1],
        own_lanes[GAIN : GAIN + 1],
    )


def solution(mesh):
    placed = (
        P("dp", None, None),
        P("dp", None, None),
        P("dp"),
        P("dp"),
        P("section", None, None),
        P("section", None),
        P("section", None, None),
        P("section", None, None),
        P("section", None, None),
        P("section", None),
        P("section", None, None),
        P("section", None),
        P("section", None),
    )

    return jax.shard_map(
        local,
        mesh=mesh,
        in_specs=placed,
        out_specs=(
            P("section", "dp", None, None),
            P("section", "dp", None, None),
            P("section", None, "dp"),
            P("section", "dp"),
            P("section", "dp", None),
            P("section", "dp", None),
            P("section", "dp", None),
            P("section", "dp"),
            P("section", "dp", None),
            P("section", "dp"),
            P("section", "dp"),
        ),
        check_vma=False,
    )
```

```python
import functools

import jax
import jax.numpy as jnp
from jax import lax
from jax.experimental import pallas as pl
from jax.experimental.pallas import tpu as pltpu
from jax.sharding import PartitionSpec as P


F32 = jnp.float32
BF16 = jnp.bfloat16
PAIR = ("section", "dp")
TILE = 512
ALL_VMEM = 67043328
HALF_ROOT = 0.7071067811865476
DENSITY = 0.3989422804014327
BLOCKS = 16
ORDERS = ((0, 1, 2, 3), (2, 0, 1, 3))
ANY = pl.BlockSpec(memory_space=pl.ANY)
HBM = pl.BlockSpec(memory_space=pltpu.HBM)
VMEM = pl.BlockSpec(memory_space=pltpu.VMEM)
SMEM = pl.BlockSpec(memory_space=pltpu.SMEM)

TAPS, CONV, UPB, DOWNB, GAIN, SCALE, SHIFT, SMALL = 0, 7, 8, 11, 12, 16, 20, 24


def position(block, order):
    place = 0
    for bit in order:
        place = 2 * place + ((block >> bit) & 1)
    return place


def dot(a, b, dims):
    return lax.dot_general(a, b, (dims, ((), ())), preferred_element_type=F32)


NN = ((1,), (0,))
NT = ((1,), (1,))
TN = ((0,), (0,))


OFFSETS = (-3, -2, -1, 1, 2, 3)


def set_shifts(shifts):
    frames = shifts.shape[1]
    row = lax.broadcasted_iota(jnp.int32, (frames, frames), 0)
    col = lax.broadcasted_iota(jnp.int32, (frames, frames), 1)
    for n, offset in enumerate(OFFSETS):
        shifts[n * frames : (n + 1) * frames] = jnp.where(col == row + offset, 1.0, 0.0).astype(BF16)


def shifted(shifts, x, offset):
    frames = x.shape[0]
    n = OFFSETS.index(offset)
    return dot(shifts[n * frames : (n + 1) * frames], x, NN)


def wide(x, width):
    return jnp.concatenate([x] * (width // 128), axis=1)


def rowsum(x):
    return jnp.sum(x, axis=0, keepdims=True)


def normalize(x, small, clip, shifts):
    conv = small[CONV : CONV + 1] + x.astype(F32) * small[3:4]
    for offset in OFFSETS:
        conv = conv + shifted(shifts, x, offset) * small[offset + 3 : offset + 4]
    centred = conv - jnp.mean(conv, axis=-1, keepdims=True)
    inv = lax.rsqrt(jnp.mean(centred * centred, axis=-1, keepdims=True) + 1e-06)
    normed = centred * inv
    scale = small[pl.ds(SCALE + clip, 1)]
    shift = small[pl.ds(SHIFT + clip, 1)]
    adapted = (normed * scale + shift).astype(BF16)
    return adapted, normed.astype(BF16), jnp.broadcast_to(inv, (x.shape[0], 128))


def prep_body(sec, speaker, taps, conv, upb, downb, gain, scale_hbm, shift_hbm, own, other, sems):
    width = own.shape[1]
    half = SMALL - SHIFT
    copies = []
    for side, out in enumerate((own, other)):
        first = (sec[0] if side == 0 else 1 - sec[0]) * half
        for clip in range(half):
            row = speaker[first + clip]
            for kind, table in enumerate((scale_hbm, shift_hbm)):
                copies.append(
                    pltpu.make_async_copy(
                        table.at[0, pl.ds(row, 1)],
                        out.at[pl.ds((SCALE, SHIFT)[kind] + clip, 1)],
                        sems.at[side, kind, clip],
                    )
                )
    for copy in copies:
        copy.start()
    for out in (own, other):
        for k in range(7):
            out[TAPS + k : TAPS + k + 1] = taps[k]
        out[CONV : CONV + 1] = conv[...]
        for k in range(DOWNB - UPB):
            out[UPB + k : UPB + k + 1] = upb[:, k * width : (k + 1) * width]
        out[DOWNB : DOWNB + 1] = downb[...]
        out[GAIN : GAIN + 1] = gain[...]
        out[GAIN + 1 : SCALE] = jnp.zeros((SCALE - GAIN - 1, width), F32)
    for copy in copies:
        copy.wait()


def forward_tiles(adapted, up, down, small, act, slope, acc):
    steps = [(j, r) for j in range(3) for r in range(acc.shape[0] // 256)]

    def hidden(j, r):
        part = dot(adapted[r * 256 : (r + 1) * 256], up[:, j * TILE : (j + 1) * TILE], NN)
        return part + small[UPB + j : UPB + j + 1]

    ahead = hidden(*steps[0])
    for n, (j, r) in enumerate(steps):
        rows = slice(r * 256, (r + 1) * 256)
        pre = ahead
        if n + 1 < len(steps):
            ahead = hidden(*steps[n + 1])
        phi = 0.5 * lax.erf(pre * HALF_ROOT) + 0.5
        low = (pre * phi).astype(BF16)
        act[j, rows] = low
        slope[j, rows] = (phi + pre * (DENSITY * jnp.exp(-0.5 * pre * pre))).astype(BF16)
        part = dot(low, down[j * TILE : (j + 1) * TILE], NN)
        acc[rows] = part if j == 0 else acc[rows] + part


def activation_tile(j, gb, down, slope, sums):
    total = jnp.zeros((1, TILE), F32)
    for r in range(gb.shape[0] // 256):
        rows = slice(r * 256, (r + 1) * 256)
        gact = dot(gb[rows], down[j * TILE : (j + 1) * TILE], NT)
        gpre = (gact * slope[j, rows].astype(F32)).astype(BF16)
        slope[j, rows] = gpre
        total = total + rowsum(gpre.astype(F32))
    sums[UPB + j : UPB + j + 1] = total


def down_pieces(j, order):
    share = 3 * TILE // BLOCKS
    at, pieces = j * TILE, []
    while at < (j + 1) * TILE:
        stop = min((at // share + 1) * share, (j + 1) * TILE)
        pieces.append((position(at // share, order), at % share, stop - at, at - j * TILE))
        at = stop
    return pieces


def up_tile(j, order, adapted, gpre, upd):
    gup = dot(adapted[...], gpre, TN).astype(BF16)
    share = TILE // BLOCKS
    for i in range(BLOCKS):
        upd[position(i, order), j * share : (j + 1) * share] = gup[i * share : (i + 1) * share]


def down_tile(j, order, gb, act, dnd):
    gdn = dot(act, gb[...], TN).astype(BF16)
    for block, first, rows, at in down_pieces(j, order):
        dnd[block, first : first + rows] = gdn[at : at + rows]


def norm_backward(gad, normed, inv, small, clip, grad_out, v, shifts):
    n = normed.astype(F32)
    width = n.shape[1]
    scale = small[pl.ds(SCALE + clip, 1)]
    g_shift = rowsum(gad)
    g_scale = rowsum(gad * n)
    gn = gad * scale
    m1 = jnp.mean(gn, axis=-1, keepdims=True)
    m2 = jnp.mean(gn * n, axis=-1, keepdims=True)
    gc = (gn - m1 - n * m2) * wide(inv, width)
    low = gc.astype(BF16)
    total = grad_out + gc * small[3:4]
    v = v.astype(F32)
    g_taps = []
    for k in range(7):
        if k == 3:
            g_taps.append(rowsum(gc * v))
            continue
        moved = shifted(shifts, low, 3 - k)
        total = total + moved * small[k : k + 1]
        g_taps.append(rowsum(moved * v))
    return total.astype(BF16), jnp.concatenate(g_taps + [rowsum(gc)], axis=0), g_scale, g_shift


def place_weights(sec, block, up_own, up_got, down_own, down_got, up, down, sems, start):
    def go(up_from, down_from):
        for source, target, sem in ((up_from, up, sems.at[0]), (down_from, down, sems.at[1])):
            copy = pltpu.make_async_copy(source, target, sem)
            copy.start() if start else copy.wait()

    if not start:
        go(up_own, down_own)
        return

    @pl.when(sec[0] == block)
    def _():
        go(up_own, down_own)

    @pl.when(sec[0] != block)
    def _():
        go(up_got, down_got)


def leaving(block, place):
    return 1 - ((place[0] >> ORDERS[block][0]) & 1)


def route_block(block, layer, sec, place, sums, kept, passed, stays, sems, start):
    half = BLOCKS // 2
    goes = leaving(block, place)

    def go(*targets):
        for side, (target, first) in enumerate(zip(targets, (goes, 1 - goes))):
            part = sums.at[pl.ds(first * half, half)]
            copy = pltpu.make_async_copy(part, target, sems.at[layer, side])
            copy.start() if start else copy.wait()

    if not start:
        go(passed, stays)
        return

    @pl.when(sec[0] == block)
    def _():
        go(kept.at[pl.ds(goes * half, half)], kept.at[pl.ds((1 - goes) * half, half)])

    @pl.when(sec[0] != block)
    def _():
        go(passed, stays)


def route(sec, upd, dnd, keep, send, sems, start):
    def go(kept, sent):
        for source, target, sem in ((kept, keep, sems.at[0]), (sent, send, sems.at[1])):
            copy = pltpu.make_async_copy(source, target, sem)
            copy.start() if start else copy.wait()

    if not start:
        go(upd, dnd)
        return

    @pl.when(sec[0] == 0)
    def _():
        go(upd, dnd)

    @pl.when(sec[0] != 0)
    def _():
        go(dnd, upd)


def main_body(
    sec, place, valid, own_small, got_small, tokens, cot, up_own, up_got, down_own, down_got,
    sums0, sums1, gin1, normed_hbm, inv_hbm, out_own, out_send, gpre_hbm, up_keep, down_keep,
    up_pass, down_pass, up_stay, down_stay, small0_out,
    up0, down0, up1, down1, act0, slope0, act1, slope1, acc, adapted0, normed, inv, adapted1, branch0,
    gb, v, grad, out0, out1, small0, small1, shifts, upd, dnd, upd0, dnd0, sems, pieces, parts,
):
    clips = acc.shape[0] // 256
    mine = pl.ds(sec[0] * clips, clips)
    loads = (
        pltpu.make_async_copy(tokens.at[mine], v, sems.at[6, 0]),
        pltpu.make_async_copy(cot.at[mine], grad, sems.at[6, 1]),
    )
    loads[0].start()
    weights = (up_own, up_got, down_own, down_got)
    place_weights(sec, 0, *weights, up0, down0, sems.at[0], True)
    place_weights(sec, 1, *weights, up1, down1, sems.at[1], True)
    loads[1].start()
    first = sec[0] == 0
    small0[...] = pick(first, own_small[...], got_small[...])
    small1[...] = pick(first, got_small[...], own_small[...])
    small0_out[...] = small0[...]
    sums0[...] = jnp.zeros_like(sums0)
    sums1[...] = jnp.zeros_like(sums1)
    set_shifts(shifts)
    loads[0].wait()

    def begin(r):
        rows = pl.ds(pl.multiple_of(r * 256, 256), 256)
        adapted0[rows], normed[rows], inv[rows] = normalize(v[r], small0, r, shifts)

    pl.loop(0, clips, unroll=True)(begin)
    saves = [
        pltpu.make_async_copy(source, target, sems.at[7 + n // 2, n % 2])
        for n, (source, target) in enumerate(
            ((normed, normed_hbm), (inv, inv_hbm))
        )
    ]
    for copy in saves:
        copy.start()
    place_weights(sec, 0, *weights, up0, down0, sems.at[0], False)
    forward_tiles(adapted0, up0, down0, small0, act0, slope0, acc)
    for copy in saves:
        copy.wait()

    def between(r):
        rows = pl.ds(pl.multiple_of(r * 256, 256), 256)
        branch = acc[rows] + small0[DOWNB : DOWNB + 1]
        branch0[rows] = branch
        result = (v[r].astype(F32) + small0[GAIN : GAIN + 1] * branch).astype(BF16)
        out0[r] = result
        adapted1[rows], normed[rows], inv[rows] = normalize(result, small1, r, shifts)

    pl.loop(0, clips, unroll=True)(between)
    place_weights(sec, 1, *weights, up1, down1, sems.at[1], False)
    forward_tiles(adapted1, up1, down1, small1, act1, slope1, acc)
    loads[1].wait()

    def top(r):
        rows = pl.ds(pl.multiple_of(r * 256, 256), 256)
        branch = acc[rows] + small1[DOWNB : DOWNB + 1]
        gain = small1[GAIN : GAIN + 1]
        out1[r] = (out0[r].astype(F32) + gain * branch).astype(BF16)
        above = grad[r].astype(F32) * valid[sec[0] * clips + r].astype(F32)
        low = (above * gain).astype(BF16)
        gb[rows] = low
        sums1[GAIN : GAIN + 1] += rowsum(above * branch)
        sums1[DOWNB : DOWNB + 1] += rowsum(low.astype(F32))

    pl.loop(0, clips)(top)
    half_own = out_own.at[mine]
    route(sec, out0, out1, half_own, out_send, sems.at[4], True)
    for j in range(3):
        activation_tile(j, gb, down1, slope1, sums1)
        for r in range(clips):
            rows = slice(r * 256, (r + 1) * 256)
            part = dot(slope1[j, rows], up1[:, j * TILE : (j + 1) * TILE], NT)
            acc[rows] = part if j == 0 else acc[rows] + part
        up_tile(j, ORDERS[1], adapted1, slope1[j], upd)
        down_tile(j, ORDERS[1], gb, act1[j], dnd)
    ends = ((up_keep, up_pass, up_stay), (down_keep, down_pass, down_stay))
    for n, source in enumerate((upd, dnd)):
        route_block(1, n, sec, place, source, *ends[n], parts.at[1], True)

    def move(r):
        return pltpu.make_async_copy(grad.at[r], gin1.at[r], pieces.at[r])

    def under(r):
        rows = pl.ds(pl.multiple_of(r * 256, 256), 256)
        above = grad[r].astype(F32) * valid[sec[0] * clips + r].astype(F32)
        gin, smalls, g_scale, g_shift = norm_backward(
            acc[rows], normed[rows], inv[rows], small1, r, above, out0[r], shifts
        )
        grad[r] = gin
        sums1[TAPS : TAPS + 8] += smalls
        sums1[pl.ds(SCALE + r, 1)] = g_scale
        sums1[pl.ds(SHIFT + r, 1)] = g_shift
        grad0 = gin.astype(F32)
        low = (grad0 * small0[GAIN : GAIN + 1]).astype(BF16)
        gb[rows] = low
        move(r).start()
        sums0[GAIN : GAIN + 1] += rowsum(grad0 * branch0[rows])
        sums0[DOWNB : DOWNB + 1] += rowsum(low.astype(F32))

    pl.loop(0, clips, unroll=True)(under)
    tiles = []
    for j in range(3):
        activation_tile(j, gb, down0, slope0, sums0)
        tiles.append(pltpu.make_async_copy(slope0.at[j], gpre_hbm.at[j], sems.at[5 + j // 2 * 3, j % 2]))
        tiles[-1].start()
        up_tile(j, ORDERS[0], adapted0, slope0[j], upd0)
    route_block(0, 0, sec, place, upd0, *ends[0], parts.at[0], True)
    for j in range(3):
        down_tile(j, ORDERS[0], gb, act0[j], dnd0)
    route_block(0, 1, sec, place, dnd0, *ends[1], parts.at[0], True)
    route(sec, out0, out1, half_own, out_send, sems.at[4], False)
    for n, source in enumerate((upd, dnd)):
        route_block(1, n, sec, place, source, *ends[n], parts.at[1], False)
    for copy in tiles + [move(r) for r in range(clips)]:
        copy.wait()
    for n, source in enumerate((upd0, dnd0)):
        route_block(0, n, sec, place, source, *ends[n], parts.at[0], False)


def last_body(
    sec, gpre, up_own, up_got, normed, inv, small, grad_out, tokens, sums0, sums1, gin, away, own, send,
    up, shifts, sums, sem,
):
    clip = pl.program_id(0)

    @pl.when(clip == 0)
    def _():
        sums[...] = sums0[...]

        @pl.when(sec[0] == 0)
        def _():
            pltpu.make_async_copy(up_own, up, sem).start()

        @pl.when(sec[0] != 0)
        def _():
            pltpu.make_async_copy(up_got, up, sem).start()

        set_shifts(shifts)
        pltpu.make_async_copy(up_own, up, sem).wait()

    gad = dot(gpre[0], up[:, :TILE], NT)
    for j in range(1, 3):
        gad = gad + dot(gpre[j], up[:, j * TILE : (j + 1) * TILE], NT)
    above = grad_out[0]
    out, smalls, g_scale, g_shift = norm_backward(
        gad, normed[...], inv[...], small, clip, above.astype(F32), tokens[0], shifts
    )
    gin[0] = jnp.where(sec[0] == 0, out, above)
    away[0] = jnp.where(sec[0] == 0, above, out)
    sums[TAPS : TAPS + 8] += smalls
    sums[pl.ds(SCALE + clip, 1)] = g_scale
    sums[pl.ds(SHIFT + clip, 1)] = g_shift

    @pl.when(clip == pl.num_programs(0) - 1)
    def _():
        own[...] = pick(sec[0] == 0, sums[...], sums1[...])
        send[...] = pick(sec[0] == 0, sums1[...], sums[...])


def pick(first, a, b):
    return jnp.where(first, a, b)


def bit_of(spot, step):
    low, high = ORDERS[0][step], ORDERS[1][step]
    return (spot[1] >> (low if low == high else pick(spot[0] == 0, low, high))) & 1


GATHER = (3, 2, 0, 1)


def gather_bit(spot, hop):
    return (spot[1] >> GATHER[hop]) & 1


def gather_slot(spot):
    slot = 0
    for hop in range(len(GATHER)):
        slot = slot + gather_bit(spot, hop) * (1 << hop)
    return slot


def fetch(copies, source, first, rows, target, sem):
    copies.append(pltpu.make_async_copy(source.at[pl.ds(first, rows)], target, sem))
    copies[-1].start()


def pack_body(step, share, sec, place, total0, total1, *refs):
    rows = (8 >> step) * share
    first = pl.multiple_of((1 - bit_of((sec[0], place[0]), step)) * rows, 32)
    if step == 1:
        came, (packet, buffer, sems) = refs[:2], refs[2:]
        copies = []
        for b in range(2):
            fetch(copies, came[b], first, rows, buffer.at[b], sems.at[b])
    else:
        came, packet = refs
    for b, total in enumerate((total0, total1)):
        if step == 1:
            copies[b].wait()
            latest = buffer[b]
        else:
            latest = came[pl.ds(b * 2 * rows + first, rows)]
        packet[b * rows : (b + 1) * rows] = (total[pl.ds(first, rows)] + latest.astype(F32)).astype(BF16)


def share_body(share, total0, total1, came, up, down):
    rows = up.shape[0]
    whole = total0[...] + came[:share].astype(F32)
    for j in range(3):
        up[:, j * TILE : (j + 1) * TILE] = whole[j * rows : (j + 1) * rows]
    down[...] = total1[...] + came[share : 2 * share].astype(F32)


def begin_rows_body(sec, place, speaker, own_sums, got_sums, packet, smalls, held, sems):
    spot = (sec[0], place[0])
    first = spot[0] == 0
    copies = []
    for n, source in enumerate((own_sums, got_sums)):
        fetch(copies, source, 0, SMALL, held.at[n], sems.at[n])
    for copy in copies:
        copy.wait()
    own, other = held[0], held[1]
    low = pick(first, own[SCALE:], other[SCALE:])
    high = pick(first, other[SCALE:], own[SCALE:])
    packet[:16] = jnp.concatenate([low, high], axis=0).astype(BF16)
    lane = lax.broadcasted_iota(jnp.int32, (1, own.shape[1]), 1)
    here = (lane >> 4) == gather_slot(spot)
    which = ((lane >> 3) & 1) * 4 + (lane & 3)
    code = jnp.zeros(lane.shape, jnp.int32)
    for c in range(8):
        code = jnp.where(here & (which == c), speaker[c], code)
    smalls[...] = own[:SCALE] + other[:SCALE]
    smalls[13:14] = (code >> 6).astype(F32)
    smalls[14:15] = (code & 63).astype(F32)
    packet[16:32] = smalls[...].astype(BF16)


def more_rows_body(hop, place, before, after, smalls_in, packet, smalls):
    size = 16 << (hop - 1)
    bit = gather_bit((0, place[0]), hop - 1)
    for source, side in ((before, bit), (after, 1 - bit)):
        packet[pl.ds(pl.multiple_of(side * size, 16), size)] = source[:size]
    smalls[...] = smalls_in[...] + after[size:].astype(F32)
    packet[2 * size :] = smalls[...].astype(BF16)


def tables_body(place, before, after, smalls_in, scale, shift, taps, conv, upb, downb, gain, rows_of):
    size = rows_of.shape[0] // 2
    bit = gather_bit((0, place[0]), len(GATHER) - 1)
    for source, side in ((before, bit), (after, 1 - bit)):
        rows_of[pl.ds(pl.multiple_of(side * size, 16), size)] = source[:size]
    total = smalls_in[...] + after[size:].astype(F32)
    owned = scale.shape[0]
    count = 2 * size
    who = total[13:14, :count] * 64.0 + total[14:15, :count]
    wanted = lax.broadcasted_iota(jnp.int32, (owned, count), 0) + place[0] * owned
    hit = who == wanted.astype(F32)
    kind = (lax.broadcasted_iota(jnp.int32, (owned, count), 1) >> 2) & 1
    for k, out in enumerate((scale, shift)):
        out[...] = dot(jnp.where(hit & (kind == k), 1.0, 0.0).astype(BF16), rows_of[...], NN)
    lanes = total.shape[1] // BLOCKS
    turn = lax.rem(BLOCKS - place[0], BLOCKS)
    cut = pltpu.roll(total, turn * lanes, 1)[:, :lanes]
    for k in range(7):
        taps[k] = cut[k : k + 1]
    conv[...] = cut[CONV : CONV + 1]
    downb[...] = cut[DOWNB : DOWNB + 1]
    gain[...] = cut[GAIN : GAIN + 1]
    line = jnp.concatenate([total[UPB + k : UPB + k + 1] for k in range(3)], axis=1)
    upb[...] = pltpu.roll(line, turn * 3 * lanes, 1)[:, : 3 * lanes]


def struct(shape, dtype):
    return jax.ShapeDtypeStruct(shape, dtype)


def params(limit=None):
    return pltpu.CompilerParams(vmem_limit_bytes=limit * 1024 * 1024 if limit else ALL_VMEM)


def cost(flops, moved):
    return pl.CostEstimate(flops=int(flops), bytes_accessed=int(moved), transcendentals=0)


def local(
    tokens, out_cotangent, speaker, valid, conv_weight, conv_bias, scale_table, shift_table,
    up_weight, up_bias, down_weight, down_bias, layer_scale,
):
    section = lax.axis_index("section").astype(jnp.int32)
    place = lax.axis_index("dp").astype(jnp.int32)
    devices = lax.axis_size("dp")
    clips, frames, width = tokens.shape
    hidden = up_weight.shape[2]
    table_rows = scale_table.shape[1]
    half = clips // 2
    rows = half * frames
    sec = section[None]
    swap = [(0, 1), (1, 0)]

    own_small, other_small = pl.pallas_call(
        prep_body,
        out_shape=[struct((SMALL, width), F32)] * 2,
        in_specs=[SMEM, SMEM] + [VMEM] * 5 + [ANY] * 2,
        out_specs=[VMEM] * 2,
        scratch_shapes=[pltpu.SemaphoreType.DMA((2, 2, half))],
        compiler_params=params(),
        name="prep",
    )(
        sec, speaker, conv_weight.transpose(1, 0, 2), conv_bias, up_bias, down_bias, layer_scale,
        scale_table, shift_table,
    )
    got_small = lax.ppermute(other_small, "section", swap)
    up_own, down_own = up_weight[0], down_weight[0]
    up_got = lax.ppermute(up_own, "section", swap)
    down_got = lax.ppermute(down_own, "section", swap)
    clip_block = (1, frames, width)
    whole_small = pl.BlockSpec((SMALL, width), lambda c, sec: (0, 0))
    half_struct = struct((half, frames, width), BF16)
    whole_struct = struct((clips, frames, width), BF16)
    small_struct = struct((SMALL, width), F32)
    flat_struct = struct((rows, width), BF16)
    tiles = hidden // TILE
    tiled = (tiles, rows, TILE)
    share = hidden // BLOCKS
    gradient = (BLOCKS, share, width)
    gradient_struct = struct(gradient, BF16)
    piece_struct = struct((BLOCKS // 2, share, width), BF16)
    product = 2 * rows * width * hidden

    (
        sums0, sums1, gin1, normed0, inv0, out_own, out_send, gpre0, up_keep,
        down_keep, up_pass, down_pass, up_stay, down_stay, small0,
    ) = pl.pallas_call(
        main_body,
        out_shape=[
            small_struct, small_struct, half_struct, flat_struct, struct((rows, 128), F32),
            whole_struct, half_struct, struct(tiled, BF16), gradient_struct, gradient_struct,
            piece_struct, piece_struct, piece_struct, piece_struct, small_struct,
        ],
        in_specs=[SMEM, SMEM, SMEM, VMEM, VMEM, HBM, HBM, HBM, ANY, HBM, ANY],
        out_specs=[VMEM, VMEM] + [HBM] * 12 + [VMEM],
        scratch_shapes=[
            pltpu.VMEM((width, hidden), BF16),
            pltpu.VMEM((hidden, width), BF16),
            pltpu.VMEM((width, hidden), BF16),
            pltpu.VMEM((hidden, width), BF16),
            pltpu.VMEM(tiled, BF16),
            pltpu.VMEM(tiled, BF16),
            pltpu.VMEM(tiled, BF16),
            pltpu.VMEM(tiled, BF16),
            pltpu.VMEM((rows, width), F32),
            pltpu.VMEM((rows, width), BF16),
            pltpu.VMEM((rows, width), BF16),
            pltpu.VMEM((rows, 128), F32),
            pltpu.VMEM((rows, width), BF16),
            pltpu.VMEM((rows, width), F32),
            pltpu.VMEM((rows, width), BF16),
            pltpu.VMEM((half, frames, width), BF16),
            pltpu.VMEM((half, frames, width), BF16),
            pltpu.VMEM((half, frames, width), BF16),
            pltpu.VMEM((half, frames, width), BF16),
            pltpu.VMEM((SMALL, width), F32),
            pltpu.VMEM((SMALL, width), F32),
            pltpu.VMEM((len(OFFSETS) * frames, frames), BF16),
            pltpu.VMEM(gradient, BF16),
            pltpu.VMEM(gradient, BF16),
            pltpu.VMEM(gradient, BF16),
            pltpu.VMEM(gradient, BF16),
            pltpu.SemaphoreType.DMA((9, 2)),
            pltpu.SemaphoreType.DMA((half,)),
            pltpu.SemaphoreType.DMA((2, 2, 2)),
        ],
        compiler_params=params(),
        cost_estimate=cost(11 * product, 24 << 20),
        name="main",
    )(
        sec, place[None], valid, own_small, got_small, tokens, out_cotangent, up_own, up_got, down_own, down_got
    )
    swapped = []
    for piece in (up_pass, down_pass, up_stay, down_stay):
        swapped.append(lax.ppermute(piece, "section", swap))
    pairs = [[up_keep, swapped[0], swapped[2]], [down_keep, swapped[1], swapped[3]]]
    got_out = lax.ppermute(out_send, "section", swap)

    gin_own, gin_send, own_sums, sums_send = pl.pallas_call(
        last_body,
        grid_spec=pltpu.PrefetchScalarGridSpec(
            num_scalar_prefetch=1,
            grid=(half,),
            in_specs=[
                pl.BlockSpec((tiles, frames, TILE), lambda c, sec: (0, c, 0)),
                HBM,
                ANY,
                pl.BlockSpec((frames, width), lambda c, sec: (c, 0)),
                pl.BlockSpec((frames, 128), lambda c, sec: (c, 0)),
                whole_small,
                pl.BlockSpec(clip_block, lambda c, sec: (c, 0, 0)),
                pl.BlockSpec(clip_block, lambda c, sec: (sec[0] * half + c, 0, 0)),
                whole_small,
                whole_small,
            ],
            out_specs=[
                pl.BlockSpec(clip_block, lambda c, sec: (sec[0] * half + c, 0, 0)),
                pl.BlockSpec(clip_block, lambda c, sec: (c, 0, 0)),
                whole_small,
                whole_small,
            ],
            scratch_shapes=[
                pltpu.VMEM((width, hidden), BF16),
                pltpu.VMEM((len(OFFSETS) * frames, frames), BF16),
                pltpu.VMEM((SMALL, width), F32),
                pltpu.SemaphoreType.DMA,
            ],
        ),
        out_shape=[whole_struct, half_struct, small_struct, small_struct],
        compiler_params=params(),
        cost_estimate=cost(2 * half * product, 12 << 20),
        name="last",
    )(sec, gpre0, up_own, up_got, normed0, inv0, small0, gin1, tokens, sums0, sums1)
    got_gin = lax.ppermute(gin_send, "section", swap)
    got_sums = lax.ppermute(sums_send, "section", swap)

    def joined(whole, got):
        return lax.dynamic_update_slice(whole, got, ((1 - section) * half, 0, 0))[None]

    block_outputs = joined(out_own, got_out)
    input_grads = joined(gin_own, got_gin)
    if devices == BLOCKS:
        outs = halved(sec, place[None], speaker, pairs, own_sums, got_sums, table_rows)
    else:
        outs = scattered(section, place, devices, speaker, pairs, own_sums, got_sums, table_rows)
    return (block_outputs, input_grads) + outs


def exchanged(packet, step):
    devices = lax.axis_size("dp")
    moves = [
        (s * devices + i, s * devices + (i ^ (1 << ORDERS[s][step])))
        for s in range(2)
        for i in range(devices)
    ]
    return lax.ppermute(packet, PAIR, moves)


def halved(sec, place, speaker, pairs, own_sums, got_sums, table_rows):
    _, share, width = pairs[0][0].shape
    pairs = [[piece.reshape(-1, width) for piece in pair] for pair in pairs]
    spot = (sec[0], place[0])
    half_rows = 8 * share

    def part(array, first, count):
        return lax.dynamic_slice_in_dim(array, first, count, 0).astype(F32)

    bit = bit_of(spot, 0)
    latest, totals = [None, None], [None, None]
    for b in (0, 1):
        keep, passed, stays = pairs[b]
        own = lax.optimization_barrier(part(keep, (1 - bit) * half_rows, half_rows))
        packet = (own + passed.astype(F32)).astype(BF16)
        latest[b] = exchanged(packet, 0)
        keep, stays, _ = lax.optimization_barrier((keep, stays, own_sums))
        totals[b] = part(keep, bit * half_rows, half_rows) + stays.astype(F32)

    def small_call(body, outs, scalars, operands, scratch=(), specs=None, limit=8):
        return pl.pallas_call(
            body,
            out_shape=outs,
            in_specs=[SMEM] * len(scalars) + (specs or [VMEM] * len(operands)),
            out_specs=[VMEM] * len(outs),
            scratch_shapes=scratch,
            compiler_params=params(limit),
            cost_estimate=cost(0, 2 << 20),
        )(*scalars, *operands)

    def row_outs(hop):
        return [struct(((16 << hop) + 16, width), BF16), struct((SCALE, width), F32)]

    rows_packet, smalls = small_call(
        begin_rows_body, row_outs(0), [sec, place, speaker],
        [own_sums, got_sums],
        [pltpu.VMEM((2, SMALL, width), F32), pltpu.SemaphoreType.DMA((2,))], [HBM] * 2,
    )
    for hop in range(len(GATHER)):
        more = lax.ppermute(
            rows_packet, "dp", [(i, i ^ (1 << GATHER[hop])) for i in range(BLOCKS)]
        )
        operands = [rows_packet, more, smalls]
        if hop + 1 < len(GATHER):
            rows_packet, smalls = small_call(
                functools.partial(more_rows_body, hop + 1), row_outs(hop + 1), [place],
                operands,
            )
    owned = table_rows // BLOCKS
    lanes = width // BLOCKS
    one = struct((1, lanes), F32)
    scale, shift, taps, conv, upb, downb, gain = small_call(
        tables_body,
        [
            struct((owned, width), F32),
            struct((owned, width), F32),
            struct((7, 1, lanes), F32),
            one,
            struct((1, 3 * lanes), F32),
            one,
            one,
        ],
        [place],
        operands,
        [pltpu.VMEM((16 * BLOCKS, width), BF16)],
    )

    for step in range(1, 4):
        rows = (8 >> step) * share
        first = bit_of(spot, step) * rows
        packet_struct = [struct((2 * rows, width), BF16)]
        if step == 1:
            (packet,) = small_call(
                functools.partial(pack_body, step, share), packet_struct, [sec, place],
                totals + latest,
                [pltpu.VMEM((2, rows, width), BF16), pltpu.SemaphoreType.DMA((2,))],
                [VMEM] * 2 + [ANY] * 2,
            )
        else:
            (packet,) = small_call(
                functools.partial(pack_body, step, share), packet_struct, [sec, place],
                totals + latest[:1],
            )
        got = exchanged(packet, step)
        bases = (0, 0) if step == 1 else (0, 2 * rows)
        totals = [
            part(totals[b], first, rows) + part(latest[b], bases[b] + first, rows) for b in range(2)
        ]
        latest = [got, got]
    up, down = small_call(
        functools.partial(share_body, share),
        [struct((width // BLOCKS, 3 * TILE), F32), struct((share, width), F32)],
        [],
        totals + latest[:1],
    )
    return (
        taps.transpose(1, 0, 2), conv, scale[None], shift[None], up[None], upb, down[None], downb, gain
    )


def scattered(section, place, devices, speaker, pairs, own_sums, got_sums, table_rows):
    first_section = section == 0
    smalls = lax.psum(own_sums[:SCALE] + got_sums[:SCALE], "dp")
    clip_rows = jnp.stack([own_sums[SCALE:], got_sums[SCALE:]])
    clip_rows = pick(first_section, clip_rows, clip_rows[::-1]).astype(BF16)
    clips = speaker.shape[0]
    width = clip_rows.shape[-1]
    clip_rows = clip_rows.reshape(2, 2, clips // 2, width).transpose(1, 0, 2, 3).reshape(2, clips, width)
    gathered = lax.all_gather(clip_rows, "dp", axis=1, tiled=True)
    who = lax.all_gather(speaker, "dp", tiled=True)
    owned = table_rows // devices
    wanted = place * owned + jnp.arange(owned, dtype=jnp.int32)
    chosen = (who[None, :] == wanted[:, None]).astype(BF16)
    tables = [jnp.dot(chosen, gathered[k], preferred_element_type=F32) for k in range(2)]
    low, high = ORDERS[0][0], ORDERS[1][0]
    leaves = 1 - ((place >> pick(first_section, low, high)) & 1)
    natural = []
    for keep, gone, stay in pairs:
        other = pick(leaves == 0, jnp.concatenate([gone, stay]), jnp.concatenate([stay, gone]))
        whole = keep.astype(F32) + other.astype(F32)
        both = [jnp.stack([whole[position(i, order)] for i in range(BLOCKS)]) for order in ORDERS]
        natural.append(pick(first_section, both[0], both[1]))
    _, rows, width = natural[0].shape
    tiles = rows * BLOCKS // TILE
    up = natural[0].reshape(BLOCKS, tiles, rows // tiles, TILE).transpose(0, 2, 1, 3)
    up_share = lax.psum_scatter(up.reshape(width, -1), "dp", scatter_dimension=0, tiled=True)
    down_share = lax.psum_scatter(natural[1].reshape(-1, width), "dp", scatter_dimension=0, tiled=True)
    lanes = width // devices
    own_lanes = lax.dynamic_slice_in_dim(smalls, place * lanes, lanes, 1)
    upb = lax.dynamic_slice_in_dim(smalls[UPB : UPB + 3].reshape(-1), place * 3 * lanes, 3 * lanes, 0)
    return (
        own_lanes[TAPS : TAPS + 7][None],
        own_lanes[CONV : CONV + 1],
        tables[0][None],
        tables[1][None],
        up_share[None],
        upb[None],
        down_share[None],
        own_lanes[DOWNB : DOWNB + 1],
        own_lanes[GAIN : GAIN + 1],
    )


def solution(mesh):
    placed = (
        P("dp", None, None),
        P("dp", None, None),
        P("dp"),
        P("dp"),
        P("section", None, None),
        P("section", None),
        P("section", None, None),
        P("section", None, None),
        P("section", None, None),
        P("section", None),
        P("section", None, None),
        P("section", None),
        P("section", None),
    )

    return jax.shard_map(
        local,
        mesh=mesh,
        in_specs=placed,
        out_specs=(
            P("section", "dp", None, None),
            P("section", "dp", None, None),
            P("section", None, "dp"),
            P("section", "dp"),
            P("section", "dp", None),
            P("section", "dp", None),
            P("section", "dp", None),
            P("section", "dp"),
            P("section", "dp", None),
            P("section", "dp"),
            P("section", "dp"),
        ),
        check_vma=False,
    )
```

```python
import functools

import jax
import jax.numpy as jnp
from jax import lax
from jax.experimental import pallas as pl
from jax.experimental.pallas import tpu as pltpu
from jax.sharding import PartitionSpec as P


F32 = jnp.float32
BF16 = jnp.bfloat16
PAIR = ("section", "dp")
TILE = 512
ALL_VMEM = 67043328
HALF_ROOT = 0.7071067811865476
DENSITY = 0.3989422804014327
BLOCKS = 16
ORDERS = ((0, 1, 2, 3), (2, 0, 1, 3))
ANY = pl.BlockSpec(memory_space=pl.ANY)
HBM = pl.BlockSpec(memory_space=pltpu.HBM)
VMEM = pl.BlockSpec(memory_space=pltpu.VMEM)
SMEM = pl.BlockSpec(memory_space=pltpu.SMEM)

TAPS, CONV, UPB, DOWNB, GAIN, CODE, SCALE, SHIFT, SMALL = 0, 7, 8, 11, 12, 13, 16, 20, 24


def position(block, order):
    place = 0
    for bit in order:
        place = 2 * place + ((block >> bit) & 1)
    return place


def dot(a, b, dims):
    return lax.dot_general(a, b, (dims, ((), ())), preferred_element_type=F32)


NN = ((1,), (0,))
NT = ((1,), (1,))
TN = ((0,), (0,))


OFFSETS = (-3, -2, -1, 1, 2, 3)


def set_shifts(shifts):
    frames = shifts.shape[1]
    row = lax.broadcasted_iota(jnp.int32, (frames, frames), 0)
    col = lax.broadcasted_iota(jnp.int32, (frames, frames), 1)
    for n, offset in enumerate(OFFSETS):
        shifts[n * frames : (n + 1) * frames] = jnp.where(col == row + offset, 1.0, 0.0).astype(BF16)


def shifted(shifts, x, offset):
    frames = x.shape[0]
    n = OFFSETS.index(offset)
    return dot(shifts[n * frames : (n + 1) * frames], x, NN)


def wide(x, width):
    return jnp.concatenate([x] * (width // 128), axis=1)


def rowsum(x):
    return jnp.sum(x, axis=0, keepdims=True)


def normalize(x, small, clip, shifts):
    conv = small[CONV : CONV + 1] + x.astype(F32) * small[3:4]
    for offset in OFFSETS:
        conv = conv + shifted(shifts, x, offset) * small[offset + 3 : offset + 4]
    centred = conv - jnp.mean(conv, axis=-1, keepdims=True)
    inv = lax.rsqrt(jnp.mean(centred * centred, axis=-1, keepdims=True) + 1e-06)
    normed = centred * inv
    scale = small[pl.ds(SCALE + clip, 1)]
    shift = small[pl.ds(SHIFT + clip, 1)]
    adapted = (normed * scale + shift).astype(BF16)
    return adapted, normed.astype(BF16), jnp.broadcast_to(inv, (x.shape[0], 128))


def prep_body(sec, place, speaker, taps, conv, upb, downb, gain, scale_hbm, shift_hbm, own, other, sems):
    width = own.shape[1]
    half = SMALL - SHIFT
    copies = []
    for side, out in enumerate((own, other)):
        first = (sec[0] if side == 0 else 1 - sec[0]) * half
        for clip in range(half):
            row = speaker[first + clip]
            for kind, table in enumerate((scale_hbm, shift_hbm)):
                copies.append(
                    pltpu.make_async_copy(
                        table.at[0, pl.ds(row, 1)],
                        out.at[pl.ds((SCALE, SHIFT)[kind] + clip, 1)],
                        sems.at[side, kind, clip],
                    )
                )
    for copy in copies:
        copy.start()
    for out in (own, other):
        for k in range(7):
            out[TAPS + k : TAPS + k + 1] = taps[k]
        out[CONV : CONV + 1] = conv[...]
        for k in range(DOWNB - UPB):
            out[UPB + k : UPB + k + 1] = upb[:, k * width : (k + 1) * width]
        out[DOWNB : DOWNB + 1] = downb[...]
        out[GAIN : GAIN + 1] = gain[...]
        out[GAIN + 1 : SCALE] = jnp.zeros((SCALE - GAIN - 1, width), F32)
    lane = lax.broadcasted_iota(jnp.int32, (1, width), 1)
    here = (lane >> 4) == gather_slot((sec[0], place[0]))
    which = ((lane >> 3) & 1) * 4 + (lane & 3)
    code = jnp.zeros(lane.shape, jnp.int32)
    for c in range(2 * half):
        code = jnp.where(here & (which == c), speaker[c], code)
    own[CODE : CODE + 1] = (code >> 6).astype(F32)
    own[CODE + 1 : CODE + 2] = (code & 63).astype(F32)
    for copy in copies:
        copy.wait()


def forward_tiles(adapted, up, down, small, act, slope, acc):
    steps = [(j, r) for j in range(3) for r in range(acc.shape[0] // 256)]

    def hidden(j, r):
        part = dot(adapted[r * 256 : (r + 1) * 256], up[:, j * TILE : (j + 1) * TILE], NN)
        return part + small[UPB + j : UPB + j + 1]

    ahead = hidden(*steps[0])
    for n, (j, r) in enumerate(steps):
        rows = slice(r * 256, (r + 1) * 256)
        pre = ahead
        if n + 1 < len(steps):
            ahead = hidden(*steps[n + 1])
        phi = 0.5 * lax.erf(pre * HALF_ROOT) + 0.5
        low = (pre * phi).astype(BF16)
        act[j, rows] = low
        slope[j, rows] = (phi + pre * (DENSITY * jnp.exp(-0.5 * pre * pre))).astype(BF16)
        part = dot(low, down[j * TILE : (j + 1) * TILE], NN)
        acc[rows] = part if j == 0 else acc[rows] + part


def activation_tile(j, gb, down, slope, sums):
    total = jnp.zeros((1, TILE), F32)
    for r in range(gb.shape[0] // 256):
        rows = slice(r * 256, (r + 1) * 256)
        gact = dot(gb[rows], down[j * TILE : (j + 1) * TILE], NT)
        gpre = (gact * slope[j, rows].astype(F32)).astype(BF16)
        slope[j, rows] = gpre
        total = total + rowsum(gpre.astype(F32))
    sums[UPB + j : UPB + j + 1] = total


def down_pieces(j, order):
    share = 3 * TILE // BLOCKS
    at, pieces = j * TILE, []
    while at < (j + 1) * TILE:
        stop = min((at // share + 1) * share, (j + 1) * TILE)
        pieces.append((position(at // share, order), at % share, stop - at, at - j * TILE))
        at = stop
    return pieces


def up_tile(j, order, adapted, gpre, upd):
    gup = dot(adapted[...], gpre, TN).astype(BF16)
    share = TILE // BLOCKS
    for i in range(BLOCKS):
        upd[position(i, order), j * share : (j + 1) * share] = gup[i * share : (i + 1) * share]


def down_tile(j, order, gb, act, dnd):
    gdn = dot(act, gb[...], TN).astype(BF16)
    for block, first, rows, at in down_pieces(j, order):
        dnd[block, first : first + rows] = gdn[at : at + rows]


def norm_backward(gad, normed, inv, small, clip, grad_out, v, shifts):
    n = normed.astype(F32)
    width = n.shape[1]
    scale = small[pl.ds(SCALE + clip, 1)]
    g_shift = rowsum(gad)
    g_scale = rowsum(gad * n)
    gn = gad * scale
    m1 = jnp.mean(gn, axis=-1, keepdims=True)
    m2 = jnp.mean(gn * n, axis=-1, keepdims=True)
    gc = (gn - m1 - n * m2) * wide(inv, width)
    low = gc.astype(BF16)
    total = grad_out + gc * small[3:4]
    v = v.astype(F32)
    g_taps = []
    for k in range(7):
        if k == 3:
            g_taps.append(rowsum(gc * v))
            continue
        moved = shifted(shifts, low, 3 - k)
        total = total + moved * small[k : k + 1]
        g_taps.append(rowsum(moved * v))
    return total.astype(BF16), jnp.concatenate(g_taps + [rowsum(gc)], axis=0), g_scale, g_shift


def place_weights(sec, block, up_own, up_got, down_own, down_got, up, down, sems, start):
    def go(up_from, down_from):
        for source, target, sem in ((up_from, up, sems.at[0]), (down_from, down, sems.at[1])):
            copy = pltpu.make_async_copy(source, target, sem)
            copy.start() if start else copy.wait()

    if not start:
        go(up_own, down_own)
        return

    @pl.when(sec[0] == block)
    def _():
        go(up_own, down_own)

    @pl.when(sec[0] != block)
    def _():
        go(up_got, down_got)


def leaving(block, place):
    return 1 - ((place[0] >> ORDERS[block][0]) & 1)


def route_block(block, layer, sec, place, sums, kept, passed, stays, sems, start):
    half = BLOCKS // 2
    goes = leaving(block, place)

    def go(*targets):
        for side, (target, first) in enumerate(zip(targets, (goes, 1 - goes))):
            part = sums.at[pl.ds(first * half, half)]
            copy = pltpu.make_async_copy(part, target, sems.at[layer, side])
            copy.start() if start else copy.wait()

    if not start:
        go(passed, stays)
        return

    @pl.when(sec[0] == block)
    def _():
        go(kept.at[pl.ds(goes * half, half)], kept.at[pl.ds((1 - goes) * half, half)])

    @pl.when(sec[0] != block)
    def _():
        go(passed, stays)


def route(sec, upd, dnd, keep, send, sems, start):
    def go(kept, sent):
        for source, target, sem in ((kept, keep, sems.at[0]), (sent, send, sems.at[1])):
            copy = pltpu.make_async_copy(source, target, sem)
            copy.start() if start else copy.wait()

    if not start:
        go(upd, dnd)
        return

    @pl.when(sec[0] == 0)
    def _():
        go(upd, dnd)

    @pl.when(sec[0] != 0)
    def _():
        go(dnd, upd)


def main_body(
    sec, place, valid, own_small, got_small, tokens, cot, up_own, up_got, down_own, down_got,
    sums0, sums1, gin1, normed_hbm, inv_hbm, out_own, out_send, gpre_hbm, up_keep, down_keep,
    up_pass, down_pass, up_stay, down_stay, small0_out,
    up0, down0, up1, down1, act0, slope0, act1, slope1, acc, adapted0, normed, inv, adapted1, branch0,
    gb, v, grad, out0, out1, small0, small1, shifts, upd, dnd, upd0, dnd0, sems, pieces, parts,
):
    clips = acc.shape[0] // 256
    mine = pl.ds(sec[0] * clips, clips)
    loads = (
        pltpu.make_async_copy(tokens.at[mine], v, sems.at[6, 0]),
        pltpu.make_async_copy(cot.at[mine], grad, sems.at[6, 1]),
    )
    loads[0].start()
    weights = (up_own, up_got, down_own, down_got)
    place_weights(sec, 0, *weights, up0, down0, sems.at[0], True)
    place_weights(sec, 1, *weights, up1, down1, sems.at[1], True)
    loads[1].start()
    first = sec[0] == 0
    small0[...] = pick(first, own_small[...], got_small[...])
    small1[...] = pick(first, got_small[...], own_small[...])
    small0_out[...] = small0[...]
    sums0[...] = jnp.zeros_like(sums0)
    sums1[...] = jnp.zeros_like(sums1)
    set_shifts(shifts)
    loads[0].wait()

    def begin(r):
        rows = pl.ds(pl.multiple_of(r * 256, 256), 256)
        adapted0[rows], normed[rows], inv[rows] = normalize(v[r], small0, r, shifts)

    pl.loop(0, clips, unroll=True)(begin)
    saves = [
        pltpu.make_async_copy(source, target, sems.at[7 + n // 2, n % 2])
        for n, (source, target) in enumerate(
            ((normed, normed_hbm), (inv, inv_hbm))
        )
    ]
    for copy in saves:
        copy.start()
    place_weights(sec, 0, *weights, up0, down0, sems.at[0], False)
    forward_tiles(adapted0, up0, down0, small0, act0, slope0, acc)
    for copy in saves:
        copy.wait()

    def between(r):
        rows = pl.ds(pl.multiple_of(r * 256, 256), 256)
        branch = acc[rows] + small0[DOWNB : DOWNB + 1]
        branch0[rows] = branch
        result = (v[r].astype(F32) + small0[GAIN : GAIN + 1] * branch).astype(BF16)
        out0[r] = result
        adapted1[rows], normed[rows], inv[rows] = normalize(result, small1, r, shifts)

    pl.loop(0, clips, unroll=True)(between)
    place_weights(sec, 1, *weights, up1, down1, sems.at[1], False)
    forward_tiles(adapted1, up1, down1, small1, act1, slope1, acc)
    loads[1].wait()

    def top(r):
        rows = pl.ds(pl.multiple_of(r * 256, 256), 256)
        branch = acc[rows] + small1[DOWNB : DOWNB + 1]
        gain = small1[GAIN : GAIN + 1]
        out1[r] = (out0[r].astype(F32) + gain * branch).astype(BF16)
        above = grad[r].astype(F32) * valid[sec[0] * clips + r].astype(F32)
        low = (above * gain).astype(BF16)
        gb[rows] = low
        sums1[GAIN : GAIN + 1] += rowsum(above * branch)
        sums1[DOWNB : DOWNB + 1] += rowsum(low.astype(F32))

    pl.loop(0, clips)(top)
    half_own = out_own.at[mine]
    route(sec, out0, out1, half_own, out_send, sems.at[4], True)
    for j in range(3):
        activation_tile(j, gb, down1, slope1, sums1)
        for r in range(clips):
            rows = slice(r * 256, (r + 1) * 256)
            part = dot(slope1[j, rows], up1[:, j * TILE : (j + 1) * TILE], NT)
            acc[rows] = part if j == 0 else acc[rows] + part
        up_tile(j, ORDERS[1], adapted1, slope1[j], upd)
        down_tile(j, ORDERS[1], gb, act1[j], dnd)
    ends = ((up_keep, up_pass, up_stay), (down_keep, down_pass, down_stay))
    for n, source in enumerate((upd, dnd)):
        route_block(1, n, sec, place, source, *ends[n], parts.at[1], True)

    def move(r):
        return pltpu.make_async_copy(grad.at[r], gin1.at[r], pieces.at[r])

    def under(r):
        rows = pl.ds(pl.multiple_of(r * 256, 256), 256)
        above = grad[r].astype(F32) * valid[sec[0] * clips + r].astype(F32)
        gin, smalls, g_scale, g_shift = norm_backward(
            acc[rows], normed[rows], inv[rows], small1, r, above, out0[r], shifts
        )
        grad[r] = gin
        sums1[TAPS : TAPS + 8] += smalls
        sums1[pl.ds(SCALE + r, 1)] = g_scale
        sums1[pl.ds(SHIFT + r, 1)] = g_shift
        grad0 = gin.astype(F32)
        low = (grad0 * small0[GAIN : GAIN + 1]).astype(BF16)
        gb[rows] = low
        move(r).start()
        sums0[GAIN : GAIN + 1] += rowsum(grad0 * branch0[rows])
        sums0[DOWNB : DOWNB + 1] += rowsum(low.astype(F32))

    pl.loop(0, clips, unroll=True)(under)
    tiles = []
    for j in range(3):
        activation_tile(j, gb, down0, slope0, sums0)
        tiles.append(pltpu.make_async_copy(slope0.at[j], gpre_hbm.at[j], sems.at[5 + j // 2 * 3, j % 2]))
        tiles[-1].start()
        up_tile(j, ORDERS[0], adapted0, slope0[j], upd0)
    route_block(0, 0, sec, place, upd0, *ends[0], parts.at[0], True)
    for j in range(3):
        down_tile(j, ORDERS[0], gb, act0[j], dnd0)
    route_block(0, 1, sec, place, dnd0, *ends[1], parts.at[0], True)
    route(sec, out0, out1, half_own, out_send, sems.at[4], False)
    for n, source in enumerate((upd, dnd)):
        route_block(1, n, sec, place, source, *ends[n], parts.at[1], False)
    for copy in tiles + [move(r) for r in range(clips)]:
        copy.wait()
    for n, source in enumerate((upd0, dnd0)):
        route_block(0, n, sec, place, source, *ends[n], parts.at[0], False)


def last_body(
    sec, gpre, up_own, up_got, normed, inv, small, grad_out, tokens, sums0, sums1, own_small, gin, away, own,
    send,
    up, shifts, sums, sem,
):
    clip = pl.program_id(0)

    @pl.when(clip == 0)
    def _():
        sums[...] = sums0[...]

        @pl.when(sec[0] == 0)
        def _():
            pltpu.make_async_copy(up_own, up, sem).start()

        @pl.when(sec[0] != 0)
        def _():
            pltpu.make_async_copy(up_got, up, sem).start()

        set_shifts(shifts)
        pltpu.make_async_copy(up_own, up, sem).wait()

    gad = dot(gpre[0], up[:, :TILE], NT)
    for j in range(1, 3):
        gad = gad + dot(gpre[j], up[:, j * TILE : (j + 1) * TILE], NT)
    above = grad_out[0]
    out, smalls, g_scale, g_shift = norm_backward(
        gad, normed[...], inv[...], small, clip, above.astype(F32), tokens[0], shifts
    )
    gin[0] = jnp.where(sec[0] == 0, out, above)
    away[0] = jnp.where(sec[0] == 0, above, out)
    sums[TAPS : TAPS + 8] += smalls
    sums[pl.ds(SCALE + clip, 1)] = g_scale
    sums[pl.ds(SHIFT + clip, 1)] = g_shift

    @pl.when(clip == pl.num_programs(0) - 1)
    def _():
        own[...] = pick(sec[0] == 0, sums[...], sums1[...])
        own[CODE : CODE + 2] = own_small[CODE : CODE + 2]
        send[...] = pick(sec[0] == 0, sums1[...], sums[...])


def pick(first, a, b):
    return jnp.where(first, a, b)


def bit_of(spot, step):
    low, high = ORDERS[0][step], ORDERS[1][step]
    return (spot[1] >> (low if low == high else pick(spot[0] == 0, low, high))) & 1


GATHER = (3, 2, 0, 1)


def gather_bit(spot, hop):
    return (spot[1] >> GATHER[hop]) & 1


def gather_slot(spot):
    slot = 0
    for hop in range(len(GATHER)):
        slot = slot + gather_bit(spot, hop) * (1 << hop)
    return slot


def fetch(copies, source, first, rows, target, sem):
    copies.append(pltpu.make_async_copy(source.at[pl.ds(first, rows)], target, sem))
    copies[-1].start()


def pack_body(step, share, sec, place, total0, total1, *refs):
    rows = (8 >> step) * share
    first = pl.multiple_of((1 - bit_of((sec[0], place[0]), step)) * rows, 32)
    if step == 1:
        came, (packet, buffer, sems) = refs[:2], refs[2:]
        copies = []
        for b in range(2):
            fetch(copies, came[b], first, rows, buffer.at[b], sems.at[b])
    else:
        came, packet = refs
    for b, total in enumerate((total0, total1)):
        if step == 1:
            copies[b].wait()
            latest = buffer[b]
        else:
            latest = came[pl.ds(b * 2 * rows + first, rows)]
        packet[b * rows : (b + 1) * rows] = (total[pl.ds(first, rows)] + latest.astype(F32)).astype(BF16)


def share_body(share, total0, total1, came, up, down):
    rows = up.shape[0]
    whole = total0[...] + came[:share].astype(F32)
    for j in range(3):
        up[:, j * TILE : (j + 1) * TILE] = whole[j * rows : (j + 1) * rows]
    down[...] = total1[...] + came[share : 2 * share].astype(F32)


def begin_rows_body(sec, own, got, packet, smalls):
    first = sec[0] == 0
    low = pick(first, own[SCALE:], got[SCALE:])
    high = pick(first, got[SCALE:], own[SCALE:])
    packet[:16] = jnp.concatenate([low, high], axis=0).astype(BF16)
    smalls[...] = own[:SCALE] + got[:SCALE]
    packet[16:32] = smalls[...].astype(BF16)


def more_rows_body(hop, place, before, after, smalls_in, packet, smalls):
    size = 16 << (hop - 1)
    bit = gather_bit((0, place[0]), hop - 1)
    for source, side in ((before, bit), (after, 1 - bit)):
        packet[pl.ds(pl.multiple_of(side * size, 16), size)] = source[:size]
    smalls[...] = smalls_in[...] + after[size:].astype(F32)
    packet[2 * size :] = smalls[...].astype(BF16)


def tables_body(place, before, after, smalls_in, scale, shift, taps, conv, upb, downb, gain, rows_of):
    size = rows_of.shape[0] // 2
    bit = gather_bit((0, place[0]), len(GATHER) - 1)
    for source, side in ((before, bit), (after, 1 - bit)):
        rows_of[pl.ds(pl.multiple_of(side * size, 16), size)] = source[:size]
    total = smalls_in[...] + after[size:].astype(F32)
    owned = scale.shape[0]
    count = 2 * size
    who = total[CODE : CODE + 1, :count] * 64.0 + total[CODE + 1 : CODE + 2, :count]
    wanted = lax.broadcasted_iota(jnp.int32, (owned, count), 0) + place[0] * owned
    hit = who == wanted.astype(F32)
    kind = (lax.broadcasted_iota(jnp.int32, (owned, count), 1) >> 2) & 1
    for k, out in enumerate((scale, shift)):
        out[...] = dot(jnp.where(hit & (kind == k), 1.0, 0.0).astype(BF16), rows_of[...], NN)
    lanes = total.shape[1] // BLOCKS
    turn = lax.rem(BLOCKS - place[0], BLOCKS)
    cut = pltpu.roll(total, turn * lanes, 1)[:, :lanes]
    for k in range(7):
        taps[k] = cut[k : k + 1]
    conv[...] = cut[CONV : CONV + 1]
    downb[...] = cut[DOWNB : DOWNB + 1]
    gain[...] = cut[GAIN : GAIN + 1]
    line = jnp.concatenate([total[UPB + k : UPB + k + 1] for k in range(3)], axis=1)
    upb[...] = pltpu.roll(line, turn * 3 * lanes, 1)[:, : 3 * lanes]


def struct(shape, dtype):
    return jax.ShapeDtypeStruct(shape, dtype)


def params(limit=None):
    return pltpu.CompilerParams(vmem_limit_bytes=limit * 1024 * 1024 if limit else ALL_VMEM)


def cost(flops, moved):
    return pl.CostEstimate(flops=int(flops), bytes_accessed=int(moved), transcendentals=0)


def local(
    tokens, out_cotangent, speaker, valid, conv_weight, conv_bias, scale_table, shift_table,
    up_weight, up_bias, down_weight, down_bias, layer_scale,
):
    section = lax.axis_index("section").astype(jnp.int32)
    place = lax.axis_index("dp").astype(jnp.int32)
    devices = lax.axis_size("dp")
    clips, frames, width = tokens.shape
    hidden = up_weight.shape[2]
    table_rows = scale_table.shape[1]
    half = clips // 2
    rows = half * frames
    sec = section[None]
    swap = [(0, 1), (1, 0)]

    own_small, other_small = pl.pallas_call(
        prep_body,
        out_shape=[struct((SMALL, width), F32)] * 2,
        in_specs=[SMEM, SMEM, SMEM] + [VMEM] * 5 + [ANY] * 2,
        out_specs=[VMEM] * 2,
        scratch_shapes=[pltpu.SemaphoreType.DMA((2, 2, half))],
        compiler_params=params(),
        name="prep",
    )(
        sec, place[None], speaker, conv_weight.transpose(1, 0, 2), conv_bias, up_bias, down_bias, layer_scale,
        scale_table, shift_table,
    )
    got_small = lax.ppermute(other_small, "section", swap)
    up_own, down_own = up_weight[0], down_weight[0]
    up_got = lax.ppermute(up_own, "section", swap)
    down_got = lax.ppermute(down_own, "section", swap)
    clip_block = (1, frames, width)
    whole_small = pl.BlockSpec((SMALL, width), lambda c, sec: (0, 0))
    half_struct = struct((half, frames, width), BF16)
    whole_struct = struct((clips, frames, width), BF16)
    small_struct = struct((SMALL, width), F32)
    flat_struct = struct((rows, width), BF16)
    tiles = hidden // TILE
    tiled = (tiles, rows, TILE)
    share = hidden // BLOCKS
    gradient = (BLOCKS, share, width)
    gradient_struct = struct(gradient, BF16)
    piece_struct = struct((BLOCKS // 2, share, width), BF16)
    product = 2 * rows * width * hidden

    (
        sums0, sums1, gin1, normed0, inv0, out_own, out_send, gpre0, up_keep,
        down_keep, up_pass, down_pass, up_stay, down_stay, small0,
    ) = pl.pallas_call(
        main_body,
        out_shape=[
            small_struct, small_struct, half_struct, flat_struct, struct((rows, 128), F32),
            whole_struct, half_struct, struct(tiled, BF16), gradient_struct, gradient_struct,
            piece_struct, piece_struct, piece_struct, piece_struct, small_struct,
        ],
        in_specs=[SMEM, SMEM, SMEM, VMEM, VMEM, HBM, HBM, HBM, ANY, HBM, ANY],
        out_specs=[VMEM, VMEM] + [HBM] * 12 + [VMEM],
        scratch_shapes=[
            pltpu.VMEM((width, hidden), BF16),
            pltpu.VMEM((hidden, width), BF16),
            pltpu.VMEM((width, hidden), BF16),
            pltpu.VMEM((hidden, width), BF16),
            pltpu.VMEM(tiled, BF16),
            pltpu.VMEM(tiled, BF16),
            pltpu.VMEM(tiled, BF16),
            pltpu.VMEM(tiled, BF16),
            pltpu.VMEM((rows, width), F32),
            pltpu.VMEM((rows, width), BF16),
            pltpu.VMEM((rows, width), BF16),
            pltpu.VMEM((rows, 128), F32),
            pltpu.VMEM((rows, width), BF16),
            pltpu.VMEM((rows, width), F32),
            pltpu.VMEM((rows, width), BF16),
            pltpu.VMEM((half, frames, width), BF16),
            pltpu.VMEM((half, frames, width), BF16),
            pltpu.VMEM((half, frames, width), BF16),
            pltpu.VMEM((half, frames, width), BF16),
            pltpu.VMEM((SMALL, width), F32),
            pltpu.VMEM((SMALL, width), F32),
            pltpu.VMEM((len(OFFSETS) * frames, frames), BF16),
            pltpu.VMEM(gradient, BF16),
            pltpu.VMEM(gradient, BF16),
            pltpu.VMEM(gradient, BF16),
            pltpu.VMEM(gradient, BF16),
            pltpu.SemaphoreType.DMA((9, 2)),
            pltpu.SemaphoreType.DMA((half,)),
            pltpu.SemaphoreType.DMA((2, 2, 2)),
        ],
        compiler_params=params(),
        cost_estimate=cost(11 * product, 24 << 20),
        name="main",
    )(
        sec, place[None], valid, own_small, got_small, tokens, out_cotangent, up_own, up_got, down_own, down_got
    )
    swapped = []
    for piece in (up_pass, down_pass, up_stay, down_stay):
        swapped.append(lax.ppermute(piece, "section", swap))
    pairs = [[up_keep, swapped[0], swapped[2]], [down_keep, swapped[1], swapped[3]]]
    got_out = lax.ppermute(out_send, "section", swap)

    gin_own, gin_send, own_sums, sums_send = pl.pallas_call(
        last_body,
        grid_spec=pltpu.PrefetchScalarGridSpec(
            num_scalar_prefetch=1,
            grid=(half,),
            in_specs=[
                pl.BlockSpec((tiles, frames, TILE), lambda c, sec: (0, c, 0)),
                HBM,
                ANY,
                pl.BlockSpec((frames, width), lambda c, sec: (c, 0)),
                pl.BlockSpec((frames, 128), lambda c, sec: (c, 0)),
                whole_small,
                pl.BlockSpec(clip_block, lambda c, sec: (c, 0, 0)),
                pl.BlockSpec(clip_block, lambda c, sec: (sec[0] * half + c, 0, 0)),
                whole_small,
                whole_small,
                whole_small,
            ],
            out_specs=[
                pl.BlockSpec(clip_block, lambda c, sec: (sec[0] * half + c, 0, 0)),
                pl.BlockSpec(clip_block, lambda c, sec: (c, 0, 0)),
                whole_small,
                whole_small,
            ],
            scratch_shapes=[
                pltpu.VMEM((width, hidden), BF16),
                pltpu.VMEM((len(OFFSETS) * frames, frames), BF16),
                pltpu.VMEM((SMALL, width), F32),
                pltpu.SemaphoreType.DMA,
            ],
        ),
        out_shape=[whole_struct, half_struct, small_struct, small_struct],
        compiler_params=params(),
        cost_estimate=cost(2 * half * product, 12 << 20),
        name="last",
    )(sec, gpre0, up_own, up_got, normed0, inv0, small0, gin1, tokens, sums0, sums1, own_small)
    got_gin = lax.ppermute(gin_send, "section", swap)
    got_sums = lax.ppermute(sums_send, "section", swap)

    def joined(whole, got):
        return lax.dynamic_update_slice(whole, got, ((1 - section) * half, 0, 0))[None]

    block_outputs = joined(out_own, got_out)
    input_grads = joined(gin_own, got_gin)
    if devices == BLOCKS:
        outs = halved(sec, place[None], pairs, own_sums, got_sums, table_rows)
    else:
        outs = scattered(section, place, devices, speaker, pairs, own_sums, got_sums, table_rows)
    return (block_outputs, input_grads) + outs


def exchanged(packet, step):
    devices = lax.axis_size("dp")
    moves = [
        (s * devices + i, s * devices + (i ^ (1 << ORDERS[s][step])))
        for s in range(2)
        for i in range(devices)
    ]
    return lax.ppermute(packet, PAIR, moves)


def halved(sec, place, pairs, own_sums, got_sums, table_rows):
    _, share, width = pairs[0][0].shape
    pairs = [[piece.reshape(-1, width) for piece in pair] for pair in pairs]
    spot = (sec[0], place[0])
    half_rows = 8 * share

    def part(array, first, count):
        return lax.dynamic_slice_in_dim(array, first, count, 0).astype(F32)

    bit = bit_of(spot, 0)
    latest, totals = [None, None], [None, None]
    for b in (0, 1):
        keep, passed, stays = pairs[b]
        own = lax.optimization_barrier(part(keep, (1 - bit) * half_rows, half_rows))
        packet = (own + passed.astype(F32)).astype(BF16)
        latest[b] = exchanged(packet, 0)
        keep, stays, _ = lax.optimization_barrier((keep, stays, own_sums))
        totals[b] = part(keep, bit * half_rows, half_rows) + stays.astype(F32)

    def small_call(body, outs, scalars, operands, scratch=(), specs=None, limit=8):
        return pl.pallas_call(
            body,
            out_shape=outs,
            in_specs=[SMEM] * len(scalars) + (specs or [VMEM] * len(operands)),
            out_specs=[VMEM] * len(outs),
            scratch_shapes=scratch,
            compiler_params=params(limit),
            cost_estimate=cost(0, 2 << 20),
        )(*scalars, *operands)

    def row_outs(hop):
        return [struct(((16 << hop) + 16, width), BF16), struct((SCALE, width), F32)]

    rows_packet, smalls = small_call(begin_rows_body, row_outs(0), [sec], [own_sums, got_sums], limit=None)
    for hop in range(len(GATHER)):
        more = lax.ppermute(
            rows_packet, "dp", [(i, i ^ (1 << GATHER[hop])) for i in range(BLOCKS)]
        )
        operands = [rows_packet, more, smalls]
        if hop + 1 < len(GATHER):
            rows_packet, smalls = small_call(
                functools.partial(more_rows_body, hop + 1), row_outs(hop + 1), [place],
                operands,
            )
    owned = table_rows // BLOCKS
    lanes = width // BLOCKS
    one = struct((1, lanes), F32)
    scale, shift, taps, conv, upb, downb, gain = small_call(
        tables_body,
        [
            struct((owned, width), F32),
            struct((owned, width), F32),
            struct((7, 1, lanes), F32),
            one,
            struct((1, 3 * lanes), F32),
            one,
            one,
        ],
        [place],
        operands,
        [pltpu.VMEM((16 * BLOCKS, width), BF16)],
    )

    for step in range(1, 4):
        rows = (8 >> step) * share
        first = bit_of(spot, step) * rows
        packet_struct = [struct((2 * rows, width), BF16)]
        if step == 1:
            (packet,) = small_call(
                functools.partial(pack_body, step, share), packet_struct, [sec, place],
                totals + latest,
                [pltpu.VMEM((2, rows, width), BF16), pltpu.SemaphoreType.DMA((2,))],
                [VMEM] * 2 + [ANY] * 2,
            )
        else:
            (packet,) = small_call(
                functools.partial(pack_body, step, share), packet_struct, [sec, place],
                totals + latest[:1],
            )
        got = exchanged(packet, step)
        bases = (0, 0) if step == 1 else (0, 2 * rows)
        totals = [
            part(totals[b], first, rows) + part(latest[b], bases[b] + first, rows) for b in range(2)
        ]
        latest = [got, got]
    up, down = small_call(
        functools.partial(share_body, share),
        [struct((width // BLOCKS, 3 * TILE), F32), struct((share, width), F32)],
        [],
        totals + latest[:1],
    )
    return (
        taps.transpose(1, 0, 2), conv, scale[None], shift[None], up[None], upb, down[None], downb, gain
    )


def scattered(section, place, devices, speaker, pairs, own_sums, got_sums, table_rows):
    first_section = section == 0
    smalls = lax.psum(own_sums[:SCALE] + got_sums[:SCALE], "dp")
    clip_rows = jnp.stack([own_sums[SCALE:], got_sums[SCALE:]])
    clip_rows = pick(first_section, clip_rows, clip_rows[::-1]).astype(BF16)
    clips = speaker.shape[0]
    width = clip_rows.shape[-1]
    clip_rows = clip_rows.reshape(2, 2, clips // 2, width).transpose(1, 0, 2, 3).reshape(2, clips, width)
    gathered = lax.all_gather(clip_rows, "dp", axis=1, tiled=True)
    who = lax.all_gather(speaker, "dp", tiled=True)
    owned = table_rows // devices
    wanted = place * owned + jnp.arange(owned, dtype=jnp.int32)
    chosen = (who[None, :] == wanted[:, None]).astype(BF16)
    tables = [jnp.dot(chosen, gathered[k], preferred_element_type=F32) for k in range(2)]
    low, high = ORDERS[0][0], ORDERS[1][0]
    leaves = 1 - ((place >> pick(first_section, low, high)) & 1)
    natural = []
    for keep, gone, stay in pairs:
        other = pick(leaves == 0, jnp.concatenate([gone, stay]), jnp.concatenate([stay, gone]))
        whole = keep.astype(F32) + other.astype(F32)
        both = [jnp.stack([whole[position(i, order)] for i in range(BLOCKS)]) for order in ORDERS]
        natural.append(pick(first_section, both[0], both[1]))
    _, rows, width = natural[0].shape
    tiles = rows * BLOCKS // TILE
    up = natural[0].reshape(BLOCKS, tiles, rows // tiles, TILE).transpose(0, 2, 1, 3)
    up_share = lax.psum_scatter(up.reshape(width, -1), "dp", scatter_dimension=0, tiled=True)
    down_share = lax.psum_scatter(natural[1].reshape(-1, width), "dp", scatter_dimension=0, tiled=True)
    lanes = width // devices
    own_lanes = lax.dynamic_slice_in_dim(smalls, place * lanes, lanes, 1)
    upb = lax.dynamic_slice_in_dim(smalls[UPB : UPB + 3].reshape(-1), place * 3 * lanes, 3 * lanes, 0)
    return (
        own_lanes[TAPS : TAPS + 7][None],
        own_lanes[CONV : CONV + 1],
        tables[0][None],
        tables[1][None],
        up_share[None],
        upb[None],
        down_share[None],
        own_lanes[DOWNB : DOWNB + 1],
        own_lanes[GAIN : GAIN + 1],
    )


def solution(mesh):
    placed = (
        P("dp", None, None),
        P("dp", None, None),
        P("dp"),
        P("dp"),
        P("section", None, None),
        P("section", None),
        P("section", None, None),
        P("section", None, None),
        P("section", None, None),
        P("section", None),
        P("section", None, None),
        P("section", None),
        P("section", None),
    )

    return jax.shard_map(
        local,
        mesh=mesh,
        in_specs=placed,
        out_specs=(
            P("section", "dp", None, None),
            P("section", "dp", None, None),
            P("section", None, "dp"),
            P("section", "dp"),
            P("section", "dp", None),
            P("section", "dp", None),
            P("section", "dp", None),
            P("section", "dp"),
            P("section", "dp", None),
            P("section", "dp"),
            P("section", "dp"),
        ),
        check_vma=False,
    )
```

```python
import functools

import jax
import jax.numpy as jnp
from jax import lax
from jax.experimental import pallas as pl
from jax.experimental.pallas import tpu as pltpu
from jax.sharding import PartitionSpec as P


F32 = jnp.float32
BF16 = jnp.bfloat16
PAIR = ("section", "dp")
TILE = 512
ALL_VMEM = 67043328
HALF_ROOT = 0.7071067811865476
DENSITY = 0.3989422804014327
BLOCKS = 16
ORDERS = ((0, 1, 2, 3), (2, 0, 1, 3))
ANY = pl.BlockSpec(memory_space=pl.ANY)
HBM = pl.BlockSpec(memory_space=pltpu.HBM)
VMEM = pl.BlockSpec(memory_space=pltpu.VMEM)
SMEM = pl.BlockSpec(memory_space=pltpu.SMEM)

TAPS, CONV, UPB, DOWNB, GAIN, CODE, SCALE, SHIFT, SMALL = 0, 7, 8, 11, 12, 13, 16, 20, 24


def position(block, order):
    place = 0
    for bit in order:
        place = 2 * place + ((block >> bit) & 1)
    return place


def dot(a, b, dims):
    return lax.dot_general(a, b, (dims, ((), ())), preferred_element_type=F32)


NN = ((1,), (0,))
NT = ((1,), (1,))
TN = ((0,), (0,))


OFFSETS = (-3, -2, -1, 1, 2, 3)


def set_shifts(shifts):
    frames = shifts.shape[1]
    row = lax.broadcasted_iota(jnp.int32, (frames, frames), 0)
    col = lax.broadcasted_iota(jnp.int32, (frames, frames), 1)
    for n, offset in enumerate(OFFSETS):
        shifts[n * frames : (n + 1) * frames] = jnp.where(col == row + offset, 1.0, 0.0).astype(BF16)


def shifted(shifts, x, offset):
    frames = x.shape[0]
    n = OFFSETS.index(offset)
    return dot(shifts[n * frames : (n + 1) * frames], x, NN)


def wide(x, width):
    return jnp.concatenate([x] * (width // 128), axis=1)


def rowsum(x):
    return jnp.sum(x, axis=0, keepdims=True)


def normalize(x, small, clip, shifts):
    conv = small[CONV : CONV + 1] + x.astype(F32) * small[3:4]
    for offset in OFFSETS:
        conv = conv + shifted(shifts, x, offset) * small[offset + 3 : offset + 4]
    centred = conv - jnp.mean(conv, axis=-1, keepdims=True)
    inv = lax.rsqrt(jnp.mean(centred * centred, axis=-1, keepdims=True) + 1e-06)
    normed = centred * inv
    scale = small[pl.ds(SCALE + clip, 1)]
    shift = small[pl.ds(SHIFT + clip, 1)]
    adapted = (normed * scale + shift).astype(BF16)
    return adapted, normed.astype(BF16), jnp.broadcast_to(inv, (x.shape[0], 128))


def prep_body(sec, place, speaker, taps, conv, upb, downb, gain, scale_hbm, shift_hbm, own, other, sems):
    width = own.shape[1]
    half = SMALL - SHIFT
    copies = []
    for side, out in enumerate((own, other)):
        first = (sec[0] if side == 0 else 1 - sec[0]) * half
        for clip in range(half):
            row = speaker[first + clip]
            for kind, table in enumerate((scale_hbm, shift_hbm)):
                copies.append(
                    pltpu.make_async_copy(
                        table.at[0, pl.ds(row, 1)],
                        out.at[pl.ds((SCALE, SHIFT)[kind] + clip, 1)],
                        sems.at[side, kind, clip],
                    )
                )
    for copy in copies:
        copy.start()
    for out in (own, other):
        for k in range(7):
            out[TAPS + k : TAPS + k + 1] = taps[k]
        out[CONV : CONV + 1] = conv[...]
        for k in range(DOWNB - UPB):
            out[UPB + k : UPB + k + 1] = upb[:, k * width : (k + 1) * width]
        out[DOWNB : DOWNB + 1] = downb[...]
        out[GAIN : GAIN + 1] = gain[...]
        out[GAIN + 1 : SCALE] = jnp.zeros((SCALE - GAIN - 1, width), F32)
    lane = lax.broadcasted_iota(jnp.int32, (1, width), 1)
    here = (lane >> 4) == gather_slot((sec[0], place[0]))
    which = ((lane >> 3) & 1) * 4 + (lane & 3)
    code = jnp.zeros(lane.shape, jnp.int32)
    for c in range(2 * half):
        code = jnp.where(here & (which == c), speaker[c], code)
    own[CODE : CODE + 1] = (code >> 6).astype(F32)
    own[CODE + 1 : CODE + 2] = (code & 63).astype(F32)
    for copy in copies:
        copy.wait()


def forward_tiles(adapted, up, down, small, act, slope, acc, before=None, after=None):
    steps = [(j, r) for j in range(3) for r in range(acc.shape[0] // 256)]

    def hidden(j, r):
        if j == 0 and before is not None:
            before(r)
        part = dot(adapted[r * 256 : (r + 1) * 256], up[:, j * TILE : (j + 1) * TILE], NN)
        return part + small[UPB + j : UPB + j + 1]

    ahead = hidden(*steps[0])
    for n, (j, r) in enumerate(steps):
        rows = slice(r * 256, (r + 1) * 256)
        pre = ahead
        if n + 1 < len(steps):
            ahead = hidden(*steps[n + 1])
        phi = 0.5 * lax.erf(pre * HALF_ROOT) + 0.5
        low = (pre * phi).astype(BF16)
        act[j, rows] = low
        slope[j, rows] = (phi + pre * (DENSITY * jnp.exp(-0.5 * pre * pre))).astype(BF16)
        part = dot(low, down[j * TILE : (j + 1) * TILE], NN)
        acc[rows] = part if j == 0 else acc[rows] + part
        if j == 2 and after is not None:
            after(r)


def activation_tile(j, gb, down, slope, sums):
    total = jnp.zeros((1, TILE), F32)
    for r in range(gb.shape[0] // 256):
        rows = slice(r * 256, (r + 1) * 256)
        gact = dot(gb[rows], down[j * TILE : (j + 1) * TILE], NT)
        gpre = (gact * slope[j, rows].astype(F32)).astype(BF16)
        slope[j, rows] = gpre
        total = total + rowsum(gpre.astype(F32))
    sums[UPB + j : UPB + j + 1] = total


def down_pieces(j, order):
    share = 3 * TILE // BLOCKS
    at, pieces = j * TILE, []
    while at < (j + 1) * TILE:
        stop = min((at // share + 1) * share, (j + 1) * TILE)
        pieces.append((position(at // share, order), at % share, stop - at, at - j * TILE))
        at = stop
    return pieces


def up_tile(j, order, adapted, gpre, upd):
    gup = dot(adapted[...], gpre, TN).astype(BF16)
    share = TILE // BLOCKS
    for i in range(BLOCKS):
        upd[position(i, order), j * share : (j + 1) * share] = gup[i * share : (i + 1) * share]


def down_tile(j, order, gb, act, dnd):
    gdn = dot(act, gb[...], TN).astype(BF16)
    for block, first, rows, at in down_pieces(j, order):
        dnd[block, first : first + rows] = gdn[at : at + rows]


def norm_backward(gad, normed, inv, small, clip, grad_out, v, shifts):
    n = normed.astype(F32)
    width = n.shape[1]
    scale = small[pl.ds(SCALE + clip, 1)]
    g_shift = rowsum(gad)
    g_scale = rowsum(gad * n)
    gn = gad * scale
    m1 = jnp.mean(gn, axis=-1, keepdims=True)
    m2 = jnp.mean(gn * n, axis=-1, keepdims=True)
    gc = (gn - m1 - n * m2) * wide(inv, width)
    low = gc.astype(BF16)
    total = grad_out + gc * small[3:4]
    v = v.astype(F32)
    g_taps = []
    for k in range(7):
        if k == 3:
            g_taps.append(rowsum(gc * v))
            continue
        moved = shifted(shifts, low, 3 - k)
        total = total + moved * small[k : k + 1]
        g_taps.append(rowsum(moved * v))
    return total.astype(BF16), jnp.concatenate(g_taps + [rowsum(gc)], axis=0), g_scale, g_shift


def place_weights(sec, block, up_own, up_got, down_own, down_got, up, down, sems, start):
    def go(up_from, down_from):
        for source, target, sem in ((up_from, up, sems.at[0]), (down_from, down, sems.at[1])):
            copy = pltpu.make_async_copy(source, target, sem)
            copy.start() if start else copy.wait()

    if not start:
        go(up_own, down_own)
        return

    @pl.when(sec[0] == block)
    def _():
        go(up_own, down_own)

    @pl.when(sec[0] != block)
    def _():
        go(up_got, down_got)


def leaving(block, place):
    return 1 - ((place[0] >> ORDERS[block][0]) & 1)


def route_block(block, layer, sec, place, sums, kept, passed, stays, sems, start):
    half = BLOCKS // 2
    goes = leaving(block, place)

    def go(*targets):
        for side, (target, first) in enumerate(zip(targets, (goes, 1 - goes))):
            part = sums.at[pl.ds(first * half, half)]
            copy = pltpu.make_async_copy(part, target, sems.at[layer, side])
            copy.start() if start else copy.wait()

    if not start:
        go(passed, stays)
        return

    @pl.when(sec[0] == block)
    def _():
        go(kept.at[pl.ds(goes * half, half)], kept.at[pl.ds((1 - goes) * half, half)])

    @pl.when(sec[0] != block)
    def _():
        go(passed, stays)


def route(sec, upd, dnd, keep, send, sems, start):
    def go(kept, sent):
        for source, target, sem in ((kept, keep, sems.at[0]), (sent, send, sems.at[1])):
            copy = pltpu.make_async_copy(source, target, sem)
            copy.start() if start else copy.wait()

    if not start:
        go(upd, dnd)
        return

    @pl.when(sec[0] == 0)
    def _():
        go(upd, dnd)

    @pl.when(sec[0] != 0)
    def _():
        go(dnd, upd)


def main_body(
    sec, place, valid, own_small, got_small, tokens, cot, up_own, up_got, down_own, down_got,
    sums0, sums1, gin1, normed_hbm, inv_hbm, out_own, out_send, gpre_hbm, up_keep, down_keep,
    up_pass, down_pass, up_stay, down_stay, small0_out,
    up0, down0, up1, down1, act0, slope0, act1, slope1, acc, adapted0, normed0, inv0, normed, inv, adapted1,
    branch0,
    gb, v, grad, out0, out1, small0, small1, shifts, upd, dnd, upd0, dnd0, sems, pieces, parts,
):
    clips = acc.shape[0] // 256
    mine = pl.ds(sec[0] * clips, clips)
    loads = (
        pltpu.make_async_copy(tokens.at[mine], v, sems.at[6, 0]),
        pltpu.make_async_copy(cot.at[mine], grad, sems.at[6, 1]),
    )
    loads[0].start()
    weights = (up_own, up_got, down_own, down_got)
    place_weights(sec, 0, *weights, up0, down0, sems.at[0], True)
    place_weights(sec, 1, *weights, up1, down1, sems.at[1], True)
    loads[1].start()
    first = sec[0] == 0
    small0[...] = pick(first, own_small[...], got_small[...])
    small1[...] = pick(first, got_small[...], own_small[...])
    small0_out[...] = small0[...]
    sums0[...] = jnp.zeros_like(sums0)
    sums1[...] = jnp.zeros_like(sums1)
    set_shifts(shifts)
    loads[0].wait()

    def begin(r):
        rows = slice(r * 256, (r + 1) * 256)
        adapted0[rows], normed0[rows], inv0[rows] = normalize(v[r], small0, r, shifts)

    def between(r):
        rows = slice(r * 256, (r + 1) * 256)
        branch = acc[rows] + small0[DOWNB : DOWNB + 1]
        branch0[rows] = branch
        result = (v[r].astype(F32) + small0[GAIN : GAIN + 1] * branch).astype(BF16)
        out0[r] = result
        adapted1[rows], normed[rows], inv[rows] = normalize(result, small1, r, shifts)

    def top(r):
        rows = slice(r * 256, (r + 1) * 256)
        branch = acc[rows] + small1[DOWNB : DOWNB + 1]
        gain = small1[GAIN : GAIN + 1]
        out1[r] = (out0[r].astype(F32) + gain * branch).astype(BF16)
        above = grad[r].astype(F32) * valid[sec[0] * clips + r].astype(F32)
        low = (above * gain).astype(BF16)
        gb[rows] = low
        sums1[GAIN : GAIN + 1] += rowsum(above * branch)
        sums1[DOWNB : DOWNB + 1] += rowsum(low.astype(F32))

    begin(0)
    place_weights(sec, 0, *weights, up0, down0, sems.at[0], False)
    forward_tiles(
        adapted0, up0, down0, small0, act0, slope0, acc, lambda r: begin(r) if r > 0 else None, between
    )
    saves = [
        pltpu.make_async_copy(source, target, sems.at[7, n])
        for n, (source, target) in enumerate(((normed0, normed_hbm), (inv0, inv_hbm)))
    ]
    for copy in saves:
        copy.start()
    place_weights(sec, 1, *weights, up1, down1, sems.at[1], False)
    loads[1].wait()
    forward_tiles(adapted1, up1, down1, small1, act1, slope1, acc, None, top)
    half_own = out_own.at[mine]
    route(sec, out0, out1, half_own, out_send, sems.at[4], True)
    for j in range(3):
        activation_tile(j, gb, down1, slope1, sums1)
        for r in range(clips):
            rows = slice(r * 256, (r + 1) * 256)
            part = dot(slope1[j, rows], up1[:, j * TILE : (j + 1) * TILE], NT)
            acc[rows] = part if j == 0 else acc[rows] + part
        up_tile(j, ORDERS[1], adapted1, slope1[j], upd)
        down_tile(j, ORDERS[1], gb, act1[j], dnd)
    ends = ((up_keep, up_pass, up_stay), (down_keep, down_pass, down_stay))
    for n, source in enumerate((upd, dnd)):
        route_block(1, n, sec, place, source, *ends[n], parts.at[1], True)

    def move(r):
        return pltpu.make_async_copy(grad.at[r], gin1.at[r], pieces.at[r])

    def under(r):
        rows = pl.ds(pl.multiple_of(r * 256, 256), 256)
        above = grad[r].astype(F32) * valid[sec[0] * clips + r].astype(F32)
        gin, smalls, g_scale, g_shift = norm_backward(
            acc[rows], normed[rows], inv[rows], small1, r, above, out0[r], shifts
        )
        grad[r] = gin
        sums1[TAPS : TAPS + 8] += smalls
        sums1[pl.ds(SCALE + r, 1)] = g_scale
        sums1[pl.ds(SHIFT + r, 1)] = g_shift
        grad0 = gin.astype(F32)
        low = (grad0 * small0[GAIN : GAIN + 1]).astype(BF16)
        gb[rows] = low
        move(r).start()
        sums0[GAIN : GAIN + 1] += rowsum(grad0 * branch0[rows])
        sums0[DOWNB : DOWNB + 1] += rowsum(low.astype(F32))

    pl.loop(0, clips, unroll=True)(under)
    tiles = []
    for j in range(3):
        activation_tile(j, gb, down0, slope0, sums0)
        tiles.append(pltpu.make_async_copy(slope0.at[j], gpre_hbm.at[j], sems.at[5 + j // 2 * 3, j % 2]))
        tiles[-1].start()
        up_tile(j, ORDERS[0], adapted0, slope0[j], upd0)
    route_block(0, 0, sec, place, upd0, *ends[0], parts.at[0], True)
    for j in range(3):
        down_tile(j, ORDERS[0], gb, act0[j], dnd0)
    route_block(0, 1, sec, place, dnd0, *ends[1], parts.at[0], True)
    route(sec, out0, out1, half_own, out_send, sems.at[4], False)
    for n, source in enumerate((upd, dnd)):
        route_block(1, n, sec, place, source, *ends[n], parts.at[1], False)
    for copy in saves + tiles + [move(r) for r in range(clips)]:
        copy.wait()
    for n, source in enumerate((upd0, dnd0)):
        route_block(0, n, sec, place, source, *ends[n], parts.at[0], False)


def last_body(
    sec, gpre, up_own, up_got, normed, inv, small, grad_out, tokens, sums0, sums1, own_small, gin, away, own,
    send,
    up, shifts, sums, sem,
):
    clip = pl.program_id(0)

    @pl.when(clip == 0)
    def _():
        sums[...] = sums0[...]

        @pl.when(sec[0] == 0)
        def _():
            pltpu.make_async_copy(up_own, up, sem).start()

        @pl.when(sec[0] != 0)
        def _():
            pltpu.make_async_copy(up_got, up, sem).start()

        set_shifts(shifts)
        pltpu.make_async_copy(up_own, up, sem).wait()

    gad = dot(gpre[0], up[:, :TILE], NT)
    for j in range(1, 3):
        gad = gad + dot(gpre[j], up[:, j * TILE : (j + 1) * TILE], NT)
    above = grad_out[0]
    out, smalls, g_scale, g_shift = norm_backward(
        gad, normed[...], inv[...], small, clip, above.astype(F32), tokens[0], shifts
    )
    gin[0] = jnp.where(sec[0] == 0, out, above)
    away[0] = jnp.where(sec[0] == 0, above, out)
    sums[TAPS : TAPS + 8] += smalls
    sums[pl.ds(SCALE + clip, 1)] = g_scale
    sums[pl.ds(SHIFT + clip, 1)] = g_shift

    @pl.when(clip == pl.num_programs(0) - 1)
    def _():
        own[...] = pick(sec[0] == 0, sums[...], sums1[...])
        own[CODE : CODE + 2] = own_small[CODE : CODE + 2]
        send[...] = pick(sec[0] == 0, sums1[...], sums[...])


def pick(first, a, b):
    return jnp.where(first, a, b)


def bit_of(spot, step):
    low, high = ORDERS[0][step], ORDERS[1][step]
    return (spot[1] >> (low if low == high else pick(spot[0] == 0, low, high))) & 1


GATHER = (3, 2, 0, 1)


def gather_bit(spot, hop):
    return (spot[1] >> GATHER[hop]) & 1


def gather_slot(spot):
    slot = 0
    for hop in range(len(GATHER)):
        slot = slot + gather_bit(spot, hop) * (1 << hop)
    return slot


def fetch(copies, source, first, rows, target, sem):
    copies.append(pltpu.make_async_copy(source.at[pl.ds(first, rows)], target, sem))
    copies[-1].start()


def pack_body(step, share, sec, place, total0, total1, *refs):
    rows = (8 >> step) * share
    first = pl.multiple_of((1 - bit_of((sec[0], place[0]), step)) * rows, 32)
    if step == 1:
        came, (packet, buffer, sems) = refs[:2], refs[2:]
        copies = []
        for b in range(2):
            fetch(copies, came[b], first, rows, buffer.at[b], sems.at[b])
    else:
        came, packet = refs
    for b, total in enumerate((total0, total1)):
        if step == 1:
            copies[b].wait()
            latest = buffer[b]
        else:
            latest = came[pl.ds(b * 2 * rows + first, rows)]
        packet[b * rows : (b + 1) * rows] = (total[pl.ds(first, rows)] + latest.astype(F32)).astype(BF16)


def share_body(share, total0, total1, came, up, down):
    rows = up.shape[0]
    whole = total0[...] + came[:share].astype(F32)
    for j in range(3):
        up[:, j * TILE : (j + 1) * TILE] = whole[j * rows : (j + 1) * rows]
    down[...] = total1[...] + came[share : 2 * share].astype(F32)


def begin_rows_body(sec, own, got, packet, smalls):
    first = sec[0] == 0
    low = pick(first, own[SCALE:], got[SCALE:])
    high = pick(first, got[SCALE:], own[SCALE:])
    packet[:16] = jnp.concatenate([low, high], axis=0).astype(BF16)
    smalls[...] = own[:SCALE] + got[:SCALE]
    packet[16:32] = smalls[...].astype(BF16)


def more_rows_body(hop, place, before, after, smalls_in, packet, smalls):
    size = 16 << (hop - 1)
    bit = gather_bit((0, place[0]), hop - 1)
    for source, side in ((before, bit), (after, 1 - bit)):
        packet[pl.ds(pl.multiple_of(side * size, 16), size)] = source[:size]
    smalls[...] = smalls_in[...] + after[size:].astype(F32)
    packet[2 * size :] = smalls[...].astype(BF16)


def tables_body(place, before, after, smalls_in, scale, shift, taps, conv, upb, downb, gain, rows_of):
    size = rows_of.shape[0] // 2
    bit = gather_bit((0, place[0]), len(GATHER) - 1)
    for source, side in ((before, bit), (after, 1 - bit)):
        rows_of[pl.ds(pl.multiple_of(side * size, 16), size)] = source[:size]
    total = smalls_in[...] + after[size:].astype(F32)
    owned = scale.shape[0]
    count = 2 * size
    who = total[CODE : CODE + 1, :count] * 64.0 + total[CODE + 1 : CODE + 2, :count]
    wanted = lax.broadcasted_iota(jnp.int32, (owned, count), 0) + place[0] * owned
    hit = who == wanted.astype(F32)
    kind = (lax.broadcasted_iota(jnp.int32, (owned, count), 1) >> 2) & 1
    for k, out in enumerate((scale, shift)):
        out[...] = dot(jnp.where(hit & (kind == k), 1.0, 0.0).astype(BF16), rows_of[...], NN)
    lanes = total.shape[1] // BLOCKS
    turn = lax.rem(BLOCKS - place[0], BLOCKS)
    cut = pltpu.roll(total, turn * lanes, 1)[:, :lanes]
    for k in range(7):
        taps[k] = cut[k : k + 1]
    conv[...] = cut[CONV : CONV + 1]
    downb[...] = cut[DOWNB : DOWNB + 1]
    gain[...] = cut[GAIN : GAIN + 1]
    line = jnp.concatenate([total[UPB + k : UPB + k + 1] for k in range(3)], axis=1)
    upb[...] = pltpu.roll(line, turn * 3 * lanes, 1)[:, : 3 * lanes]


def struct(shape, dtype):
    return jax.ShapeDtypeStruct(shape, dtype)


def params(limit=None):
    return pltpu.CompilerParams(vmem_limit_bytes=limit * 1024 * 1024 if limit else ALL_VMEM)


def cost(flops, moved):
    return pl.CostEstimate(flops=int(flops), bytes_accessed=int(moved), transcendentals=0)


def local(
    tokens, out_cotangent, speaker, valid, conv_weight, conv_bias, scale_table, shift_table,
    up_weight, up_bias, down_weight, down_bias, layer_scale,
):
    section = lax.axis_index("section").astype(jnp.int32)
    place = lax.axis_index("dp").astype(jnp.int32)
    devices = lax.axis_size("dp")
    clips, frames, width = tokens.shape
    hidden = up_weight.shape[2]
    table_rows = scale_table.shape[1]
    half = clips // 2
    rows = half * frames
    sec = section[None]
    swap = [(0, 1), (1, 0)]

    own_small, other_small = pl.pallas_call(
        prep_body,
        out_shape=[struct((SMALL, width), F32)] * 2,
        in_specs=[SMEM, SMEM, SMEM] + [VMEM] * 5 + [ANY] * 2,
        out_specs=[VMEM] * 2,
        scratch_shapes=[pltpu.SemaphoreType.DMA((2, 2, half))],
        compiler_params=params(),
        name="prep",
    )(
        sec, place[None], speaker, conv_weight.transpose(1, 0, 2), conv_bias, up_bias, down_bias, layer_scale,
        scale_table, shift_table,
    )
    got_small = lax.ppermute(other_small, "section", swap)
    up_own, down_own = up_weight[0], down_weight[0]
    up_got = lax.ppermute(up_own, "section", swap)
    down_got = lax.ppermute(down_own, "section", swap)
    clip_block = (1, frames, width)
    whole_small = pl.BlockSpec((SMALL, width), lambda c, sec: (0, 0))
    half_struct = struct((half, frames, width), BF16)
    whole_struct = struct((clips, frames, width), BF16)
    small_struct = struct((SMALL, width), F32)
    flat_struct = struct((rows, width), BF16)
    tiles = hidden // TILE
    tiled = (tiles, rows, TILE)
    share = hidden // BLOCKS
    gradient = (BLOCKS, share, width)
    gradient_struct = struct(gradient, BF16)
    piece_struct = struct((BLOCKS // 2, share, width), BF16)
    product = 2 * rows * width * hidden

    (
        sums0, sums1, gin1, normed0, inv0, out_own, out_send, gpre0, up_keep,
        down_keep, up_pass, down_pass, up_stay, down_stay, small0,
    ) = pl.pallas_call(
        main_body,
        out_shape=[
            small_struct, small_struct, half_struct, flat_struct, struct((rows, 128), F32),
            whole_struct, half_struct, struct(tiled, BF16), gradient_struct, gradient_struct,
            piece_struct, piece_struct, piece_struct, piece_struct, small_struct,
        ],
        in_specs=[SMEM, SMEM, SMEM, VMEM, VMEM, HBM, HBM, HBM, ANY, HBM, ANY],
        out_specs=[VMEM, VMEM] + [HBM] * 12 + [VMEM],
        scratch_shapes=[
            pltpu.VMEM((width, hidden), BF16),
            pltpu.VMEM((hidden, width), BF16),
            pltpu.VMEM((width, hidden), BF16),
            pltpu.VMEM((hidden, width), BF16),
            pltpu.VMEM(tiled, BF16),
            pltpu.VMEM(tiled, BF16),
            pltpu.VMEM(tiled, BF16),
            pltpu.VMEM(tiled, BF16),
            pltpu.VMEM((rows, width), F32),
            pltpu.VMEM((rows, width), BF16),
            pltpu.VMEM((rows, width), BF16),
            pltpu.VMEM((rows, 128), F32),
            pltpu.VMEM((rows, width), BF16),
            pltpu.VMEM((rows, 128), F32),
            pltpu.VMEM((rows, width), BF16),
            pltpu.VMEM((rows, width), F32),
            pltpu.VMEM((rows, width), BF16),
            pltpu.VMEM((half, frames, width), BF16),
            pltpu.VMEM((half, frames, width), BF16),
            pltpu.VMEM((half, frames, width), BF16),
            pltpu.VMEM((half, frames, width), BF16),
            pltpu.VMEM((SMALL, width), F32),
            pltpu.VMEM((SMALL, width), F32),
            pltpu.VMEM((len(OFFSETS) * frames, frames), BF16),
            pltpu.VMEM(gradient, BF16),
            pltpu.VMEM(gradient, BF16),
            pltpu.VMEM(gradient, BF16),
            pltpu.VMEM(gradient, BF16),
            pltpu.SemaphoreType.DMA((9, 2)),
            pltpu.SemaphoreType.DMA((half,)),
            pltpu.SemaphoreType.DMA((2, 2, 2)),
        ],
        compiler_params=params(),
        cost_estimate=cost(11 * product, 24 << 20),
        name="main",
    )(
        sec, place[None], valid, own_small, got_small, tokens, out_cotangent, up_own, up_got, down_own, down_got
    )
    swapped = []
    for piece in (up_pass, down_pass, up_stay, down_stay):
        swapped.append(lax.ppermute(piece, "section", swap))
    pairs = [[up_keep, swapped[0], swapped[2]], [down_keep, swapped[1], swapped[3]]]
    got_out = lax.ppermute(out_send, "section", swap)

    gin_own, gin_send, own_sums, sums_send = pl.pallas_call(
        last_body,
        grid_spec=pltpu.PrefetchScalarGridSpec(
            num_scalar_prefetch=1,
            grid=(half,),
            in_specs=[
                pl.BlockSpec((tiles, frames, TILE), lambda c, sec: (0, c, 0)),
                HBM,
                ANY,
                pl.BlockSpec((frames, width), lambda c, sec: (c, 0)),
                pl.BlockSpec((frames, 128), lambda c, sec: (c, 0)),
                whole_small,
                pl.BlockSpec(clip_block, lambda c, sec: (c, 0, 0)),
                pl.BlockSpec(clip_block, lambda c, sec: (sec[0] * half + c, 0, 0)),
                whole_small,
                whole_small,
                whole_small,
            ],
            out_specs=[
                pl.BlockSpec(clip_block, lambda c, sec: (sec[0] * half + c, 0, 0)),
                pl.BlockSpec(clip_block, lambda c, sec: (c, 0, 0)),
                whole_small,
                whole_small,
            ],
            scratch_shapes=[
                pltpu.VMEM((width, hidden), BF16),
                pltpu.VMEM((len(OFFSETS) * frames, frames), BF16),
                pltpu.VMEM((SMALL, width), F32),
                pltpu.SemaphoreType.DMA,
            ],
        ),
        out_shape=[whole_struct, half_struct, small_struct, small_struct],
        compiler_params=params(),
        cost_estimate=cost(2 * half * product, 12 << 20),
        name="last",
    )(sec, gpre0, up_own, up_got, normed0, inv0, small0, gin1, tokens, sums0, sums1, own_small)
    got_gin = lax.ppermute(gin_send, "section", swap)
    got_sums = lax.ppermute(sums_send, "section", swap)

    def joined(whole, got):
        return lax.dynamic_update_slice(whole, got, ((1 - section) * half, 0, 0))[None]

    block_outputs = joined(out_own, got_out)
    input_grads = joined(gin_own, got_gin)
    if devices == BLOCKS:
        outs = halved(sec, place[None], pairs, own_sums, got_sums, table_rows)
    else:
        outs = scattered(section, place, devices, speaker, pairs, own_sums, got_sums, table_rows)
    return (block_outputs, input_grads) + outs


def exchanged(packet, step):
    devices = lax.axis_size("dp")
    moves = [
        (s * devices + i, s * devices + (i ^ (1 << ORDERS[s][step])))
        for s in range(2)
        for i in range(devices)
    ]
    return lax.ppermute(packet, PAIR, moves)


def halved(sec, place, pairs, own_sums, got_sums, table_rows):
    _, share, width = pairs[0][0].shape
    pairs = [[piece.reshape(-1, width) for piece in pair] for pair in pairs]
    spot = (sec[0], place[0])
    half_rows = 8 * share

    def part(array, first, count):
        return lax.dynamic_slice_in_dim(array, first, count, 0).astype(F32)

    bit = bit_of(spot, 0)
    latest, totals = [None, None], [None, None]
    for b in (0, 1):
        keep, passed, stays = pairs[b]
        own = lax.optimization_barrier(part(keep, (1 - bit) * half_rows, half_rows))
        packet = (own + passed.astype(F32)).astype(BF16)
        latest[b] = exchanged(packet, 0)
        keep, stays, _ = lax.optimization_barrier((keep, stays, own_sums))
        totals[b] = part(keep, bit * half_rows, half_rows) + stays.astype(F32)

    def small_call(body, outs, scalars, operands, scratch=(), specs=None, limit=8):
        return pl.pallas_call(
            body,
            out_shape=outs,
            in_specs=[SMEM] * len(scalars) + (specs or [VMEM] * len(operands)),
            out_specs=[VMEM] * len(outs),
            scratch_shapes=scratch,
            compiler_params=params(limit),
            cost_estimate=cost(0, 2 << 20),
        )(*scalars, *operands)

    def row_outs(hop):
        return [struct(((16 << hop) + 16, width), BF16), struct((SCALE, width), F32)]

    rows_packet, smalls = small_call(begin_rows_body, row_outs(0), [sec], [own_sums, got_sums], limit=None)
    for hop in range(len(GATHER)):
        more = lax.ppermute(
            rows_packet, "dp", [(i, i ^ (1 << GATHER[hop])) for i in range(BLOCKS)]
        )
        operands = [rows_packet, more, smalls]
        if hop + 1 < len(GATHER):
            rows_packet, smalls = small_call(
                functools.partial(more_rows_body, hop + 1), row_outs(hop + 1), [place],
                operands,
            )
    owned = table_rows // BLOCKS
    lanes = width // BLOCKS
    one = struct((1, lanes), F32)
    scale, shift, taps, conv, upb, downb, gain = small_call(
        tables_body,
        [
            struct((owned, width), F32),
            struct((owned, width), F32),
            struct((7, 1, lanes), F32),
            one,
            struct((1, 3 * lanes), F32),
            one,
            one,
        ],
        [place],
        operands,
        [pltpu.VMEM((16 * BLOCKS, width), BF16)],
    )

    for step in range(1, 4):
        rows = (8 >> step) * share
        first = bit_of(spot, step) * rows
        packet_struct = [struct((2 * rows, width), BF16)]
        if step == 1:
            (packet,) = small_call(
                functools.partial(pack_body, step, share), packet_struct, [sec, place],
                totals + latest,
                [pltpu.VMEM((2, rows, width), BF16), pltpu.SemaphoreType.DMA((2,))],
                [VMEM] * 2 + [ANY] * 2,
            )
        else:
            (packet,) = small_call(
                functools.partial(pack_body, step, share), packet_struct, [sec, place],
                totals + latest[:1],
            )
        got = exchanged(packet, step)
        bases = (0, 0) if step == 1 else (0, 2 * rows)
        totals = [
            part(totals[b], first, rows) + part(latest[b], bases[b] + first, rows) for b in range(2)
        ]
        latest = [got, got]
    up, down = small_call(
        functools.partial(share_body, share),
        [struct((width // BLOCKS, 3 * TILE), F32), struct((share, width), F32)],
        [],
        totals + latest[:1],
    )
    return (
        taps.transpose(1, 0, 2), conv, scale[None], shift[None], up[None], upb, down[None], downb, gain
    )


def scattered(section, place, devices, speaker, pairs, own_sums, got_sums, table_rows):
    first_section = section == 0
    smalls = lax.psum(own_sums[:SCALE] + got_sums[:SCALE], "dp")
    clip_rows = jnp.stack([own_sums[SCALE:], got_sums[SCALE:]])
    clip_rows = pick(first_section, clip_rows, clip_rows[::-1]).astype(BF16)
    clips = speaker.shape[0]
    width = clip_rows.shape[-1]
    clip_rows = clip_rows.reshape(2, 2, clips // 2, width).transpose(1, 0, 2, 3).reshape(2, clips, width)
    gathered = lax.all_gather(clip_rows, "dp", axis=1, tiled=True)
    who = lax.all_gather(speaker, "dp", tiled=True)
    owned = table_rows // devices
    wanted = place * owned + jnp.arange(owned, dtype=jnp.int32)
    chosen = (who[None, :] == wanted[:, None]).astype(BF16)
    tables = [jnp.dot(chosen, gathered[k], preferred_element_type=F32) for k in range(2)]
    low, high = ORDERS[0][0], ORDERS[1][0]
    leaves = 1 - ((place >> pick(first_section, low, high)) & 1)
    natural = []
    for keep, gone, stay in pairs:
        other = pick(leaves == 0, jnp.concatenate([gone, stay]), jnp.concatenate([stay, gone]))
        whole = keep.astype(F32) + other.astype(F32)
        both = [jnp.stack([whole[position(i, order)] for i in range(BLOCKS)]) for order in ORDERS]
        natural.append(pick(first_section, both[0], both[1]))
    _, rows, width = natural[0].shape
    tiles = rows * BLOCKS // TILE
    up = natural[0].reshape(BLOCKS, tiles, rows // tiles, TILE).transpose(0, 2, 1, 3)
    up_share = lax.psum_scatter(up.reshape(width, -1), "dp", scatter_dimension=0, tiled=True)
    down_share = lax.psum_scatter(natural[1].reshape(-1, width), "dp", scatter_dimension=0, tiled=True)
    lanes = width // devices
    own_lanes = lax.dynamic_slice_in_dim(smalls, place * lanes, lanes, 1)
    upb = lax.dynamic_slice_in_dim(smalls[UPB : UPB + 3].reshape(-1), place * 3 * lanes, 3 * lanes, 0)
    return (
        own_lanes[TAPS : TAPS + 7][None],
        own_lanes[CONV : CONV + 1],
        tables[0][None],
        tables[1][None],
        up_share[None],
        upb[None],
        down_share[None],
        own_lanes[DOWNB : DOWNB + 1],
        own_lanes[GAIN : GAIN + 1],
    )


def solution(mesh):
    placed = (
        P("dp", None, None),
        P("dp", None, None),
        P("dp"),
        P("dp"),
        P("section", None, None),
        P("section", None),
        P("section", None, None),
        P("section", None, None),
        P("section", None, None),
        P("section", None),
        P("section", None, None),
        P("section", None),
        P("section", None),
    )

    return jax.shard_map(
        local,
        mesh=mesh,
        in_specs=placed,
        out_specs=(
            P("section", "dp", None, None),
            P("section", "dp", None, None),
            P("section", None, "dp"),
            P("section", "dp"),
            P("section", "dp", None),
            P("section", "dp", None),
            P("section", "dp", None),
            P("section", "dp"),
            P("section", "dp", None),
            P("section", "dp"),
            P("section", "dp"),
        ),
        check_vma=False,
    )
```

```python
import functools

import jax
import jax.numpy as jnp
from jax import lax
from jax.experimental import pallas as pl
from jax.experimental.pallas import tpu as pltpu
from jax.sharding import PartitionSpec as P


F32 = jnp.float32
BF16 = jnp.bfloat16
PAIR = ("section", "dp")
TILE = 512
ALL_VMEM = 67043328
HALF_ROOT = 0.7071067811865476
DENSITY = 0.3989422804014327
BLOCKS = 16
ORDERS = ((0, 1, 2, 3), (2, 0, 1, 3))
ANY = pl.BlockSpec(memory_space=pl.ANY)
HBM = pl.BlockSpec(memory_space=pltpu.HBM)
VMEM = pl.BlockSpec(memory_space=pltpu.VMEM)
SMEM = pl.BlockSpec(memory_space=pltpu.SMEM)

TAPS, CONV, UPB, DOWNB, GAIN, CODE, SCALE, SHIFT, SMALL = 0, 7, 8, 11, 12, 13, 16, 20, 24


def position(block, order):
    place = 0
    for bit in order:
        place = 2 * place + ((block >> bit) & 1)
    return place


def dot(a, b, dims):
    return lax.dot_general(a, b, (dims, ((), ())), preferred_element_type=F32)


NN = ((1,), (0,))
NT = ((1,), (1,))
TN = ((0,), (0,))


OFFSETS = (-3, -2, -1, 1, 2, 3)


def set_shifts(shifts):
    frames = shifts.shape[1]
    row = lax.broadcasted_iota(jnp.int32, (frames, frames), 0)
    col = lax.broadcasted_iota(jnp.int32, (frames, frames), 1)
    for n, offset in enumerate(OFFSETS):
        shifts[n * frames : (n + 1) * frames] = jnp.where(col == row + offset, 1.0, 0.0).astype(BF16)


def shifted(shifts, x, offset):
    frames = x.shape[0]
    n = OFFSETS.index(offset)
    return dot(shifts[n * frames : (n + 1) * frames], x, NN)


def wide(x, width):
    return jnp.concatenate([x] * (width // 128), axis=1)


def rowsum(x):
    return jnp.sum(x, axis=0, keepdims=True)


def normalize(x, small, clip, shifts):
    conv = small[CONV : CONV + 1] + x.astype(F32) * small[3:4]
    for offset in OFFSETS:
        conv = conv + shifted(shifts, x, offset) * small[offset + 3 : offset + 4]
    centred = conv - jnp.mean(conv, axis=-1, keepdims=True)
    inv = lax.rsqrt(jnp.mean(centred * centred, axis=-1, keepdims=True) + 1e-06)
    normed = centred * inv
    scale = small[pl.ds(SCALE + clip, 1)]
    shift = small[pl.ds(SHIFT + clip, 1)]
    adapted = (normed * scale + shift).astype(BF16)
    return adapted, normed.astype(BF16), jnp.broadcast_to(inv, (x.shape[0], 128))


def prep_body(sec, place, speaker, taps, conv, upb, downb, gain, scale_hbm, shift_hbm, own, other, sems):
    width = own.shape[1]
    half = SMALL - SHIFT
    copies = []
    for side, out in enumerate((own, other)):
        first = (sec[0] if side == 0 else 1 - sec[0]) * half
        for clip in range(half):
            row = speaker[first + clip]
            for kind, table in enumerate((scale_hbm, shift_hbm)):
                copies.append(
                    pltpu.make_async_copy(
                        table.at[0, pl.ds(row, 1)],
                        out.at[pl.ds((SCALE, SHIFT)[kind] + clip, 1)],
                        sems.at[side, kind, clip],
                    )
                )
    for copy in copies:
        copy.start()
    for out in (own, other):
        for k in range(7):
            out[TAPS + k : TAPS + k + 1] = taps[k]
        out[CONV : CONV + 1] = conv[...]
        for k in range(DOWNB - UPB):
            out[UPB + k : UPB + k + 1] = upb[:, k * width : (k + 1) * width]
        out[DOWNB : DOWNB + 1] = downb[...]
        out[GAIN : GAIN + 1] = gain[...]
        out[GAIN + 1 : SCALE] = jnp.zeros((SCALE - GAIN - 1, width), F32)
    lane = lax.broadcasted_iota(jnp.int32, (1, width), 1)
    here = (lane >> 4) == gather_slot((sec[0], place[0]))
    which = ((lane >> 3) & 1) * 4 + (lane & 3)
    code = jnp.zeros(lane.shape, jnp.int32)
    for c in range(2 * half):
        code = jnp.where(here & (which == c), speaker[c], code)
    own[CODE : CODE + 1] = (code >> 6).astype(F32)
    own[CODE + 1 : CODE + 2] = (code & 63).astype(F32)
    for copy in copies:
        copy.wait()


def forward_tiles(adapted, up, down, small, act, slope, acc):
    steps = [(j, r) for j in range(3) for r in range(acc.shape[0] // 256)]

    def hidden(j, r):
        part = dot(adapted[r * 256 : (r + 1) * 256], up[:, j * TILE : (j + 1) * TILE], NN)
        return part + small[UPB + j : UPB + j + 1]

    ahead = hidden(*steps[0])
    for n, (j, r) in enumerate(steps):
        rows = slice(r * 256, (r + 1) * 256)
        pre = ahead
        if n + 1 < len(steps):
            ahead = hidden(*steps[n + 1])
        phi = 0.5 * lax.erf(pre * HALF_ROOT) + 0.5
        low = (pre * phi).astype(BF16)
        act[j, rows] = low
        slope[j, rows] = (phi + pre * (DENSITY * jnp.exp(-0.5 * pre * pre))).astype(BF16)
        part = dot(low, down[j * TILE : (j + 1) * TILE], NN)
        acc[rows] = part if j == 0 else acc[rows] + part


def activation_tile(j, gb, down, slope, sums):
    total = jnp.zeros((1, TILE), F32)
    for r in range(gb.shape[0] // 256):
        rows = slice(r * 256, (r + 1) * 256)
        gact = dot(gb[rows], down[j * TILE : (j + 1) * TILE], NT)
        gpre = (gact * slope[j, rows].astype(F32)).astype(BF16)
        slope[j, rows] = gpre
        total = total + rowsum(gpre.astype(F32))
    sums[UPB + j : UPB + j + 1] = total


def down_pieces(j, order):
    share = 3 * TILE // BLOCKS
    at, pieces = j * TILE, []
    while at < (j + 1) * TILE:
        stop = min((at // share + 1) * share, (j + 1) * TILE)
        pieces.append((position(at // share, order), at % share, stop - at, at - j * TILE))
        at = stop
    return pieces


def up_tile(j, order, adapted, gpre, upd):
    gup = dot(adapted[...], gpre, TN).astype(BF16)
    share = TILE // BLOCKS
    for i in range(BLOCKS):
        upd[position(i, order), j * share : (j + 1) * share] = gup[i * share : (i + 1) * share]


def down_tile(j, order, gb, act, dnd):
    gdn = dot(act, gb[...], TN).astype(BF16)
    for block, first, rows, at in down_pieces(j, order):
        dnd[block, first : first + rows] = gdn[at : at + rows]


def norm_backward(gad, normed, inv, small, clip, grad_out, v, shifts):
    n = normed.astype(F32)
    width = n.shape[1]
    scale = small[pl.ds(SCALE + clip, 1)]
    g_shift = rowsum(gad)
    g_scale = rowsum(gad * n)
    gn = gad * scale
    m1 = jnp.mean(gn, axis=-1, keepdims=True)
    m2 = jnp.mean(gn * n, axis=-1, keepdims=True)
    gc = (gn - m1 - n * m2) * wide(inv, width)
    low = gc.astype(BF16)
    total = grad_out + gc * small[3:4]
    v = v.astype(F32)
    g_taps = []
    for k in range(7):
        if k == 3:
            g_taps.append(rowsum(gc * v))
            continue
        moved = shifted(shifts, low, 3 - k)
        total = total + moved * small[k : k + 1]
        g_taps.append(rowsum(moved * v))
    return total.astype(BF16), jnp.concatenate(g_taps + [rowsum(gc)], axis=0), g_scale, g_shift


def place_weights(sec, block, up_own, up_got, down_own, down_got, up, down, sems, start):
    def go(up_from, down_from):
        for source, target, sem in ((up_from, up, sems.at[0]), (down_from, down, sems.at[1])):
            copy = pltpu.make_async_copy(source, target, sem)
            copy.start() if start else copy.wait()

    if not start:
        go(up_own, down_own)
        return

    @pl.when(sec[0] == block)
    def _():
        go(up_own, down_own)

    @pl.when(sec[0] != block)
    def _():
        go(up_got, down_got)


def leaving(block, place):
    return 1 - ((place[0] >> ORDERS[block][0]) & 1)


def route_block(block, sec, place, sums, kept, passed, stays, sems, start, rows):
    half = BLOCKS // 2
    goes = leaving(block, place)

    def go(*targets):
        for side, (target, first) in enumerate(zip(targets, (goes, 1 - goes))):
            part = sums.at[pl.ds(first * half, half), rows]
            copy = pltpu.make_async_copy(part, target.at[:, rows], sems.at[side])
            copy.start() if start else copy.wait()

    if not start:
        go(passed, stays)
        return

    @pl.when(sec[0] == block)
    def _():
        go(kept.at[pl.ds(goes * half, half)], kept.at[pl.ds((1 - goes) * half, half)])

    @pl.when(sec[0] != block)
    def _():
        go(passed, stays)


def route(sec, upd, dnd, keep, send, sems, start):
    def go(kept, sent):
        for source, target, sem in ((kept, keep, sems.at[0]), (sent, send, sems.at[1])):
            copy = pltpu.make_async_copy(source, target, sem)
            copy.start() if start else copy.wait()

    if not start:
        go(upd, dnd)
        return

    @pl.when(sec[0] == 0)
    def _():
        go(upd, dnd)

    @pl.when(sec[0] != 0)
    def _():
        go(dnd, upd)


def main_body(
    sec, place, valid, own_small, got_small, tokens, cot, up_own, up_got, down_own, down_got,
    sums0, sums1, gin1, normed_hbm, inv_hbm, out_own, out_send, gpre_hbm, up_keep, down_keep,
    up_pass, down_pass, up_stay, down_stay, small0_out,
    up0, down0, up1, down1, act0, slope0, act1, slope1, acc, adapted0, normed, inv, adapted1, branch0,
    gb, v, grad, out0, out1, small0, small1, shifts, upd, dnd, upd0, dnd0, sems, pieces, parts,
):
    clips = acc.shape[0] // 256
    mine = pl.ds(sec[0] * clips, clips)
    loads = (
        pltpu.make_async_copy(tokens.at[mine], v, sems.at[6, 0]),
        pltpu.make_async_copy(cot.at[mine], grad, sems.at[6, 1]),
    )
    loads[0].start()
    weights = (up_own, up_got, down_own, down_got)
    place_weights(sec, 0, *weights, up0, down0, sems.at[0], True)
    place_weights(sec, 1, *weights, up1, down1, sems.at[1], True)
    loads[1].start()
    first = sec[0] == 0
    small0[...] = pick(first, own_small[...], got_small[...])
    small1[...] = pick(first, got_small[...], own_small[...])
    small0_out[...] = small0[...]
    sums0[...] = jnp.zeros_like(sums0)
    sums1[...] = jnp.zeros_like(sums1)
    set_shifts(shifts)
    loads[0].wait()

    def begin(r):
        rows = pl.ds(pl.multiple_of(r * 256, 256), 256)
        adapted0[rows], normed[rows], inv[rows] = normalize(v[r], small0, r, shifts)

    pl.loop(0, clips, unroll=True)(begin)
    saves = [
        pltpu.make_async_copy(source, target, sems.at[7 + n // 2, n % 2])
        for n, (source, target) in enumerate(
            ((normed, normed_hbm), (inv, inv_hbm))
        )
    ]
    for copy in saves:
        copy.start()
    place_weights(sec, 0, *weights, up0, down0, sems.at[0], False)
    forward_tiles(adapted0, up0, down0, small0, act0, slope0, acc)
    for copy in saves:
        copy.wait()

    def between(r):
        rows = pl.ds(pl.multiple_of(r * 256, 256), 256)
        branch = acc[rows] + small0[DOWNB : DOWNB + 1]
        branch0[rows] = branch
        result = (v[r].astype(F32) + small0[GAIN : GAIN + 1] * branch).astype(BF16)
        out0[r] = result
        adapted1[rows], normed[rows], inv[rows] = normalize(result, small1, r, shifts)

    pl.loop(0, clips, unroll=True)(between)
    place_weights(sec, 1, *weights, up1, down1, sems.at[1], False)
    forward_tiles(adapted1, up1, down1, small1, act1, slope1, acc)
    loads[1].wait()

    def top(r):
        rows = pl.ds(pl.multiple_of(r * 256, 256), 256)
        branch = acc[rows] + small1[DOWNB : DOWNB + 1]
        gain = small1[GAIN : GAIN + 1]
        out1[r] = (out0[r].astype(F32) + gain * branch).astype(BF16)
        above = grad[r].astype(F32) * valid[sec[0] * clips + r].astype(F32)
        low = (above * gain).astype(BF16)
        gb[rows] = low
        sums1[GAIN : GAIN + 1] += rowsum(above * branch)
        sums1[DOWNB : DOWNB + 1] += rowsum(low.astype(F32))

    pl.loop(0, clips, unroll=True)(top)
    half_own = out_own.at[mine]
    route(sec, out0, out1, half_own, out_send, sems.at[4], True)
    for j in range(3):
        activation_tile(j, gb, down1, slope1, sums1)
        for r in range(clips):
            rows = slice(r * 256, (r + 1) * 256)
            part = dot(slope1[j, rows], up1[:, j * TILE : (j + 1) * TILE], NT)
            acc[rows] = part if j == 0 else acc[rows] + part
        up_tile(j, ORDERS[1], adapted1, slope1[j], upd)
        down_tile(j, ORDERS[1], gb, act1[j], dnd)
    ends = ((up_keep, up_pass, up_stay), (down_keep, down_pass, down_stay))
    share = upd.shape[1]
    every = pl.ds(0, share)
    for n, source in enumerate((upd, dnd)):
        route_block(1, sec, place, source, *ends[n], parts.at[n], True, every)

    def move(r):
        return pltpu.make_async_copy(grad.at[r], gin1.at[r], pieces.at[r])

    def under(r):
        rows = pl.ds(pl.multiple_of(r * 256, 256), 256)
        above = grad[r].astype(F32) * valid[sec[0] * clips + r].astype(F32)
        gin, smalls, g_scale, g_shift = norm_backward(
            acc[rows], normed[rows], inv[rows], small1, r, above, out0[r], shifts
        )
        grad[r] = gin
        sums1[TAPS : TAPS + 8] += smalls
        sums1[pl.ds(SCALE + r, 1)] = g_scale
        sums1[pl.ds(SHIFT + r, 1)] = g_shift
        grad0 = gin.astype(F32)
        low = (grad0 * small0[GAIN : GAIN + 1]).astype(BF16)
        gb[rows] = low
        move(r).start()
        sums0[GAIN : GAIN + 1] += rowsum(grad0 * branch0[rows])
        sums0[DOWNB : DOWNB + 1] += rowsum(low.astype(F32))

    pl.loop(0, clips, unroll=True)(under)
    for j in range(3):
        down_tile(j, ORDERS[0], gb, act0[j], dnd0)
    route_block(0, sec, place, dnd0, *ends[1], parts.at[2], True, every)
    tiles = []
    thirds = [pl.ds(j * share // 3, share // 3) for j in range(3)]
    for j in range(3):
        activation_tile(j, gb, down0, slope0, sums0)
        tiles.append(pltpu.make_async_copy(slope0.at[j], gpre_hbm.at[j], sems.at[5 + j // 2 * 3, j % 2]))
        tiles[-1].start()
        up_tile(j, ORDERS[0], adapted0, slope0[j], upd0)
        route_block(0, sec, place, upd0, *ends[0], parts.at[3 + j], True, thirds[j])
    route(sec, out0, out1, half_own, out_send, sems.at[4], False)
    for n, source in enumerate((upd, dnd)):
        route_block(1, sec, place, source, *ends[n], parts.at[n], False, every)
    for copy in tiles + [move(r) for r in range(clips)]:
        copy.wait()
    route_block(0, sec, place, dnd0, *ends[1], parts.at[2], False, every)
    for j in range(3):
        route_block(0, sec, place, upd0, *ends[0], parts.at[3 + j], False, thirds[j])


def last_body(
    sec, gpre, up_own, up_got, normed, inv, small, grad_out, tokens, sums0, sums1, own_small, gin, away, own,
    send,
    up, shifts, sums, sem,
):
    clip = pl.program_id(0)

    @pl.when(clip == 0)
    def _():
        sums[...] = sums0[...]

        @pl.when(sec[0] == 0)
        def _():
            pltpu.make_async_copy(up_own, up, sem).start()

        @pl.when(sec[0] != 0)
        def _():
            pltpu.make_async_copy(up_got, up, sem).start()

        set_shifts(shifts)
        pltpu.make_async_copy(up_own, up, sem).wait()

    gad = dot(gpre[0], up[:, :TILE], NT)
    for j in range(1, 3):
        gad = gad + dot(gpre[j], up[:, j * TILE : (j + 1) * TILE], NT)
    above = grad_out[0]
    out, smalls, g_scale, g_shift = norm_backward(
        gad, normed[...], inv[...], small, clip, above.astype(F32), tokens[0], shifts
    )
    gin[0] = jnp.where(sec[0] == 0, out, above)
    away[0] = jnp.where(sec[0] == 0, above, out)
    sums[TAPS : TAPS + 8] += smalls
    sums[pl.ds(SCALE + clip, 1)] = g_scale
    sums[pl.ds(SHIFT + clip, 1)] = g_shift

    @pl.when(clip == pl.num_programs(0) - 1)
    def _():
        own[...] = pick(sec[0] == 0, sums[...], sums1[...])
        own[CODE : CODE + 2] = own_small[CODE : CODE + 2]
        send[...] = pick(sec[0] == 0, sums1[...], sums[...])


def pick(first, a, b):
    return jnp.where(first, a, b)


def bit_of(spot, step):
    low, high = ORDERS[0][step], ORDERS[1][step]
    return (spot[1] >> (low if low == high else pick(spot[0] == 0, low, high))) & 1


GATHER = (3, 2, 0, 1)


def gather_bit(spot, hop):
    return (spot[1] >> GATHER[hop]) & 1


def gather_slot(spot):
    slot = 0
    for hop in range(len(GATHER)):
        slot = slot + gather_bit(spot, hop) * (1 << hop)
    return slot


def fetch(copies, source, first, rows, target, sem):
    copies.append(pltpu.make_async_copy(source.at[pl.ds(first, rows)], target, sem))
    copies[-1].start()


def pack_body(step, share, sec, place, total0, total1, *refs):
    rows = (8 >> step) * share
    first = pl.multiple_of((1 - bit_of((sec[0], place[0]), step)) * rows, 32)
    if step == 1:
        came, (packet, buffer, sems) = refs[:2], refs[2:]
        copies = []
        for b in range(2):
            fetch(copies, came[b], first, rows, buffer.at[b], sems.at[b])
    else:
        came, packet = refs
    for b, total in enumerate((total0, total1)):
        if step == 1:
            copies[b].wait()
            latest = buffer[b]
        else:
            latest = came[pl.ds(b * 2 * rows + first, rows)]
        packet[b * rows : (b + 1) * rows] = (total[pl.ds(first, rows)] + latest.astype(F32)).astype(BF16)


def share_body(share, total0, total1, came, up, down):
    rows = up.shape[0]
    whole = total0[...] + came[:share].astype(F32)
    for j in range(3):
        up[:, j * TILE : (j + 1) * TILE] = whole[j * rows : (j + 1) * rows]
    down[...] = total1[...] + came[share : 2 * share].astype(F32)


def begin_rows_body(sec, own, got, packet, smalls):
    first = sec[0] == 0
    low = pick(first, own[SCALE:], got[SCALE:])
    high = pick(first, got[SCALE:], own[SCALE:])
    packet[:16] = jnp.concatenate([low, high], axis=0).astype(BF16)
    smalls[...] = own[:SCALE] + got[:SCALE]
    packet[16:32] = smalls[...].astype(BF16)


def more_rows_body(hop, place, before, after, smalls_in, packet, smalls):
    size = 16 << (hop - 1)
    bit = gather_bit((0, place[0]), hop - 1)
    for source, side in ((before, bit), (after, 1 - bit)):
        packet[pl.ds(pl.multiple_of(side * size, 16), size)] = source[:size]
    smalls[...] = smalls_in[...] + after[size:].astype(F32)
    packet[2 * size :] = smalls[...].astype(BF16)


def tables_body(place, before, after, smalls_in, scale, shift, taps, conv, upb, downb, gain, rows_of):
    size = rows_of.shape[0] // 2
    bit = gather_bit((0, place[0]), len(GATHER) - 1)
    for source, side in ((before, bit), (after, 1 - bit)):
        rows_of[pl.ds(pl.multiple_of(side * size, 16), size)] = source[:size]
    total = smalls_in[...] + after[size:].astype(F32)
    owned = scale.shape[0]
    count = 2 * size
    who = total[CODE : CODE + 1, :count] * 64.0 + total[CODE + 1 : CODE + 2, :count]
    wanted = lax.broadcasted_iota(jnp.int32, (owned, count), 0) + place[0] * owned
    hit = who == wanted.astype(F32)
    kind = (lax.broadcasted_iota(jnp.int32, (owned, count), 1) >> 2) & 1
    for k, out in enumerate((scale, shift)):
        out[...] = dot(jnp.where(hit & (kind == k), 1.0, 0.0).astype(BF16), rows_of[...], NN)
    lanes = total.shape[1] // BLOCKS
    turn = lax.rem(BLOCKS - place[0], BLOCKS)
    cut = pltpu.roll(total, turn * lanes, 1)[:, :lanes]
    for k in range(7):
        taps[k] = cut[k : k + 1]
    conv[...] = cut[CONV : CONV + 1]
    downb[...] = cut[DOWNB : DOWNB + 1]
    gain[...] = cut[GAIN : GAIN + 1]
    line = jnp.concatenate([total[UPB + k : UPB + k + 1] for k in range(3)], axis=1)
    upb[...] = pltpu.roll(line, turn * 3 * lanes, 1)[:, : 3 * lanes]


def struct(shape, dtype):
    return jax.ShapeDtypeStruct(shape, dtype)


def params(limit=None):
    return pltpu.CompilerParams(vmem_limit_bytes=limit * 1024 * 1024 if limit else ALL_VMEM)


def cost(flops, moved):
    return pl.CostEstimate(flops=int(flops), bytes_accessed=int(moved), transcendentals=0)


def local(
    tokens, out_cotangent, speaker, valid, conv_weight, conv_bias, scale_table, shift_table,
    up_weight, up_bias, down_weight, down_bias, layer_scale,
):
    section = lax.axis_index("section").astype(jnp.int32)
    place = lax.axis_index("dp").astype(jnp.int32)
    devices = lax.axis_size("dp")
    clips, frames, width = tokens.shape
    hidden = up_weight.shape[2]
    table_rows = scale_table.shape[1]
    half = clips // 2
    rows = half * frames
    sec = section[None]
    swap = [(0, 1), (1, 0)]

    own_small, other_small = pl.pallas_call(
        prep_body,
        out_shape=[struct((SMALL, width), F32)] * 2,
        in_specs=[SMEM, SMEM, SMEM] + [VMEM] * 5 + [ANY] * 2,
        out_specs=[VMEM] * 2,
        scratch_shapes=[pltpu.SemaphoreType.DMA((2, 2, half))],
        compiler_params=params(),
        name="prep",
    )(
        sec, place[None], speaker, conv_weight.transpose(1, 0, 2), conv_bias, up_bias, down_bias, layer_scale,
        scale_table, shift_table,
    )
    got_small = lax.ppermute(other_small, "section", swap)
    up_own, down_own = up_weight[0], down_weight[0]
    up_got = lax.ppermute(up_own, "section", swap)
    down_got = lax.ppermute(down_own, "section", swap)
    clip_block = (1, frames, width)
    whole_small = pl.BlockSpec((SMALL, width), lambda c, sec: (0, 0))
    half_struct = struct((half, frames, width), BF16)
    whole_struct = struct((clips, frames, width), BF16)
    small_struct = struct((SMALL, width), F32)
    flat_struct = struct((rows, width), BF16)
    tiles = hidden // TILE
    tiled = (tiles, rows, TILE)
    share = hidden // BLOCKS
    gradient = (BLOCKS, share, width)
    gradient_struct = struct(gradient, BF16)
    piece_struct = struct((BLOCKS // 2, share, width), BF16)
    product = 2 * rows * width * hidden

    (
        sums0, sums1, gin1, normed0, inv0, out_own, out_send, gpre0, up_keep,
        down_keep, up_pass, down_pass, up_stay, down_stay, small0,
    ) = pl.pallas_call(
        main_body,
        out_shape=[
            small_struct, small_struct, half_struct, flat_struct, struct((rows, 128), F32),
            whole_struct, half_struct, struct(tiled, BF16), gradient_struct, gradient_struct,
            piece_struct, piece_struct, piece_struct, piece_struct, small_struct,
        ],
        in_specs=[SMEM, SMEM, SMEM, VMEM, VMEM, HBM, HBM, HBM, ANY, HBM, ANY],
        out_specs=[VMEM, VMEM] + [HBM] * 12 + [VMEM],
        scratch_shapes=[
            pltpu.VMEM((width, hidden), BF16),
            pltpu.VMEM((hidden, width), BF16),
            pltpu.VMEM((width, hidden), BF16),
            pltpu.VMEM((hidden, width), BF16),
            pltpu.VMEM(tiled, BF16),
            pltpu.VMEM(tiled, BF16),
            pltpu.VMEM(tiled, BF16),
            pltpu.VMEM(tiled, BF16),
            pltpu.VMEM((rows, width), F32),
            pltpu.VMEM((rows, width), BF16),
            pltpu.VMEM((rows, width), BF16),
            pltpu.VMEM((rows, 128), F32),
            pltpu.VMEM((rows, width), BF16),
            pltpu.VMEM((rows, width), F32),
            pltpu.VMEM((rows, width), BF16),
            pltpu.VMEM((half, frames, width), BF16),
            pltpu.VMEM((half, frames, width), BF16),
            pltpu.VMEM((half, frames, width), BF16),
            pltpu.VMEM((half, frames, width), BF16),
            pltpu.VMEM((SMALL, width), F32),
            pltpu.VMEM((SMALL, width), F32),
            pltpu.VMEM((len(OFFSETS) * frames, frames), BF16),
            pltpu.VMEM(gradient, BF16),
            pltpu.VMEM(gradient, BF16),
            pltpu.VMEM(gradient, BF16),
            pltpu.VMEM(gradient, BF16),
            pltpu.SemaphoreType.DMA((9, 2)),
            pltpu.SemaphoreType.DMA((half,)),
            pltpu.SemaphoreType.DMA((6, 2)),
        ],
        compiler_params=params(),
        cost_estimate=cost(11 * product, 24 << 20),
        name="main",
    )(
        sec, place[None], valid, own_small, got_small, tokens, out_cotangent, up_own, up_got, down_own, down_got
    )
    swapped = []
    for piece in (up_pass, down_pass, up_stay, down_stay):
        swapped.append(lax.ppermute(piece, "section", swap))
    pairs = [[up_keep, swapped[0], swapped[2]], [down_keep, swapped[1], swapped[3]]]
    got_out = lax.ppermute(out_send, "section", swap)

    gin_own, gin_send, own_sums, sums_send = pl.pallas_call(
        last_body,
        grid_spec=pltpu.PrefetchScalarGridSpec(
            num_scalar_prefetch=1,
            grid=(half,),
            in_specs=[
                pl.BlockSpec((tiles, frames, TILE), lambda c, sec: (0, c, 0)),
                HBM,
                ANY,
                pl.BlockSpec((frames, width), lambda c, sec: (c, 0)),
                pl.BlockSpec((frames, 128), lambda c, sec: (c, 0)),
                whole_small,
                pl.BlockSpec(clip_block, lambda c, sec: (c, 0, 0)),
                pl.BlockSpec(clip_block, lambda c, sec: (sec[0] * half + c, 0, 0)),
                whole_small,
                whole_small,
                whole_small,
            ],
            out_specs=[
                pl.BlockSpec(clip_block, lambda c, sec: (sec[0] * half + c, 0, 0)),
                pl.BlockSpec(clip_block, lambda c, sec: (c, 0, 0)),
                whole_small,
                whole_small,
            ],
            scratch_shapes=[
                pltpu.VMEM((width, hidden), BF16),
                pltpu.VMEM((len(OFFSETS) * frames, frames), BF16),
                pltpu.VMEM((SMALL, width), F32),
                pltpu.SemaphoreType.DMA,
            ],
        ),
        out_shape=[whole_struct, half_struct, small_struct, small_struct],
        compiler_params=params(),
        cost_estimate=cost(2 * half * product, 12 << 20),
        name="last",
    )(sec, gpre0, up_own, up_got, normed0, inv0, small0, gin1, tokens, sums0, sums1, own_small)
    got_gin = lax.ppermute(gin_send, "section", swap)
    got_sums = lax.ppermute(sums_send, "section", swap)

    def joined(whole, got):
        return lax.dynamic_update_slice(whole, got, ((1 - section) * half, 0, 0))[None]

    block_outputs = joined(out_own, got_out)
    input_grads = joined(gin_own, got_gin)
    if devices == BLOCKS:
        outs = halved(sec, place[None], pairs, own_sums, got_sums, table_rows)
    else:
        outs = scattered(section, place, devices, speaker, pairs, own_sums, got_sums, table_rows)
    return (block_outputs, input_grads) + outs


def exchanged(packet, step):
    devices = lax.axis_size("dp")
    moves = [
        (s * devices + i, s * devices + (i ^ (1 << ORDERS[s][step])))
        for s in range(2)
        for i in range(devices)
    ]
    return lax.ppermute(packet, PAIR, moves)


def halved(sec, place, pairs, own_sums, got_sums, table_rows):
    _, share, width = pairs[0][0].shape
    pairs = [[piece.reshape(-1, width) for piece in pair] for pair in pairs]
    spot = (sec[0], place[0])
    half_rows = 8 * share

    def part(array, first, count):
        return lax.dynamic_slice_in_dim(array, first, count, 0).astype(F32)

    bit = bit_of(spot, 0)
    latest, totals = [None, None], [None, None]
    for b in (0, 1):
        keep, passed, stays = pairs[b]
        own = lax.optimization_barrier(part(keep, (1 - bit) * half_rows, half_rows))
        packet = (own + passed.astype(F32)).astype(BF16)
        latest[b] = exchanged(packet, 0)
        keep, stays, _ = lax.optimization_barrier((keep, stays, own_sums))
        totals[b] = part(keep, bit * half_rows, half_rows) + stays.astype(F32)

    def small_call(body, outs, scalars, operands, scratch=(), specs=None, limit=8):
        return pl.pallas_call(
            body,
            out_shape=outs,
            in_specs=[SMEM] * len(scalars) + (specs or [VMEM] * len(operands)),
            out_specs=[VMEM] * len(outs),
            scratch_shapes=scratch,
            compiler_params=params(limit),
            cost_estimate=cost(0, 2 << 20),
        )(*scalars, *operands)

    def row_outs(hop):
        return [struct(((16 << hop) + 16, width), BF16), struct((SCALE, width), F32)]

    rows_packet, smalls = small_call(begin_rows_body, row_outs(0), [sec], [own_sums, got_sums], limit=None)
    for hop in range(len(GATHER)):
        more = lax.ppermute(
            rows_packet, "dp", [(i, i ^ (1 << GATHER[hop])) for i in range(BLOCKS)]
        )
        operands = [rows_packet, more, smalls]
        if hop + 1 < len(GATHER):
            rows_packet, smalls = small_call(
                functools.partial(more_rows_body, hop + 1), row_outs(hop + 1), [place],
                operands,
            )
    owned = table_rows // BLOCKS
    lanes = width // BLOCKS
    one = struct((1, lanes), F32)
    scale, shift, taps, conv, upb, downb, gain = small_call(
        tables_body,
        [
            struct((owned, width), F32),
            struct((owned, width), F32),
            struct((7, 1, lanes), F32),
            one,
            struct((1, 3 * lanes), F32),
            one,
            one,
        ],
        [place],
        operands,
        [pltpu.VMEM((16 * BLOCKS, width), BF16)],
    )

    for step in range(1, 4):
        rows = (8 >> step) * share
        first = bit_of(spot, step) * rows
        packet_struct = [struct((2 * rows, width), BF16)]
        if step == 1:
            (packet,) = small_call(
                functools.partial(pack_body, step, share), packet_struct, [sec, place],
                totals + latest,
                [pltpu.VMEM((2, rows, width), BF16), pltpu.SemaphoreType.DMA((2,))],
                [VMEM] * 2 + [ANY] * 2,
            )
        else:
            (packet,) = small_call(
                functools.partial(pack_body, step, share), packet_struct, [sec, place],
                totals + latest[:1],
            )
        got = exchanged(packet, step)
        bases = (0, 0) if step == 1 else (0, 2 * rows)
        totals = [
            part(totals[b], first, rows) + part(latest[b], bases[b] + first, rows) for b in range(2)
        ]
        latest = [got, got]
    up, down = small_call(
        functools.partial(share_body, share),
        [struct((width // BLOCKS, 3 * TILE), F32), struct((share, width), F32)],
        [],
        totals + latest[:1],
    )
    return (
        taps.transpose(1, 0, 2), conv, scale[None], shift[None], up[None], upb, down[None], downb, gain
    )


def scattered(section, place, devices, speaker, pairs, own_sums, got_sums, table_rows):
    first_section = section == 0
    smalls = lax.psum(own_sums[:SCALE] + got_sums[:SCALE], "dp")
    clip_rows = jnp.stack([own_sums[SCALE:], got_sums[SCALE:]])
    clip_rows = pick(first_section, clip_rows, clip_rows[::-1]).astype(BF16)
    clips = speaker.shape[0]
    width = clip_rows.shape[-1]
    clip_rows = clip_rows.reshape(2, 2, clips // 2, width).transpose(1, 0, 2, 3).reshape(2, clips, width)
    gathered = lax.all_gather(clip_rows, "dp", axis=1, tiled=True)
    who = lax.all_gather(speaker, "dp", tiled=True)
    owned = table_rows // devices
    wanted = place * owned + jnp.arange(owned, dtype=jnp.int32)
    chosen = (who[None, :] == wanted[:, None]).astype(BF16)
    tables = [jnp.dot(chosen, gathered[k], preferred_element_type=F32) for k in range(2)]
    low, high = ORDERS[0][0], ORDERS[1][0]
    leaves = 1 - ((place >> pick(first_section, low, high)) & 1)
    natural = []
    for keep, gone, stay in pairs:
        other = pick(leaves == 0, jnp.concatenate([gone, stay]), jnp.concatenate([stay, gone]))
        whole = keep.astype(F32) + other.astype(F32)
        both = [jnp.stack([whole[position(i, order)] for i in range(BLOCKS)]) for order in ORDERS]
        natural.append(pick(first_section, both[0], both[1]))
    _, rows, width = natural[0].shape
    tiles = rows * BLOCKS // TILE
    up = natural[0].reshape(BLOCKS, tiles, rows // tiles, TILE).transpose(0, 2, 1, 3)
    up_share = lax.psum_scatter(up.reshape(width, -1), "dp", scatter_dimension=0, tiled=True)
    down_share = lax.psum_scatter(natural[1].reshape(-1, width), "dp", scatter_dimension=0, tiled=True)
    lanes = width // devices
    own_lanes = lax.dynamic_slice_in_dim(smalls, place * lanes, lanes, 1)
    upb = lax.dynamic_slice_in_dim(smalls[UPB : UPB + 3].reshape(-1), place * 3 * lanes, 3 * lanes, 0)
    return (
        own_lanes[TAPS : TAPS + 7][None],
        own_lanes[CONV : CONV + 1],
        tables[0][None],
        tables[1][None],
        up_share[None],
        upb[None],
        down_share[None],
        own_lanes[DOWNB : DOWNB + 1],
        own_lanes[GAIN : GAIN + 1],
    )


def solution(mesh):
    placed = (
        P("dp", None, None),
        P("dp", None, None),
        P("dp"),
        P("dp"),
        P("section", None, None),
        P("section", None),
        P("section", None, None),
        P("section", None, None),
        P("section", None, None),
        P("section", None),
        P("section", None, None),
        P("section", None),
        P("section", None),
    )

    return jax.shard_map(
        local,
        mesh=mesh,
        in_specs=placed,
        out_specs=(
            P("section", "dp", None, None),
            P("section", "dp", None, None),
            P("section", None, "dp"),
            P("section", "dp"),
            P("section", "dp", None),
            P("section", "dp", None),
            P("section", "dp", None),
            P("section", "dp"),
            P("section", "dp", None),
            P("section", "dp"),
            P("section", "dp"),
        ),
        check_vma=False,
    )
```
